32 devices in a mesh: node: 2 (over y), gz: 16 (over z, x, core).
Axes of the slice: x: 2, y: 2, z: 4, core: 2. Of those that a mesh axis runs over, the one named last changes fastest.
Arguments:
- source: float32 [2, 64, 512, 256], P(None, ('node', 'gz')), parts along dimension 1, may hold values from -56 to 56
- layer_ids: int32 [64, 256], P(('node', 'gz')), parts along dimension 0, may hold values from 0 to 15
- conduct_table: float32 [16], replicated, may hold values from 0.35 to 3.75
- shift: float32 [4], P('node'), parts along dimension 0, may hold values from 0.2 to 1
Outputs:
- solution_field: float32 [2, 64, 512, 256], P(None, ('node', 'gz')), parts along dimension 1
- residual_norms: float32 [4], P('node'), parts along dimension 0
The draws below stay inside these ranges and needn't reach their ends.
There are 2 independent parts, one for each index of `node`. The reference program is written for one: setup_inputs(seed, part) draws one part's arguments, and reference() takes and returns one part's arrays. A program takes and returns all parts, laid end to end along the dimension named above; an argument that names none is the same for every part. Nothing has to cross between parts.
All inputs are finite; a program needn't handle non-finite values.
Results may differ from the reference program's by a relative error of at most 0.0003.
Values sent between devices are 32-bit elements; how exact they have to be, the bound alone decides.
A program may use at most 64 MiB of HBM per device.

```python
import jax
import jax.numpy as jnp
from jax import lax

NX = 512
NY = 256
ITERS = 2
LAYERS = 16
NZ = 32


def draw_source(key, part):
    keys = jax.random.split(key, 5)
    z_ramp = 1.0 + 2.0 * lax.iota(jnp.float32, NZ) / max(NZ - 1, 1)
    z_ramp = z_ramp[None, :, None, None]
    x_pos = lax.iota(jnp.float32, NX)[None, None, :, None] * (2.0 * jnp.pi / NX)
    amp_one = jnp.clip(jax.random.normal(keys[1], (2, NZ, 1, NY), jnp.float32), -2.0, 2.0)
    amp_two = jnp.clip(jax.random.normal(keys[2], (2, NZ, 1, NY), jnp.float32), -2.0, 2.0)
    phase_one = jax.random.uniform(keys[3], (2, NZ, 1, NY), jnp.float32, 0.0, 2.0 * jnp.pi)
    phase_two = jax.random.uniform(keys[4], (2, NZ, 1, NY), jnp.float32, 0.0, 2.0 * jnp.pi)
    smooth = amp_one * jnp.cos(x_pos + phase_one) + 0.5 * amp_two * jnp.cos(2.0 * x_pos + phase_two)
    texture = jnp.clip(jax.random.normal(keys[0], (2, NZ, NX, NY), jnp.float32), -4.0, 4.0)
    values = z_ramp * (texture + smooth)
    return values.astype(jnp.float32)


def draw_layer_ids(key, part):
    depth = lax.iota(jnp.int32, NZ)[:, None]
    base_layer = depth * LAYERS // NZ
    jitter = jax.random.randint(key, (NZ, NY), -2, 3, jnp.int32)
    return jnp.clip(base_layer + jitter, 0, LAYERS - 1).astype(jnp.int32)


def draw_conduct_table(key, part):
    levels = lax.iota(jnp.float32, LAYERS) / (LAYERS - 1)
    base_layer = 0.5 * jnp.exp(jnp.log(6.0) * levels)
    factor = jax.random.uniform(key, (LAYERS,), jnp.float32, 0.8, 1.25)
    return (base_layer * factor).astype(jnp.float32)


def setup_inputs(seed: int = 0, part: int = 0) -> dict:
    seeds = jax.random.split(jax.random.key(seed), 5)
    part_splits = jax.random.split(jax.random.fold_in(seeds[4], part), 5)
    source = draw_source(jax.random.fold_in(jax.random.fold_in(seeds[4], part), 71), part)
    layer_ids = draw_layer_ids(jax.random.fold_in(jax.random.fold_in(seeds[4], part), 71), part)
    conduct_table = draw_conduct_table(jax.random.fold_in(seeds[4], 71), part)
    shift = jnp.clip(jax.random.uniform(part_splits[3], (2,), jnp.float32, 0.2, 1.0), 0.2, 1.0)
    return {"source": source, "layer_ids": layer_ids, "conduct_table": conduct_table, "shift": shift}


relax = 0.6
highest = lax.Precision.HIGHEST

def sine_table(length):
    indices = lax.iota(jnp.int32, length) + 1
    product = indices[:, None] * indices[None, :] % (2 * (length + 1))
    return jnp.sqrt(2.0 / (length + 1)) * jnp.sin(jnp.pi / (length + 1) * product.astype(jnp.float32))

def sine_eigen(length):
    indices = lax.iota(jnp.float32, length) + 1.0
    return 2.0 - 2.0 * jnp.cos(jnp.pi / (length + 1) * indices)

def expand(weights):
    return weights[None, :, None, :]

def yz_part(field, upper, lower, conduct, cond_hi, cond_lo):
    cond_pad = jnp.pad(conduct, ((0, 0), (1, 1)), mode='edge')
    face_yp = 0.5 * (conduct + cond_pad[:, 2:])
    face_ym = 0.5 * (conduct + cond_pad[:, :-2])
    face_zp = 0.5 * (conduct + cond_hi)
    face_zm = 0.5 * (conduct + cond_lo)
    field_pad = jnp.pad(field, ((0, 0), (0, 0), (0, 0), (1, 1)))
    total = expand(face_yp) * (field - field_pad[..., 2:]) + expand(face_ym) * (field - field_pad[..., :-2])
    return total + expand(face_zp) * (field - upper) + expand(face_zm) * (field - lower)

def shift_mult(shift_re, shift_im, field):
    return jnp.stack([shift_re * field[0] - shift_im * field[1], shift_re * field[1] + shift_im * field[0]])

def sine_both(field, sine_y, sine_z):
    field = jnp.einsum('pzxy,yj->pzxj', field, sine_y, precision=highest)
    return jnp.einsum('pzxy,zk->pkxy', field, sine_z, precision=highest)

def precondition(spectra, mode_eig, mean_cond, shift_re, shift_im, sine_y, sine_z, eig_y, eig_z):
    coeffs = sine_both(spectra, sine_y, sine_z)
    eigen = eig_z[:, None, None] + mode_eig[None, :, None] + eig_y[None, None, :]
    real_den = shift_re + mean_cond * eigen
    modulus = real_den * real_den + shift_im * shift_im
    scaled = jnp.stack([(coeffs[0] * real_den + coeffs[1] * shift_im) / modulus, (coeffs[1] * real_den - coeffs[0] * shift_im) / modulus])
    return sine_both(scaled, sine_y, sine_z)

def reference(source, layer_ids, conduct_table, shift):
    conduct = conduct_table[layer_ids]
    shift_re = shift[0]
    shift_im = shift[1]
    mean_cond = jnp.mean(conduct)
    cond_z = jnp.pad(conduct, ((1, 1), (0, 0)), mode='edge')
    cond_hi = cond_z[2:]
    cond_lo = cond_z[:-2]
    sine_y = sine_table(NY)
    sine_z = sine_table(NZ)
    eig_y = sine_eigen(NY)
    eig_z = sine_eigen(NZ)
    mode_ids = lax.iota(jnp.int32, NX).astype(jnp.float32)
    mode_eig = 2.0 - 2.0 * jnp.cos(2.0 * jnp.pi / NX * mode_ids)
    solution = jnp.zeros_like(source)
    norms = []
    for iteration in range(ITERS):
        padded = jnp.pad(solution, ((0, 0), (1, 1), (0, 0), (0, 0)))
        lap = expand(conduct) * (2.0 * solution - jnp.roll(solution, 1, 2) - jnp.roll(solution, -1, 2))
        lap = lap + yz_part(solution, padded[:, 2:], padded[:, :-2], conduct, cond_hi, cond_lo)
        resid = source - (shift_mult(shift_re, shift_im, solution) + lap)
        norms.append(jnp.sqrt(jnp.sum(resid * resid) / (NX * NY * NZ)))
        spectrum = jnp.fft.fft(lax.complex(resid[0], resid[1]), axis=1)
        spectra = jnp.stack([jnp.real(spectrum), jnp.imag(spectrum)])
        update = precondition(spectra, mode_eig, mean_cond, shift_re, shift_im, sine_y, sine_z, eig_y, eig_z)
        inverse = jnp.fft.ifft(lax.complex(update[0], update[1]), axis=1)
        solution = solution + relax * jnp.stack([jnp.real(inverse), jnp.imag(inverse)])
    return (solution, jnp.stack(norms))
```

```python
import functools

import jax
import jax.numpy as jnp
import numpy as np
from jax import lax
from jax.experimental import pallas as pl
from jax.experimental.pallas import tpu as pltpu
from jax.sharding import PartitionSpec as P

ITERS = 2


relax = 0.6
highest = lax.Precision.HIGH


def with_halo(cells, sides, width):
    for axis, dim in sides:
        count = lax.axis_size(axis)
        ends = count - 1
        head = lax.slice_in_dim(cells, 0, width, axis=dim)
        tail = lax.slice_in_dim(cells, cells.shape[dim] - width, cells.shape[dim], axis=dim)
        cells = jnp.concatenate(
            [
                lax.ppermute(tail, axis, [(i, (i + 1) % count) for i in range(ends)]),
                cells,
                lax.ppermute(head, axis, [((i + 1) % count, i) for i in range(ends)]),
            ],
            axis=dim,
        )
    return cells


def sine_table(length):
    indices = lax.iota(jnp.int32, length) + 1
    product = indices[:, None] * indices[None, :] % (2 * (length + 1))
    return jnp.sqrt(2.0 / (length + 1)) * jnp.sin(
        jnp.pi / (length + 1) * product.astype(jnp.float32)
    )


def sine_eigen(length):
    indices = lax.iota(jnp.float32, length) + 1.0
    return 2.0 - 2.0 * jnp.cos(jnp.pi / (length + 1) * indices)


def dft_tables(length):
    indices = lax.iota(jnp.int32, length)
    product = indices[:, None] * indices[None, :] % length
    angles = 2.0 * jnp.pi / length * product.astype(jnp.float32)
    return (jnp.cos(angles), jnp.sin(angles))


def transform(field, cos_t, sin_t, inverse):

    def project(component, matrix):
        return jnp.einsum("zxy,xk->zky", component, matrix, precision=highest)

    re_cos = project(field[0], cos_t)
    re_sin = project(field[0], sin_t)
    im_cos = project(field[1], cos_t)
    im_sin = project(field[1], sin_t)
    if inverse:
        return jnp.stack([re_cos - im_sin, im_cos + re_sin]) / cos_t.shape[0]
    return jnp.stack([re_cos + im_sin, im_cos - re_sin])


def expand(weights):
    return weights[None, :, None, :]


def yz_part(field, upper, lower, conduct, cond_hi, cond_lo):
    cond_pad = jnp.pad(conduct, ((0, 0), (1, 1)), mode="edge")
    face_yp = 0.5 * (conduct + cond_pad[:, 2:])
    face_ym = 0.5 * (conduct + cond_pad[:, :-2])
    face_zp = 0.5 * (conduct + cond_hi)
    face_zm = 0.5 * (conduct + cond_lo)
    field_pad = jnp.pad(field, ((0, 0), (0, 0), (0, 0), (1, 1)))
    total = expand(face_yp) * (field - field_pad[..., 2:]) + expand(face_ym) * (
        field - field_pad[..., :-2]
    )
    return total + expand(face_zp) * (field - upper) + expand(face_zm) * (field - lower)


def shift_mult(shift_re, shift_im, field):
    return jnp.stack(
        [shift_re * field[0] - shift_im * field[1], shift_re * field[1] + shift_im * field[0]]
    )


def sine_both(field, sine_y, sine_z):
    field = jnp.einsum("pzxy,yj->pzxj", field, sine_y, precision=highest)
    return jnp.einsum("pzxy,zk->pkxy", field, sine_z, precision=highest)


def precondition(coeffs, mode_eig, mean_cond, shift_re, shift_im, sine_y, sine_z, eig_y, eig_z):
    coeffs = sine_both(coeffs, sine_y, sine_z)
    eigen = eig_z[:, None, None] + mode_eig[None, :, None] + eig_y[None, None, :]
    real_den = shift_re + mean_cond * eigen
    inv = 1.0 / (real_den * real_den + shift_im * shift_im)
    scaled = jnp.stack(
        [
            (coeffs[0] * real_den + coeffs[1] * shift_im) * inv,
            (coeffs[1] * real_den - coeffs[0] * shift_im) * inv,
        ]
    )
    return sine_both(scaled, sine_y, sine_z)


def body_plain(source, layer_ids, conduct_table, shift):
    shift_re = shift[0]
    shift_im = shift[1]
    planes = source.shape[1]
    length_x = source.shape[2]
    length_y = source.shape[3]
    groups = lax.axis_size("gz")
    length_z = planes * groups
    modes = length_x // groups
    first_mode = lax.axis_index("gz") * modes
    layers = conduct_table.shape[0]
    onehot = layer_ids[:, :, None] == lax.iota(jnp.int32, layers)[None, None, :]
    local = jnp.sum(jnp.where(onehot, conduct_table[None, None, :], 0.0), axis=-1)
    conduct = lax.all_gather(local, "gz", axis=0, tiled=True)
    mean_cond = jnp.sum(conduct) / (length_y * length_z)
    cond_z = jnp.pad(conduct, ((1, 1), (0, 0)), mode="edge")
    cos_t, sin_t = dft_tables(length_x)
    sine_y = sine_table(length_y)
    sine_z = sine_table(length_z)
    eig_y = sine_eigen(length_y)
    eig_z = sine_eigen(length_z)
    mode_ids = (first_mode + lax.iota(jnp.int32, modes)).astype(jnp.float32)
    mode_eig = 2.0 - 2.0 * jnp.cos(2.0 * jnp.pi / length_x * mode_ids)
    cells = length_x * length_y * length_z
    spectra = transform(source, cos_t, sin_t, False)
    forcing = lax.all_to_all(spectra, "gz", split_axis=2, concat_axis=1, tiled=True)
    partials = []
    solution = jnp.zeros_like(forcing)
    for iteration in range(ITERS):
        if iteration == 0:
            resid = forcing
        else:
            padded = jnp.pad(solution, ((0, 0), (1, 1), (0, 0), (0, 0)))
            lap = expand(conduct) * mode_eig[None, None, :, None] * solution
            lap = lap + yz_part(
                solution, padded[:, 2:], padded[:, :-2], conduct, cond_z[2:], cond_z[:-2]
            )
            resid = forcing - (shift_mult(shift_re, shift_im, solution) + lap)
        partials.append(jnp.sum(resid * resid) / length_x)
        update = precondition(
            resid, mode_eig, mean_cond, shift_re, shift_im, sine_y, sine_z, eig_y, eig_z
        )
        solution = solution + relax * update
    slabs = lax.all_to_all(solution, "gz", split_axis=1, concat_axis=2, tiled=True)
    result = transform(slabs, cos_t, sin_t, True)
    sums = jnp.sum(lax.all_gather(jnp.stack(partials)[None, :], "gz", axis=0, tiled=True), axis=0)
    return (result, jnp.sqrt(sums / cells))


RADIX = 4


def halves(table):
    high = table.astype(jnp.bfloat16)
    low = (table - high.astype(np.float32)).astype(jnp.bfloat16)
    return (jnp.asarray(high), jnp.asarray(low))


def radix_tables(length_x):
    count = length_x // RADIX
    pos = np.arange(count)
    forward = []
    for residue in range(RADIX):
        modes = RADIX * pos + residue
        angle = 2.0 * np.pi / length_x * (modes[:, None] * pos[None, :] % length_x)
        cos_t, sin_t = np.cos(angle), np.sin(angle)
        forward.append(np.block([[cos_t, sin_t], [-sin_t, cos_t]]))
    forward = np.stack(forward)
    backward = np.swapaxes(forward, 1, 2) / length_x
    return (forward.astype(np.float32), backward.astype(np.float32))


def sine_host(length):
    indices = np.arange(length) + 1
    product = indices[:, None] * indices[None, :] % (2 * (length + 1))
    return (np.sqrt(2.0 / (length + 1)) * np.sin(np.pi / (length + 1) * product)).astype(np.float32)


def split(values):
    high = values.astype(jnp.bfloat16)
    return (high, (values - high.astype(jnp.float32)).astype(jnp.bfloat16))


def dot3(left, right):
    mul = functools.partial(jnp.dot, preferred_element_type=jnp.float32)
    return mul(left[0], right[0]) + (mul(left[0], right[1]) + mul(left[1], right[0]))


def turn(re, im, quarter):
    quarter = quarter % 4
    return [(re, im), (-im, re), (-re, -im), (im, -re)][quarter]


def combine(parts, quarters):
    re, im = turn(*parts[0], quarters[0])
    for part, quarter in zip(parts[1:], quarters[1:]):
        more_re, more_im = turn(*part, quarter)
        re, im = re + more_re, im + more_im
    return (re, im)


def times(left, right):
    return (left[0] * right[0] - left[1] * right[1], left[0] * right[1] + left[1] * right[0])


def plus(left, right):
    return (left[0] + right[0], left[1] + right[1])


def pair(ref, *index):
    return (ref[(*index, 0)], ref[(*index, 1)])


def put(ref, values, *index):
    ref[(*index, 0)] = values[0]
    ref[(*index, 1)] = values[1]


def choose(test, left, right):
    return (jnp.where(test, left[0], right[0]), jnp.where(test, left[1], right[1]))


def kernel(
    groups,
    planes,
    chunks,
    layers,
    source_hbm,
    ids_hbm,
    table,
    shift,
    mode_hbm,
    eig_hbm,
    fwd_hi_hbm,
    fwd_lo_hbm,
    sine_hi_hbm,
    sine_lo_hbm,
    slabs,
    sums,
    source,
    ids,
    mode_eig,
    eig_y,
    fwd_hi,
    fwd_lo,
    sine_hi,
    sine_lo,
    spectra,
    forcing,
    cond_own,
    cond_all,
    cond,
    faces,
    work,
    alpha,
    lines,
    field,
    result,
    sum_own,
    squares,
    pair_out,
    pair_in,
    rest_out,
    comb_out,
    comb_in,
    load_sem,
    in_send,
    in_recv,
    cond_send,
    cond_recv,
    out_send,
    out_recv,
    sum_send,
    sum_recv,
    own_sem,
    pair_send,
    pair_recv,
    comb_send,
    comb_recv,
):
    me = lax.axis_index("gz")
    side = lax.rem(me, RADIX)
    team = me // RADIX
    teams = groups // RADIX
    length_x = source.shape[2]
    length_y = source.shape[3]
    length_z = groups * planes
    depth = RADIX * planes
    count = length_x // RADIX
    modes = count // chunks
    first_level = team * depth
    last_level = length_z - first_level - depth

    loads = [
        pltpu.make_async_copy(src, dst, load_sem.at[index])
        for index, (src, dst) in enumerate(
            [
                (source_hbm, source),
                (fwd_hi_hbm, fwd_hi),
                (fwd_lo_hbm, fwd_lo),
                (ids_hbm, ids),
                (mode_hbm.at[side], mode_eig),
                (eig_hbm, eig_y),
                (sine_hi_hbm, sine_hi),
                (sine_lo_hbm, sine_lo),
            ]
        )
    ]
    for load in [loads[3], *loads[:3], *loads[4:]]:
        load.start()

    def remote(src, dst, send, recv, target):
        return pltpu.make_async_remote_copy(
            src_ref=src,
            dst_ref=dst,
            send_sem=send,
            recv_sem=recv,
            device_id={"gz": target},
            device_id_type=pl.DeviceIdType.MESH,
        )

    def peer(offset):
        return lax.rem(me + offset, groups)

    def mate(offset):
        return lax.rem(side + offset, RADIX)

    def rows(index):
        return pl.ds(index * planes, planes)

    def cond_copy(offset):
        return remote(
            cond_own, cond_all.at[me], cond_send.at[offset], cond_recv.at[offset], peer(offset)
        )

    def sum_copy(offset):
        return remote(
            sum_own, sums.at[me], sum_send.at[offset], sum_recv.at[offset], peer(offset)
        )

    def in_copy(chunk, offset):
        target = mate(offset)
        return remote(
            spectra.at[target, chunk],
            forcing.at[chunk, rows(side)],
            in_send.at[chunk, offset],
            in_recv.at[chunk, offset],
            team * RADIX + target,
        )

    def out_copy(chunk, offset):
        target = mate(offset)
        return remote(
            result.at[chunk, rows(target)],
            slabs.at[side, chunk],
            out_send.at[chunk, offset],
            out_recv.at[chunk, offset],
            team * RADIX + target,
        )

    def own_copy(chunk):
        return pltpu.make_async_copy(
            result.at[chunk, rows(side)], slabs.at[side, chunk], own_sem.at[chunk]
        )

    even = lax.rem(team, 2) == 0
    inner = (team == 1) | (team == 2)
    lower = team < 2
    partner = team + 1 - 2 * lax.rem(team, 2)

    def pair_copy(turn_id, chunk):
        return remote(
            pair_out.at[turn_id, chunk],
            pair_in.at[turn_id, chunk],
            pair_send.at[turn_id, chunk],
            pair_recv.at[turn_id, chunk],
            partner * RADIX + side,
        )

    def comb_copy(turn_id, chunk, which):
        target = [teams - 1 - team, (teams - 1) * (2 - team)][which]
        return remote(
            comb_out.at[turn_id, chunk],
            comb_in.at[turn_id, chunk],
            comb_send.at[turn_id, chunk, which],
            comb_recv.at[turn_id, chunk],
            target * RADIX + side,
        )

    def each_peer(act):
        def run(offset, carry):
            act(offset)
            return carry

        lax.fori_loop(1, groups, run, 0)

    barrier = pltpu.get_barrier_semaphore()

    @each_peer
    def _(offset):
        pl.semaphore_signal(
            barrier, inc=1, device_id={"gz": peer(offset)}, device_id_type=pl.DeviceIdType.MESH
        )

    loads[3].wait()
    found = jnp.zeros((planes, length_y), jnp.float32)
    for layer in range(layers):
        found = found + jnp.where(ids[...] == layer, table[layer], 0.0)
    cond_own[...] = found
    cond_all[me] = found
    for load in loads[:3]:
        load.wait()

    def forward(plane, carry):
        parts = [
            (
                source[0, plane, q * count : (q + 1) * count, :],
                source[1, plane, q * count : (q + 1) * count, :],
            )
            for q in range(RADIX)
        ]
        for residue in range(RADIX):
            mixed = combine(parts, [-residue * q for q in range(RADIX)])
            right = split(jnp.concatenate(mixed, axis=0))
            values = dot3((fwd_hi[residue], fwd_lo[residue]), right)
            for chunk in range(chunks):
                for part in range(2):
                    start = part * count + chunk * modes
                    spectra[residue, chunk, plane, part] = values[start : start + modes]
        return carry

    lax.fori_loop(0, planes, forward, 0)
    pl.semaphore_wait(barrier, groups - 1)

    @each_peer
    def _(offset):
        cond_copy(offset).start()

    def send_in(chunk, carry):
        for offset in (2, 3, 1):
            in_copy(chunk, offset).start()
        return carry

    lax.fori_loop(0, chunks, send_in, 0)

    def keep(chunk, carry):
        forcing[chunk, rows(side)] = spectra[side, chunk]
        return carry

    lax.fori_loop(0, chunks, keep, 0)
    for load in loads[4:]:
        load.wait()

    @each_peer
    def _(offset):
        cond_copy(offset).wait()

    def spread(index, total):
        for plane in range(planes):
            row = jnp.broadcast_to(cond_all[index, plane : plane + 1, :], (8, length_y))
            cond[index * planes + plane + 1] = row
            total = total + row
        return total

    total = lax.fori_loop(0, groups, spread, jnp.zeros((8, length_y), jnp.float32))
    cond[0] = cond[1]
    cond[length_z + 1] = cond[length_z]
    mean_cond = jnp.sum(total) / (8 * length_y * length_z)
    shift_re = shift[0]
    shift_im = shift[1]
    scale = relax / mean_cond
    offset_re = shift_re / mean_cond
    diag_im = shift_im / mean_cond
    none = jnp.zeros((modes, length_y), jnp.float32)
    one = jnp.ones((modes, length_y), jnp.float32)
    row_lane = lax.broadcasted_iota(jnp.int32, (8, length_y), 1)
    last = length_y - 1

    def make_faces(index, carry):
        level = first_level + index
        here = cond[level + 1]
        right = jnp.where(row_lane == last, here, pltpu.roll(here, last, 1))
        left = jnp.where(row_lane == 0, here, pltpu.roll(here, 1, 1))
        face_yp = 0.5 * (here + right)
        face_ym = 0.5 * (here + left)
        face_zp = 0.5 * (here + cond[level + 2])
        face_zm = 0.5 * (here + cond[level])
        faces[index, 0] = here
        faces[index, 1] = face_yp + face_ym + face_zp + face_zm + shift_re
        faces[index, 2] = jnp.where(row_lane == last, 0.0, face_yp)
        faces[index, 3] = jnp.where(row_lane == 0, 0.0, face_ym)
        faces[index, 4] = face_zp
        faces[index, 5] = face_zm
        return carry

    lax.fori_loop(0, depth, make_faces, 0)

    def eigen(chunk):
        return jnp.concatenate([mode_eig[chunk]] * (length_y // 128), axis=1)

    def factors(chunk):
        diag_re = eigen(chunk) + (eig_y[0:1, :] + offset_re)

        def factor(level, carry):
            gap_re = diag_re - carry[0]
            gap_im = diag_im - carry[1]
            inverse = 1.0 / (gap_re * gap_re + gap_im * gap_im)
            now = (gap_re * inverse, -gap_im * inverse)
            put(alpha, now, chunk, level)
            return now

        def segment(index, carry):
            def inner_level(level, state):
                now = factor(index * depth + level + 1, state[:2])
                return (*now, *times(now, state[2:]))

            state = lax.fori_loop(0, depth, inner_level, (*carry, one, none))
            put(lines, state[2:], chunk, index)
            return state[:2]

        put(alpha, (none, none), chunk, 0)
        lax.fori_loop(0, teams, segment, (none, none))

    sine = (sine_hi[...], sine_lo[...])

    def sine_rows(values):
        flat = values.reshape(values.shape[0] * 2 * modes, length_y)
        return dot3(split(flat), sine).reshape(values.shape)

    def launch(turn_id, chunk):
        def rise(index, carry):
            up = times(
                pair(alpha, chunk, first_level + index + 1),
                plus(pair(work, chunk, index), carry[:2]),
            )
            down = times(
                pair(alpha, chunk, last_level + index + 1),
                plus(pair(work, chunk, depth - 1 - index), carry[2:]),
            )
            return (*up, *down)

        ends = lax.fori_loop(0, depth, rise, (none, none, none, none))
        put(pair_out, choose(even, ends[:2], ends[2:]), turn_id, chunk)
        pair_copy(turn_id, chunk).start()
        put(rest_out, choose(even, ends[2:], ends[:2]), turn_id, chunk)

    def relay(turn_id, chunk):
        pair_copy(turn_id, chunk).wait_recv()

        @pl.when(inner)
        def _():
            more = times(pair(lines, chunk, 1), pair(pair_in, turn_id, chunk))
            put(comb_out, plus(pair(rest_out, turn_id, chunk), more), turn_id, chunk)
            comb_copy(turn_id, chunk, 1).start()
            comb_copy(turn_id, chunk, 0).start()

    def solve(turn_id, chunk):
        comb_copy(turn_id, chunk, 0).wait_recv()
        near = pair(pair_in, turn_id, chunk)
        wide = pair(comb_in, turn_id, chunk)
        joined = plus(near, times(pair(lines, chunk, teams - 2), wide))
        far = choose(inner, wide, joined)
        near = choose(inner, near, (none, none))
        below = choose(lower, near, far)
        above = choose(lower, far, near)

        def ahead(index, carry):
            factor = pair(alpha, chunk, first_level + index + 1)
            now = times(factor, plus(pair(work, chunk, index), carry))
            put(work, now, chunk, index)
            return now

        reached = lax.fori_loop(0, depth, ahead, below)
        factor = pair(alpha, chunk, first_level + depth)
        edge = pair(alpha, chunk, last_level)
        echo = times(factor, edge)
        gap_re = 1.0 - echo[0]
        inverse = 1.0 / (gap_re * gap_re + echo[1] * echo[1])
        top = plus(reached, times(factor, above))
        top = times(top, (gap_re * inverse, echo[1] * inverse))
        outer = plus(above, times(edge, top))
        put(work, outer, chunk, depth + 1)

        def behind(step, carry):
            index = depth - 1 - step
            factor = pair(alpha, chunk, first_level + index + 1)
            now = plus(pair(work, chunk, index), times(factor, carry))
            put(work, now, chunk, index)
            return now

        bottom = lax.fori_loop(0, depth, behind, outer)
        put(work, plus(below, times(pair(alpha, chunk, first_level), bottom)), chunk, depth)

    def blocks(values):
        return values.reshape(modes // 8, 8, length_y)

    def residual(chunk):
        eig = blocks(eigen(chunk))

        def run(index, carry):
            given_sum, rest_sum = carry
            center = faces[index, 0] * eig + faces[index, 1]
            values = pair(field, chunk, index + 1)
            turned = (-shift_im * values[1], shift_im * values[0])
            above = pair(field, chunk, index + 2)
            below = pair(field, chunk, index)
            for part in range(2):
                value = values[part]
                applied = center * blocks(value) + blocks(turned[part])
                applied = applied - faces[index, 2] * blocks(pltpu.roll(value, last, 1))
                applied = applied - faces[index, 3] * blocks(pltpu.roll(value, 1, 1))
                applied = applied - faces[index, 4] * blocks(above[part])
                applied = applied - faces[index, 5] * blocks(below[part])
                given = forcing[chunk, index, part]
                rest = given - applied.reshape(modes, length_y)
                work[chunk, index, part] = rest
                given_sum = given_sum + given * given
                rest_sum = rest_sum + rest * rest
            return (given_sum, rest_sum)

        given_sum, rest_sum = lax.fori_loop(0, depth, run, (none, none))
        squares[0] = squares[0] + given_sum
        squares[1] = squares[1] + rest_sum

    squares[0] = none
    squares[1] = none
    factors(0)

    def step(index, carry):
        @pl.when(index < chunks)
        def _():
            chunk = index
            for offset in range(1, RADIX):
                in_copy(chunk, offset).wait()
            work[chunk, pl.ds(0, depth)] = sine_rows(forcing[chunk])
            launch(0, chunk)

        def at(lag, act):
            @pl.when((index >= lag) & (index < chunks + lag))
            def _():
                act(index - lag)

        at(LAGS[0], functools.partial(relay, 0))
        at(LAGS[2], functools.partial(relay, 1))

        def finish(chunk):
            solve(1, chunk)
            values = sine_rows(work[chunk, pl.ds(0, depth)]) * scale
            result[chunk] = field[chunk, pl.ds(1, depth)] + values
            for offset in (2, 3, 1):
                out_copy(chunk, offset).start()
            own_copy(chunk).start()

        at(LAGS[3], finish)

        def middle(chunk):
            solve(0, chunk)
            values = sine_rows(work[chunk]) * scale
            field[chunk, pl.ds(1, depth)] = values[:depth]
            field[chunk, 0] = values[depth]
            field[chunk, depth + 1] = values[depth + 1]
            residual(chunk)
            work[chunk, pl.ds(0, depth)] = sine_rows(work[chunk, pl.ds(0, depth)])
            launch(1, chunk)

        at(LAGS[1], middle)

        @pl.when(index + 1 < chunks)
        def _():
            factors(index + 1)

        @pl.when(index == chunks - 1 + LAGS[1])
        def _():
            row = lax.broadcasted_iota(jnp.int32, (ITERS, 128), 0)
            both = jnp.where(row == 0, jnp.sum(squares[0]), jnp.sum(squares[1]))
            sum_own[...] = both / length_x

            @each_peer
            def _(offset):
                sum_copy(offset).start()

            pltpu.make_async_copy(sum_own, sums.at[me], own_sem.at[chunks]).start()

        return carry

    lax.fori_loop(0, chunks + LAGS[3], step, 0)

    def settle(chunk, carry):
        for turn_id in range(2):
            pair_copy(turn_id, chunk).wait_send()

            @pl.when(inner)
            def _():
                comb_copy(turn_id, chunk, 0).wait_send()
                comb_copy(turn_id, chunk, 1).wait_send()

        own_copy(chunk).wait()
        for offset in range(1, RADIX):
            out_copy(chunk, offset).wait()
        return carry

    pltpu.make_async_copy(sum_own, sums.at[me], own_sem.at[chunks]).wait()

    @each_peer
    def _(offset):
        sum_copy(offset).wait()

    lax.fori_loop(0, chunks, settle, 0)


def ending(
    cells, slabs_hbm, bwd_hi_hbm, bwd_lo_hbm, sums, out, norms, slabs, bwd_hi, bwd_lo, stage, sem, out_sem
):
    chunks, planes, _, modes, length_y = slabs.shape[1:]
    count = chunks * modes

    def load(residue, plane):
        return pltpu.make_async_copy(
            slabs_hbm.at[residue, :, plane], slabs.at[residue, :, plane], sem.at[residue, plane]
        )

    tables = [
        [
            pltpu.make_async_copy(src.at[residue], dst.at[residue], sem.at[residue, planes + index])
            for index, (src, dst) in enumerate([(bwd_hi_hbm, bwd_hi), (bwd_lo_hbm, bwd_lo)])
        ]
        for residue in range(RADIX)
    ]
    for residue in range(RADIX):
        load(residue, 0).start()
        for table in tables[residue]:
            table.start()
    for plane in range(1, planes):
        for residue in range(RADIX):
            load(residue, plane).start()

    def store(plane, q):
        return pltpu.make_async_copy(
            stage.at[:, plane, pl.ds(q * count, count), :],
            out.at[:, plane, pl.ds(q * count, count), :],
            out_sem.at[plane, q],
        )

    for plane in range(planes):
        parts = []
        for residue in range(RADIX):
            load(residue, plane).wait()
            if plane == 0:
                for table in tables[residue]:
                    table.wait()
            blocks = [
                slabs[residue, chunk, plane, part] for part in range(2) for chunk in range(chunks)
            ]
            right = split(jnp.concatenate(blocks, axis=0))
            values = dot3((bwd_hi[residue], bwd_lo[residue]), right)
            parts.append((values[:count], values[count:]))
        for q in range(RADIX):
            re, im = combine(parts, [residue * q for residue in range(RADIX)])
            stage[0, plane, q * count : (q + 1) * count, :] = re
            stage[1, plane, q * count : (q + 1) * count, :] = im
            store(plane, q).start()
    total = jnp.sqrt(jnp.sum(sums[...], axis=0) / cells)
    for index in range(ITERS):
        norms[index] = total[index, 0]
    for plane in range(planes):
        for q in range(RADIX):
            store(plane, q).wait()


CHUNKS = 8
LAGS = (1, 3, 4, 6)


def body(source, layer_ids, conduct_table, shift):
    planes = source.shape[1]
    length_x = source.shape[2]
    length_y = source.shape[3]
    groups = lax.axis_size("gz")
    length_z = planes * groups
    count = length_x // RADIX
    modes = count // CHUNKS
    if groups != 4 * RADIX or modes % 8 or planes > 8 or length_z > 64 or length_y % 128:
        return body_plain(source, layer_ids, conduct_table, shift)
    depth = planes * RADIX
    layers = conduct_table.shape[0]
    mode_ids = RADIX * np.arange(count)[None, :] + np.arange(RADIX)[:, None]
    mode_eig = (2.0 - 2.0 * np.cos(2.0 * np.pi / length_x * mode_ids)).astype(np.float32)
    mode_eig = np.broadcast_to(mode_eig[:, :, None], (RADIX, count, 128))
    mode_eig = np.ascontiguousarray(mode_eig).reshape(RADIX, CHUNKS, modes, 128)
    eig_y = 4.0 - 2.0 * np.cos(np.pi / (length_y + 1) * (np.arange(length_y) + 1.0))
    eig_y = np.ascontiguousarray(np.broadcast_to(eig_y.astype(np.float32), (8, length_y)))
    forward, backward = radix_tables(length_x)
    tables = [*halves(forward), *halves(sine_host(length_y))]
    tile = (2, modes, length_y)
    smem = pl.BlockSpec(memory_space=pltpu.SMEM)
    hbm = pl.BlockSpec(memory_space=pl.ANY)
    f32 = jnp.float32
    dma = pltpu.SemaphoreType.DMA
    slabs, sums = pl.pallas_call(
        functools.partial(kernel, groups, planes, CHUNKS, layers),
        out_shape=(
            jax.ShapeDtypeStruct((RADIX, CHUNKS, planes, *tile), f32),
            jax.ShapeDtypeStruct((groups, ITERS, 128), f32),
        ),
        in_specs=[hbm] * 2 + [smem] * 2 + [hbm] * 6,
        out_specs=(hbm, hbm),
        scratch_shapes=[
            pltpu.VMEM(source.shape, f32),
            pltpu.VMEM(layer_ids.shape, jnp.int32),
            pltpu.VMEM((CHUNKS, modes, 128), f32),
            pltpu.VMEM((8, length_y), f32),
        ]
        + [pltpu.VMEM(table.shape, jnp.bfloat16) for table in tables]
        + [
            pltpu.VMEM((RADIX, CHUNKS, planes, *tile), f32),
            pltpu.VMEM((CHUNKS, depth, *tile), f32),
            pltpu.VMEM((planes, length_y), f32),
            pltpu.VMEM((groups, planes, length_y), f32),
            pltpu.VMEM((length_z + 2, 8, length_y), f32),
            pltpu.VMEM((depth, 6, 8, length_y), f32),
            pltpu.VMEM((CHUNKS, depth + 2, *tile), f32),
            pltpu.VMEM((CHUNKS, length_z + 1, *tile), f32),
            pltpu.VMEM((CHUNKS, groups // RADIX, *tile), f32),
            pltpu.VMEM((CHUNKS, depth + 2, *tile), f32),
            pltpu.VMEM((CHUNKS, depth, *tile), f32),
            pltpu.VMEM((ITERS, 128), f32),
            pltpu.VMEM(tile, f32),
        ]
        + [pltpu.VMEM((ITERS, CHUNKS, *tile), f32)] * 5
        + [dma((8,))]
        + [dma((CHUNKS, RADIX))] * 2
        + [dma((groups,))] * 2
        + [dma((CHUNKS, RADIX))] * 2
        + [dma((groups,))] * 2
        + [dma((CHUNKS + 1,))]
        + [dma((ITERS, CHUNKS))] * 2
        + [dma((ITERS, CHUNKS, 2)), dma((ITERS, CHUNKS))],
        compiler_params=pltpu.CompilerParams(
            collective_id=0, has_side_effects=True, vmem_limit_bytes=58 << 20
        ),
    )(source, layer_ids, conduct_table, shift, jnp.asarray(mode_eig), jnp.asarray(eig_y), *tables)
    cells = length_x * length_y * length_z
    back = halves(backward)
    vmem = pl.BlockSpec(memory_space=pltpu.VMEM)
    return pl.pallas_call(
        functools.partial(ending, cells),
        out_shape=(
            jax.ShapeDtypeStruct(source.shape, f32),
            jax.ShapeDtypeStruct((ITERS,), f32),
        ),
        in_specs=[hbm] * 3 + [vmem],
        out_specs=(hbm, smem),
        scratch_shapes=[
            pltpu.VMEM(slabs.shape, f32),
            pltpu.VMEM(back[0].shape, jnp.bfloat16),
            pltpu.VMEM(back[1].shape, jnp.bfloat16),
            pltpu.VMEM(source.shape, f32),
            dma((RADIX, planes + 2)),
            dma((planes, RADIX)),
        ],
        compiler_params=pltpu.CompilerParams(vmem_limit_bytes=32 << 20),
    )(slabs, *back, sums)


def solution(mesh):
    placed = (P(None, ("node", "gz"), None, None), P(("node", "gz"), None), P(), P("node"))
    return jax.shard_map(
        body,
        mesh=mesh,
        in_specs=placed,
        out_specs=(P(None, ("node", "gz"), None, None), P("node")),
        check_vma=False,
    )
```

```python
import functools

import jax
import jax.numpy as jnp
import numpy as np
from jax import lax
from jax.experimental import pallas as pl
from jax.experimental.pallas import tpu as pltpu
from jax.sharding import PartitionSpec as P

ITERS = 2


relax = 0.6
highest = lax.Precision.HIGH


def with_halo(cells, sides, width):
    for axis, dim in sides:
        count = lax.axis_size(axis)
        ends = count - 1
        head = lax.slice_in_dim(cells, 0, width, axis=dim)
        tail = lax.slice_in_dim(cells, cells.shape[dim] - width, cells.shape[dim], axis=dim)
        cells = jnp.concatenate(
            [
                lax.ppermute(tail, axis, [(i, (i + 1) % count) for i in range(ends)]),
                cells,
                lax.ppermute(head, axis, [((i + 1) % count, i) for i in range(ends)]),
            ],
            axis=dim,
        )
    return cells


def sine_table(length):
    indices = lax.iota(jnp.int32, length) + 1
    product = indices[:, None] * indices[None, :] % (2 * (length + 1))
    return jnp.sqrt(2.0 / (length + 1)) * jnp.sin(
        jnp.pi / (length + 1) * product.astype(jnp.float32)
    )


def sine_eigen(length):
    indices = lax.iota(jnp.float32, length) + 1.0
    return 2.0 - 2.0 * jnp.cos(jnp.pi / (length + 1) * indices)


def dft_tables(length):
    indices = lax.iota(jnp.int32, length)
    product = indices[:, None] * indices[None, :] % length
    angles = 2.0 * jnp.pi / length * product.astype(jnp.float32)
    return (jnp.cos(angles), jnp.sin(angles))


def transform(field, cos_t, sin_t, inverse):

    def project(component, matrix):
        return jnp.einsum("zxy,xk->zky", component, matrix, precision=highest)

    re_cos = project(field[0], cos_t)
    re_sin = project(field[0], sin_t)
    im_cos = project(field[1], cos_t)
    im_sin = project(field[1], sin_t)
    if inverse:
        return jnp.stack([re_cos - im_sin, im_cos + re_sin]) / cos_t.shape[0]
    return jnp.stack([re_cos + im_sin, im_cos - re_sin])


def expand(weights):
    return weights[None, :, None, :]


def yz_part(field, upper, lower, conduct, cond_hi, cond_lo):
    cond_pad = jnp.pad(conduct, ((0, 0), (1, 1)), mode="edge")
    face_yp = 0.5 * (conduct + cond_pad[:, 2:])
    face_ym = 0.5 * (conduct + cond_pad[:, :-2])
    face_zp = 0.5 * (conduct + cond_hi)
    face_zm = 0.5 * (conduct + cond_lo)
    field_pad = jnp.pad(field, ((0, 0), (0, 0), (0, 0), (1, 1)))
    total = expand(face_yp) * (field - field_pad[..., 2:]) + expand(face_ym) * (
        field - field_pad[..., :-2]
    )
    return total + expand(face_zp) * (field - upper) + expand(face_zm) * (field - lower)


def shift_mult(shift_re, shift_im, field):
    return jnp.stack(
        [shift_re * field[0] - shift_im * field[1], shift_re * field[1] + shift_im * field[0]]
    )


def sine_both(field, sine_y, sine_z):
    field = jnp.einsum("pzxy,yj->pzxj", field, sine_y, precision=highest)
    return jnp.einsum("pzxy,zk->pkxy", field, sine_z, precision=highest)


def precondition(coeffs, mode_eig, mean_cond, shift_re, shift_im, sine_y, sine_z, eig_y, eig_z):
    coeffs = sine_both(coeffs, sine_y, sine_z)
    eigen = eig_z[:, None, None] + mode_eig[None, :, None] + eig_y[None, None, :]
    real_den = shift_re + mean_cond * eigen
    inv = 1.0 / (real_den * real_den + shift_im * shift_im)
    scaled = jnp.stack(
        [
            (coeffs[0] * real_den + coeffs[1] * shift_im) * inv,
            (coeffs[1] * real_den - coeffs[0] * shift_im) * inv,
        ]
    )
    return sine_both(scaled, sine_y, sine_z)


def body_plain(source, layer_ids, conduct_table, shift):
    shift_re = shift[0]
    shift_im = shift[1]
    planes = source.shape[1]
    length_x = source.shape[2]
    length_y = source.shape[3]
    groups = lax.axis_size("gz")
    length_z = planes * groups
    modes = length_x // groups
    first_mode = lax.axis_index("gz") * modes
    layers = conduct_table.shape[0]
    onehot = layer_ids[:, :, None] == lax.iota(jnp.int32, layers)[None, None, :]
    local = jnp.sum(jnp.where(onehot, conduct_table[None, None, :], 0.0), axis=-1)
    conduct = lax.all_gather(local, "gz", axis=0, tiled=True)
    mean_cond = jnp.sum(conduct) / (length_y * length_z)
    cond_z = jnp.pad(conduct, ((1, 1), (0, 0)), mode="edge")
    cos_t, sin_t = dft_tables(length_x)
    sine_y = sine_table(length_y)
    sine_z = sine_table(length_z)
    eig_y = sine_eigen(length_y)
    eig_z = sine_eigen(length_z)
    mode_ids = (first_mode + lax.iota(jnp.int32, modes)).astype(jnp.float32)
    mode_eig = 2.0 - 2.0 * jnp.cos(2.0 * jnp.pi / length_x * mode_ids)
    cells = length_x * length_y * length_z
    spectra = transform(source, cos_t, sin_t, False)
    forcing = lax.all_to_all(spectra, "gz", split_axis=2, concat_axis=1, tiled=True)
    partials = []
    solution = jnp.zeros_like(forcing)
    for iteration in range(ITERS):
        if iteration == 0:
            resid = forcing
        else:
            padded = jnp.pad(solution, ((0, 0), (1, 1), (0, 0), (0, 0)))
            lap = expand(conduct) * mode_eig[None, None, :, None] * solution
            lap = lap + yz_part(
                solution, padded[:, 2:], padded[:, :-2], conduct, cond_z[2:], cond_z[:-2]
            )
            resid = forcing - (shift_mult(shift_re, shift_im, solution) + lap)
        partials.append(jnp.sum(resid * resid) / length_x)
        update = precondition(
            resid, mode_eig, mean_cond, shift_re, shift_im, sine_y, sine_z, eig_y, eig_z
        )
        solution = solution + relax * update
    slabs = lax.all_to_all(solution, "gz", split_axis=1, concat_axis=2, tiled=True)
    result = transform(slabs, cos_t, sin_t, True)
    sums = jnp.sum(lax.all_gather(jnp.stack(partials)[None, :], "gz", axis=0, tiled=True), axis=0)
    return (result, jnp.sqrt(sums / cells))


RADIX = 4


def halves(table):
    high = table.astype(jnp.bfloat16)
    low = (table - high.astype(np.float32)).astype(jnp.bfloat16)
    return (jnp.asarray(high), jnp.asarray(low))


def radix_tables(length_x):
    count = length_x // RADIX
    pos = np.arange(count)
    forward = []
    for residue in range(RADIX):
        modes = RADIX * pos + residue
        angle = 2.0 * np.pi / length_x * (modes[:, None] * pos[None, :] % length_x)
        cos_t, sin_t = np.cos(angle), np.sin(angle)
        forward.append(np.block([[cos_t, sin_t], [-sin_t, cos_t]]))
    forward = np.stack(forward)
    backward = np.swapaxes(forward, 1, 2) / length_x
    return (forward.astype(np.float32), backward.astype(np.float32))


def sine_host(length):
    indices = np.arange(length) + 1
    product = indices[:, None] * indices[None, :] % (2 * (length + 1))
    return (np.sqrt(2.0 / (length + 1)) * np.sin(np.pi / (length + 1) * product)).astype(np.float32)


def split(values):
    high = values.astype(jnp.bfloat16)
    return (high, (values - high.astype(jnp.float32)).astype(jnp.bfloat16))


def dot3(left, right):
    mul = functools.partial(jnp.dot, preferred_element_type=jnp.float32)
    return mul(left[0], right[0]) + (mul(left[0], right[1]) + mul(left[1], right[0]))


def dot_wide(left, right):
    wide = jnp.concatenate([left[0], left[1], left[0]], axis=1)
    return jnp.dot(wide, right, preferred_element_type=jnp.float32)


def turn(re, im, quarter):
    quarter = quarter % 4
    return [(re, im), (-im, re), (-re, -im), (im, -re)][quarter]


def combine(parts, quarters):
    re, im = turn(*parts[0], quarters[0])
    for part, quarter in zip(parts[1:], quarters[1:]):
        more_re, more_im = turn(*part, quarter)
        re, im = re + more_re, im + more_im
    return (re, im)


def times(left, right):
    return (left[0] * right[0] - left[1] * right[1], left[0] * right[1] + left[1] * right[0])


def plus(left, right):
    return (left[0] + right[0], left[1] + right[1])


def pair(ref, *index):
    return (ref[(*index, 0)], ref[(*index, 1)])


def put(ref, values, *index):
    ref[(*index, 0)] = values[0]
    ref[(*index, 1)] = values[1]


def choose(test, left, right):
    return (jnp.where(test, left[0], right[0]), jnp.where(test, left[1], right[1]))


def kernel(
    groups,
    planes,
    chunks,
    layers,
    source_hbm,
    ids_hbm,
    table,
    shift,
    mode_hbm,
    eig_hbm,
    fwd_hi_hbm,
    fwd_lo_hbm,
    sine_hi_hbm,
    sine_lo_hbm,
    slabs,
    sums,
    source,
    ids,
    mode_eig,
    eig_y,
    fwd_hi,
    fwd_lo,
    sine_hi,
    sine_lo,
    spectra,
    forcing,
    cond_own,
    cond_all,
    cond,
    faces,
    work,
    alpha,
    lines,
    field,
    result,
    sum_own,
    squares,
    pair_out,
    pair_in,
    rest_out,
    comb_out,
    comb_in,
    load_sem,
    in_send,
    in_recv,
    cond_send,
    cond_recv,
    out_send,
    out_recv,
    sum_send,
    sum_recv,
    own_sem,
    pair_send,
    pair_recv,
    comb_send,
    comb_recv,
):
    me = lax.axis_index("gz")
    side = lax.rem(me, RADIX)
    team = me // RADIX
    teams = groups // RADIX
    length_x = source.shape[2]
    length_y = source.shape[3]
    length_z = groups * planes
    depth = RADIX * planes
    count = length_x // RADIX
    modes = count // chunks
    first_level = team * depth
    last_level = length_z - first_level - depth

    loads = [
        pltpu.make_async_copy(src, dst, load_sem.at[index])
        for index, (src, dst) in enumerate(
            [
                (source_hbm, source),
                (fwd_hi_hbm, fwd_hi),
                (fwd_lo_hbm, fwd_lo),
                (ids_hbm, ids),
                (mode_hbm.at[side], mode_eig),
                (eig_hbm, eig_y),
                (sine_hi_hbm, sine_hi),
                (sine_lo_hbm, sine_lo),
            ]
        )
    ]
    for load in [loads[3], *loads[:3], *loads[4:]]:
        load.start()

    def remote(src, dst, send, recv, target):
        return pltpu.make_async_remote_copy(
            src_ref=src,
            dst_ref=dst,
            send_sem=send,
            recv_sem=recv,
            device_id={"gz": target},
            device_id_type=pl.DeviceIdType.MESH,
        )

    def peer(offset):
        return lax.rem(me + offset, groups)

    def mate(offset):
        return lax.rem(side + offset, RADIX)

    def rows(index):
        return pl.ds(index * planes, planes)

    def cond_copy(offset):
        return remote(
            cond_own, cond_all.at[me], cond_send.at[offset], cond_recv.at[offset], peer(offset)
        )

    def sum_copy(offset):
        return remote(
            sum_own, sums.at[me], sum_send.at[offset], sum_recv.at[offset], peer(offset)
        )

    def in_copy(chunk, offset):
        target = mate(offset)
        return remote(
            spectra.at[target, chunk],
            forcing.at[chunk, rows(side)],
            in_send.at[chunk, offset],
            in_recv.at[chunk, offset],
            team * RADIX + target,
        )

    def out_copy(chunk, offset):
        target = mate(offset)
        return remote(
            result.at[chunk, rows(target)],
            slabs.at[side, chunk],
            out_send.at[chunk, offset],
            out_recv.at[chunk, offset],
            team * RADIX + target,
        )

    def own_copy(chunk):
        return pltpu.make_async_copy(
            result.at[chunk, rows(side)], slabs.at[side, chunk], own_sem.at[chunk]
        )

    even = lax.rem(team, 2) == 0
    inner = (team == 1) | (team == 2)
    lower = team < 2
    partner = team + 1 - 2 * lax.rem(team, 2)

    def pair_copy(turn_id, chunk):
        return remote(
            pair_out.at[turn_id, chunk],
            pair_in.at[turn_id, chunk],
            pair_send.at[turn_id, chunk],
            pair_recv.at[turn_id, chunk],
            partner * RADIX + side,
        )

    def comb_copy(turn_id, chunk, which):
        target = [teams - 1 - team, (teams - 1) * (2 - team)][which]
        return remote(
            comb_out.at[turn_id, chunk],
            comb_in.at[turn_id, chunk],
            comb_send.at[turn_id, chunk, which],
            comb_recv.at[turn_id, chunk],
            target * RADIX + side,
        )

    def each_peer(act):
        def run(offset, carry):
            act(offset)
            return carry

        lax.fori_loop(1, groups, run, 0)

    barrier = pltpu.get_barrier_semaphore()

    @each_peer
    def _(offset):
        pl.semaphore_signal(
            barrier, inc=1, device_id={"gz": peer(offset)}, device_id_type=pl.DeviceIdType.MESH
        )

    loads[3].wait()
    found = jnp.zeros((planes, length_y), jnp.float32)
    for layer in range(layers):
        found = found + jnp.where(ids[...] == layer, table[layer], 0.0)
    cond_own[...] = found
    cond_all[me] = found
    for load in loads[:3]:
        load.wait()

    def forward(plane, carry):
        parts = [
            (
                source[0, plane, q * count : (q + 1) * count, :],
                source[1, plane, q * count : (q + 1) * count, :],
            )
            for q in range(RADIX)
        ]
        for residue in range(RADIX):
            mixed = combine(parts, [-residue * q for q in range(RADIX)])
            right = split(jnp.concatenate(mixed, axis=0))
            values = dot3((fwd_hi[residue], fwd_lo[residue]), right)
            for chunk in range(chunks):
                for part in range(2):
                    start = part * count + chunk * modes
                    spectra[residue, chunk, plane, part] = values[start : start + modes]
        return carry

    lax.fori_loop(0, planes, forward, 0)
    pl.semaphore_wait(barrier, groups - 1)

    @each_peer
    def _(offset):
        cond_copy(offset).start()

    def send_in(chunk, carry):
        for offset in (2, 3, 1):
            in_copy(chunk, offset).start()
        return carry

    lax.fori_loop(0, chunks, send_in, 0)

    def keep(chunk, carry):
        forcing[chunk, rows(side)] = spectra[side, chunk]
        return carry

    lax.fori_loop(0, chunks, keep, 0)
    for load in loads[4:]:
        load.wait()

    @each_peer
    def _(offset):
        cond_copy(offset).wait()

    def spread(index, total):
        for plane in range(planes):
            row = jnp.broadcast_to(cond_all[index, plane : plane + 1, :], (8, length_y))
            cond[index * planes + plane + 1] = row
            total = total + row
        return total

    total = lax.fori_loop(0, groups, spread, jnp.zeros((8, length_y), jnp.float32))
    cond[0] = cond[1]
    cond[length_z + 1] = cond[length_z]
    mean_cond = jnp.sum(total) / (8 * length_y * length_z)
    shift_re = shift[0]
    shift_im = shift[1]
    scale = relax / mean_cond
    offset_re = shift_re / mean_cond
    diag_im = shift_im / mean_cond
    none = jnp.zeros((modes, length_y), jnp.float32)
    one = jnp.ones((modes, length_y), jnp.float32)
    row_lane = lax.broadcasted_iota(jnp.int32, (8, length_y), 1)
    last = length_y - 1

    def make_faces(index, carry):
        level = first_level + index
        here = cond[level + 1]
        right = jnp.where(row_lane == last, here, pltpu.roll(here, last, 1))
        left = jnp.where(row_lane == 0, here, pltpu.roll(here, 1, 1))
        face_yp = 0.5 * (here + right)
        face_ym = 0.5 * (here + left)
        face_zp = 0.5 * (here + cond[level + 2])
        face_zm = 0.5 * (here + cond[level])
        faces[index, 0] = here
        faces[index, 1] = face_yp + face_ym + face_zp + face_zm + shift_re
        faces[index, 2] = jnp.where(row_lane == last, 0.0, face_yp)
        faces[index, 3] = jnp.where(row_lane == 0, 0.0, face_ym)
        faces[index, 4] = face_zp
        faces[index, 5] = face_zm
        return carry

    lax.fori_loop(0, depth, make_faces, 0)

    def eigen(chunk):
        return jnp.concatenate([mode_eig[chunk]] * (length_y // 128), axis=1)

    def factors(chunk):
        diag_re = eigen(chunk) + (eig_y[0:1, :] + offset_re)

        def factor(level, carry):
            gap_re = diag_re - carry[0]
            gap_im = diag_im - carry[1]
            inverse = 1.0 / (gap_re * gap_re + gap_im * gap_im)
            now = (gap_re * inverse, -gap_im * inverse)
            put(alpha, now, chunk, level)
            return now

        def segment(index, carry):
            def inner_level(level, state):
                now = factor(index * depth + level + 1, state[:2])
                return (*now, *times(now, state[2:]))

            state = lax.fori_loop(0, depth, inner_level, (*carry, one, none), unroll=True)
            put(lines, state[2:], chunk, index)
            return state[:2]

        put(alpha, (none, none), chunk, 0)
        lax.fori_loop(0, teams, segment, (none, none))

    sine = jnp.concatenate([sine_hi[...], sine_hi[...], sine_lo[...]], axis=0)

    def sine_rows(values):
        flat = values.reshape(values.shape[0] * 2 * modes, length_y)
        return dot_wide(split(flat), sine).reshape(values.shape)

    def launch(turn_id, chunk):
        def rise(index, carry):
            up = times(
                pair(alpha, chunk, first_level + index + 1),
                plus(pair(work, chunk, index), carry[:2]),
            )
            down = times(
                pair(alpha, chunk, last_level + index + 1),
                plus(pair(work, chunk, depth - 1 - index), carry[2:]),
            )
            return (*up, *down)

        ends = lax.fori_loop(0, depth, rise, (none, none, none, none), unroll=True)
        put(pair_out, choose(even, ends[:2], ends[2:]), turn_id, chunk)
        pair_copy(turn_id, chunk).start()
        put(rest_out, choose(even, ends[2:], ends[:2]), turn_id, chunk)

    def relay(turn_id, chunk):
        pair_copy(turn_id, chunk).wait_recv()

        @pl.when(inner)
        def _():
            more = times(pair(lines, chunk, 1), pair(pair_in, turn_id, chunk))
            put(comb_out, plus(pair(rest_out, turn_id, chunk), more), turn_id, chunk)
            comb_copy(turn_id, chunk, 1).start()
            comb_copy(turn_id, chunk, 0).start()

    def solve(turn_id, chunk):
        comb_copy(turn_id, chunk, 0).wait_recv()
        near = pair(pair_in, turn_id, chunk)
        wide = pair(comb_in, turn_id, chunk)
        joined = plus(near, times(pair(lines, chunk, teams - 2), wide))
        far = choose(inner, wide, joined)
        near = choose(inner, near, (none, none))
        below = choose(lower, near, far)
        above = choose(lower, far, near)

        def ahead(index, carry):
            factor = pair(alpha, chunk, first_level + index + 1)
            now = times(factor, plus(pair(work, chunk, index), carry))
            put(work, now, chunk, index)
            return now

        reached = lax.fori_loop(0, depth, ahead, below, unroll=True)
        factor = pair(alpha, chunk, first_level + depth)
        edge = pair(alpha, chunk, last_level)
        echo = times(factor, edge)
        gap_re = 1.0 - echo[0]
        inverse = 1.0 / (gap_re * gap_re + echo[1] * echo[1])
        top = plus(reached, times(factor, above))
        top = times(top, (gap_re * inverse, echo[1] * inverse))
        outer = plus(above, times(edge, top))
        put(work, outer, chunk, depth + 1)

        def behind(step, carry):
            index = depth - 1 - step
            factor = pair(alpha, chunk, first_level + index + 1)
            now = plus(pair(work, chunk, index), times(factor, carry))
            put(work, now, chunk, index)
            return now

        bottom = lax.fori_loop(0, depth, behind, outer, unroll=True)
        put(work, plus(below, times(pair(alpha, chunk, first_level), bottom)), chunk, depth)

    def blocks(values):
        return values.reshape(modes // 8, 8, length_y)

    def residual(chunk):
        eig = blocks(eigen(chunk))

        def run(index, carry):
            given_sum, rest_sum = carry
            center = faces[index, 0] * eig + faces[index, 1]
            values = pair(field, chunk, index + 1)
            turned = (-shift_im * values[1], shift_im * values[0])
            above = pair(field, chunk, index + 2)
            below = pair(field, chunk, index)
            for part in range(2):
                value = values[part]
                applied = center * blocks(value) + blocks(turned[part])
                applied = applied - faces[index, 2] * blocks(pltpu.roll(value, last, 1))
                applied = applied - faces[index, 3] * blocks(pltpu.roll(value, 1, 1))
                applied = applied - faces[index, 4] * blocks(above[part])
                applied = applied - faces[index, 5] * blocks(below[part])
                given = forcing[chunk, index, part]
                rest = given - applied.reshape(modes, length_y)
                work[chunk, index, part] = rest
                given_sum = given_sum + given * given
                rest_sum = rest_sum + rest * rest
            return (given_sum, rest_sum)

        given_sum, rest_sum = lax.fori_loop(0, depth, run, (none, none), unroll=4)
        squares[0] = squares[0] + given_sum
        squares[1] = squares[1] + rest_sum

    squares[0] = none
    squares[1] = none
    factors(0)

    def begin(chunk):
        for offset in range(1, RADIX):
            in_copy(chunk, offset).wait()
        work[chunk, pl.ds(0, depth)] = sine_rows(forcing[chunk])
        launch(0, chunk)

    def middle(chunk):
        solve(0, chunk)
        values = sine_rows(work[chunk]) * scale
        field[chunk, pl.ds(1, depth)] = values[:depth]
        field[chunk, 0] = values[depth]
        field[chunk, depth + 1] = values[depth + 1]
        residual(chunk)
        work[chunk, pl.ds(0, depth)] = sine_rows(work[chunk, pl.ds(0, depth)])
        launch(1, chunk)

        @pl.when(chunk == chunks - 1)
        def _():
            row = lax.broadcasted_iota(jnp.int32, (ITERS, 128), 0)
            both = jnp.where(row == 0, jnp.sum(squares[0]), jnp.sum(squares[1]))
            sum_own[...] = both / length_x

            @each_peer
            def _(offset):
                sum_copy(offset).start()

            pltpu.make_async_copy(sum_own, sums.at[me], own_sem.at[chunks]).start()

    def finish(chunk):
        solve(1, chunk)
        values = sine_rows(work[chunk, pl.ds(0, depth)]) * scale
        result[chunk] = field[chunk, pl.ds(1, depth)] + values
        for offset in (2, 3, 1):
            out_copy(chunk, offset).start()
        own_copy(chunk).start()

    def ready(chunk):
        @pl.when(chunk + 1 < chunks)
        def _():
            factors(chunk + 1)

    stages = {
        "begin": (0, begin),
        "ready": (0, ready),
        "relay": (LAGS[0], functools.partial(relay, 0)),
        "middle": (LAGS[1], middle),
        "again": (LAGS[2], functools.partial(relay, 1)),
        "finish": (LAGS[3], finish),
    }

    def step(index, carry):
        for name in ORDER:
            lag, act = stages[name]

            @pl.when((index >= lag) & (index < chunks + lag))
            def _():
                act(index - lag)

        return carry

    lax.fori_loop(0, chunks + LAGS[3], step, 0)

    def settle(chunk, carry):
        for turn_id in range(2):
            pair_copy(turn_id, chunk).wait_send()

            @pl.when(inner)
            def _():
                comb_copy(turn_id, chunk, 0).wait_send()
                comb_copy(turn_id, chunk, 1).wait_send()

        own_copy(chunk).wait()
        for offset in range(1, RADIX):
            out_copy(chunk, offset).wait()
        return carry

    pltpu.make_async_copy(sum_own, sums.at[me], own_sem.at[chunks]).wait()

    @each_peer
    def _(offset):
        sum_copy(offset).wait()

    lax.fori_loop(0, chunks, settle, 0)


def ending(
    cells, slabs_hbm, sums_hbm, bwd_hi, bwd_lo, out, norms, slabs, sums, stage, sem, sum_sem, out_sem
):
    chunks, planes, _, modes, length_y = slabs.shape[1:]
    count = chunks * modes

    def load(residue, plane):
        return pltpu.make_async_copy(
            slabs_hbm.at[residue, :, plane], slabs.at[residue, :, plane], sem.at[residue, plane]
        )

    for plane in range(planes):
        for residue in range(RADIX):
            load(residue, plane).start()
    total = pltpu.make_async_copy(sums_hbm, sums, sum_sem)
    total.start()

    def store(plane, q):
        return pltpu.make_async_copy(
            stage.at[:, plane, pl.ds(q * count, count), :],
            out.at[:, plane, pl.ds(q * count, count), :],
            out_sem.at[plane, q],
        )

    for plane in range(planes):
        parts = []
        for residue in range(RADIX):
            load(residue, plane).wait()
            blocks = [
                slabs[residue, chunk, plane, part] for part in range(2) for chunk in range(chunks)
            ]
            right = split(jnp.concatenate(blocks, axis=0))
            values = dot3((bwd_hi[residue], bwd_lo[residue]), right)
            parts.append((values[:count], values[count:]))
        for q in range(RADIX):
            re, im = combine(parts, [residue * q for residue in range(RADIX)])
            stage[0, plane, q * count : (q + 1) * count, :] = re
            stage[1, plane, q * count : (q + 1) * count, :] = im
            store(plane, q).start()
    total.wait()
    root = jnp.sqrt(jnp.sum(sums[...], axis=0) / cells)
    for index in range(ITERS):
        norms[index] = root[index, 0]
    for plane in range(planes):
        for q in range(RADIX):
            store(plane, q).wait()


CHUNKS = 8
LAGS = (1, 2, 3, 5)
ORDER = ("begin", "relay", "finish", "middle", "ready", "again")


def body(source, layer_ids, conduct_table, shift):
    planes = source.shape[1]
    length_x = source.shape[2]
    length_y = source.shape[3]
    groups = lax.axis_size("gz")
    length_z = planes * groups
    count = length_x // RADIX
    modes = count // CHUNKS
    if groups != 4 * RADIX or modes % 8 or planes > 8 or length_z > 64 or length_y % 128:
        return body_plain(source, layer_ids, conduct_table, shift)
    depth = planes * RADIX
    layers = conduct_table.shape[0]
    mode_ids = RADIX * np.arange(count)[None, :] + np.arange(RADIX)[:, None]
    mode_eig = (2.0 - 2.0 * np.cos(2.0 * np.pi / length_x * mode_ids)).astype(np.float32)
    mode_eig = np.broadcast_to(mode_eig[:, :, None], (RADIX, count, 128))
    mode_eig = np.ascontiguousarray(mode_eig).reshape(RADIX, CHUNKS, modes, 128)
    eig_y = 4.0 - 2.0 * np.cos(np.pi / (length_y + 1) * (np.arange(length_y) + 1.0))
    eig_y = np.ascontiguousarray(np.broadcast_to(eig_y.astype(np.float32), (8, length_y)))
    forward, backward = radix_tables(length_x)
    tables = [*halves(forward), *halves(sine_host(length_y))]
    tile = (2, modes, length_y)
    smem = pl.BlockSpec(memory_space=pltpu.SMEM)
    hbm = pl.BlockSpec(memory_space=pl.ANY)
    f32 = jnp.float32
    dma = pltpu.SemaphoreType.DMA
    slabs, sums = pl.pallas_call(
        functools.partial(kernel, groups, planes, CHUNKS, layers),
        out_shape=(
            jax.ShapeDtypeStruct((RADIX, CHUNKS, planes, *tile), f32),
            jax.ShapeDtypeStruct((groups, ITERS, 128), f32),
        ),
        in_specs=[hbm] * 2 + [smem] * 2 + [hbm] * 6,
        out_specs=(hbm, hbm),
        scratch_shapes=[
            pltpu.VMEM(source.shape, f32),
            pltpu.VMEM(layer_ids.shape, jnp.int32),
            pltpu.VMEM((CHUNKS, modes, 128), f32),
            pltpu.VMEM((8, length_y), f32),
        ]
        + [pltpu.VMEM(table.shape, jnp.bfloat16) for table in tables]
        + [
            pltpu.VMEM((RADIX, CHUNKS, planes, *tile), f32),
            pltpu.VMEM((CHUNKS, depth, *tile), f32),
            pltpu.VMEM((planes, length_y), f32),
            pltpu.VMEM((groups, planes, length_y), f32),
            pltpu.VMEM((length_z + 2, 8, length_y), f32),
            pltpu.VMEM((depth, 6, 8, length_y), f32),
            pltpu.VMEM((CHUNKS, depth + 2, *tile), f32),
            pltpu.VMEM((CHUNKS, length_z + 1, *tile), f32),
            pltpu.VMEM((CHUNKS, groups // RADIX, *tile), f32),
            pltpu.VMEM((CHUNKS, depth + 2, *tile), f32),
            pltpu.VMEM((CHUNKS, depth, *tile), f32),
            pltpu.VMEM((ITERS, 128), f32),
            pltpu.VMEM(tile, f32),
        ]
        + [pltpu.VMEM((ITERS, CHUNKS, *tile), f32)] * 5
        + [dma((8,))]
        + [dma((CHUNKS, RADIX))] * 2
        + [dma((groups,))] * 2
        + [dma((CHUNKS, RADIX))] * 2
        + [dma((groups,))] * 2
        + [dma((CHUNKS + 1,))]
        + [dma((ITERS, CHUNKS))] * 2
        + [dma((ITERS, CHUNKS, 2)), dma((ITERS, CHUNKS))],
        compiler_params=pltpu.CompilerParams(
            collective_id=0, has_side_effects=True, vmem_limit_bytes=58 << 20
        ),
    )(source, layer_ids, conduct_table, shift, jnp.asarray(mode_eig), jnp.asarray(eig_y), *tables)
    cells = length_x * length_y * length_z
    back = halves(backward)
    vmem = pl.BlockSpec(memory_space=pltpu.VMEM)
    return pl.pallas_call(
        functools.partial(ending, cells),
        out_shape=(
            jax.ShapeDtypeStruct(source.shape, f32),
            jax.ShapeDtypeStruct((ITERS,), f32),
        ),
        in_specs=[pl.BlockSpec(memory_space=pltpu.HBM)] * 2 + [vmem] * 2,
        out_specs=(hbm, smem),
        scratch_shapes=[
            pltpu.VMEM(slabs.shape, f32),
            pltpu.VMEM(sums.shape, f32),
            pltpu.VMEM(source.shape, f32),
            dma((RADIX, planes)),
            dma,
            dma((planes, RADIX)),
        ],
        compiler_params=pltpu.CompilerParams(vmem_limit_bytes=62 << 20),
    )(slabs, sums, *back)


def solution(mesh):
    placed = (P(None, ("node", "gz"), None, None), P(("node", "gz"), None), P(), P("node"))
    return jax.shard_map(
        body,
        mesh=mesh,
        in_specs=placed,
        out_specs=(P(None, ("node", "gz"), None, None), P("node")),
        check_vma=False,
    )
```

```python
import functools

import jax
import jax.numpy as jnp
import numpy as np
from jax import lax
from jax.experimental import pallas as pl
from jax.experimental.pallas import tpu as pltpu
from jax.sharding import PartitionSpec as P

ITERS = 2


relax = 0.6
highest = lax.Precision.HIGH


def with_halo(cells, sides, width):
    for axis, dim in sides:
        count = lax.axis_size(axis)
        ends = count - 1
        head = lax.slice_in_dim(cells, 0, width, axis=dim)
        tail = lax.slice_in_dim(cells, cells.shape[dim] - width, cells.shape[dim], axis=dim)
        cells = jnp.concatenate(
            [
                lax.ppermute(tail, axis, [(i, (i + 1) % count) for i in range(ends)]),
                cells,
                lax.ppermute(head, axis, [((i + 1) % count, i) for i in range(ends)]),
            ],
            axis=dim,
        )
    return cells


def sine_table(length):
    indices = lax.iota(jnp.int32, length) + 1
    product = indices[:, None] * indices[None, :] % (2 * (length + 1))
    return jnp.sqrt(2.0 / (length + 1)) * jnp.sin(
        jnp.pi / (length + 1) * product.astype(jnp.float32)
    )


def sine_eigen(length):
    indices = lax.iota(jnp.float32, length) + 1.0
    return 2.0 - 2.0 * jnp.cos(jnp.pi / (length + 1) * indices)


def dft_tables(length):
    indices = lax.iota(jnp.int32, length)
    product = indices[:, None] * indices[None, :] % length
    angles = 2.0 * jnp.pi / length * product.astype(jnp.float32)
    return (jnp.cos(angles), jnp.sin(angles))


def transform(field, cos_t, sin_t, inverse):

    def project(component, matrix):
        return jnp.einsum("zxy,xk->zky", component, matrix, precision=highest)

    re_cos = project(field[0], cos_t)
    re_sin = project(field[0], sin_t)
    im_cos = project(field[1], cos_t)
    im_sin = project(field[1], sin_t)
    if inverse:
        return jnp.stack([re_cos - im_sin, im_cos + re_sin]) / cos_t.shape[0]
    return jnp.stack([re_cos + im_sin, im_cos - re_sin])


def expand(weights):
    return weights[None, :, None, :]


def yz_part(field, upper, lower, conduct, cond_hi, cond_lo):
    cond_pad = jnp.pad(conduct, ((0, 0), (1, 1)), mode="edge")
    face_yp = 0.5 * (conduct + cond_pad[:, 2:])
    face_ym = 0.5 * (conduct + cond_pad[:, :-2])
    face_zp = 0.5 * (conduct + cond_hi)
    face_zm = 0.5 * (conduct + cond_lo)
    field_pad = jnp.pad(field, ((0, 0), (0, 0), (0, 0), (1, 1)))
    total = expand(face_yp) * (field - field_pad[..., 2:]) + expand(face_ym) * (
        field - field_pad[..., :-2]
    )
    return total + expand(face_zp) * (field - upper) + expand(face_zm) * (field - lower)


def shift_mult(shift_re, shift_im, field):
    return jnp.stack(
        [shift_re * field[0] - shift_im * field[1], shift_re * field[1] + shift_im * field[0]]
    )


def sine_both(field, sine_y, sine_z):
    field = jnp.einsum("pzxy,yj->pzxj", field, sine_y, precision=highest)
    return jnp.einsum("pzxy,zk->pkxy", field, sine_z, precision=highest)


def precondition(coeffs, mode_eig, mean_cond, shift_re, shift_im, sine_y, sine_z, eig_y, eig_z):
    coeffs = sine_both(coeffs, sine_y, sine_z)
    eigen = eig_z[:, None, None] + mode_eig[None, :, None] + eig_y[None, None, :]
    real_den = shift_re + mean_cond * eigen
    inv = 1.0 / (real_den * real_den + shift_im * shift_im)
    scaled = jnp.stack(
        [
            (coeffs[0] * real_den + coeffs[1] * shift_im) * inv,
            (coeffs[1] * real_den - coeffs[0] * shift_im) * inv,
        ]
    )
    return sine_both(scaled, sine_y, sine_z)


def body_plain(source, layer_ids, conduct_table, shift):
    shift_re = shift[0]
    shift_im = shift[1]
    planes = source.shape[1]
    length_x = source.shape[2]
    length_y = source.shape[3]
    groups = lax.axis_size("gz")
    length_z = planes * groups
    modes = length_x // groups
    first_mode = lax.axis_index("gz") * modes
    layers = conduct_table.shape[0]
    onehot = layer_ids[:, :, None] == lax.iota(jnp.int32, layers)[None, None, :]
    local = jnp.sum(jnp.where(onehot, conduct_table[None, None, :], 0.0), axis=-1)
    conduct = lax.all_gather(local, "gz", axis=0, tiled=True)
    mean_cond = jnp.sum(conduct) / (length_y * length_z)
    cond_z = jnp.pad(conduct, ((1, 1), (0, 0)), mode="edge")
    cos_t, sin_t = dft_tables(length_x)
    sine_y = sine_table(length_y)
    sine_z = sine_table(length_z)
    eig_y = sine_eigen(length_y)
    eig_z = sine_eigen(length_z)
    mode_ids = (first_mode + lax.iota(jnp.int32, modes)).astype(jnp.float32)
    mode_eig = 2.0 - 2.0 * jnp.cos(2.0 * jnp.pi / length_x * mode_ids)
    cells = length_x * length_y * length_z
    spectra = transform(source, cos_t, sin_t, False)
    forcing = lax.all_to_all(spectra, "gz", split_axis=2, concat_axis=1, tiled=True)
    partials = []
    solution = jnp.zeros_like(forcing)
    for iteration in range(ITERS):
        if iteration == 0:
            resid = forcing
        else:
            padded = jnp.pad(solution, ((0, 0), (1, 1), (0, 0), (0, 0)))
            lap = expand(conduct) * mode_eig[None, None, :, None] * solution
            lap = lap + yz_part(
                solution, padded[:, 2:], padded[:, :-2], conduct, cond_z[2:], cond_z[:-2]
            )
            resid = forcing - (shift_mult(shift_re, shift_im, solution) + lap)
        partials.append(jnp.sum(resid * resid) / length_x)
        update = precondition(
            resid, mode_eig, mean_cond, shift_re, shift_im, sine_y, sine_z, eig_y, eig_z
        )
        solution = solution + relax * update
    slabs = lax.all_to_all(solution, "gz", split_axis=1, concat_axis=2, tiled=True)
    result = transform(slabs, cos_t, sin_t, True)
    sums = jnp.sum(lax.all_gather(jnp.stack(partials)[None, :], "gz", axis=0, tiled=True), axis=0)
    return (result, jnp.sqrt(sums / cells))


RADIX = 4


def halves(table):
    high = table.astype(jnp.bfloat16)
    low = (table - high.astype(np.float32)).astype(jnp.bfloat16)
    return (jnp.asarray(high), jnp.asarray(low))


def radix_tables(length_x):
    count = length_x // RADIX
    pos = np.arange(count)
    forward = []
    for residue in range(RADIX):
        modes = RADIX * pos + residue
        angle = 2.0 * np.pi / length_x * (modes[:, None] * pos[None, :] % length_x)
        cos_t, sin_t = np.cos(angle), np.sin(angle)
        forward.append(np.block([[cos_t, sin_t], [-sin_t, cos_t]]))
    forward = np.stack(forward)
    backward = np.swapaxes(forward, 1, 2) / length_x
    return (forward.astype(np.float32), backward.astype(np.float32))


def sine_host(length):
    indices = np.arange(length) + 1
    product = indices[:, None] * indices[None, :] % (2 * (length + 1))
    return (np.sqrt(2.0 / (length + 1)) * np.sin(np.pi / (length + 1) * product)).astype(np.float32)


def split(values):
    high = values.astype(jnp.bfloat16)
    return (high, (values - high.astype(jnp.float32)).astype(jnp.bfloat16))


def dot3(left, right):
    mul = functools.partial(jnp.dot, preferred_element_type=jnp.float32)
    return mul(left[0], right[0]) + (mul(left[0], right[1]) + mul(left[1], right[0]))


def dot_wide(left, right):
    wide = jnp.concatenate([left[0], left[1], left[0]], axis=1)
    return jnp.dot(wide, right, preferred_element_type=jnp.float32)


def turn(re, im, quarter):
    quarter = quarter % 4
    return [(re, im), (-im, re), (-re, -im), (im, -re)][quarter]


def combine(parts, quarters):
    re, im = turn(*parts[0], quarters[0])
    for part, quarter in zip(parts[1:], quarters[1:]):
        more_re, more_im = turn(*part, quarter)
        re, im = re + more_re, im + more_im
    return (re, im)


def times(left, right):
    return (left[0] * right[0] - left[1] * right[1], left[0] * right[1] + left[1] * right[0])


def plus(left, right):
    return (left[0] + right[0], left[1] + right[1])


def pair(ref, *index):
    return (ref[(*index, 0)], ref[(*index, 1)])


def put(ref, values, *index):
    ref[(*index, 0)] = values[0]
    ref[(*index, 1)] = values[1]


def choose(test, left, right):
    return (jnp.where(test, left[0], right[0]), jnp.where(test, left[1], right[1]))


def kernel(
    groups,
    planes,
    chunks,
    layers,
    source_hbm,
    ids_hbm,
    table_hbm,
    shift_hbm,
    mode_hbm,
    eig_hbm,
    fwd_hi_hbm,
    fwd_lo_hbm,
    sine_hi_hbm,
    sine_lo_hbm,
    slabs,
    sums,
    source,
    ids,
    table,
    shift,
    mode_eig,
    eig_y,
    fwd_hi,
    fwd_lo,
    sine_hi,
    sine_lo,
    spectra,
    forcing,
    cond_own,
    cond_all,
    cond,
    faces,
    work,
    alpha,
    lines,
    field,
    result,
    sum_own,
    squares,
    pair_out,
    pair_in,
    rest_out,
    comb_out,
    comb_in,
    load_sem,
    in_send,
    in_recv,
    cond_send,
    cond_recv,
    out_send,
    out_recv,
    sum_send,
    sum_recv,
    own_sem,
    pair_send,
    pair_recv,
    comb_send,
    comb_recv,
):
    me = lax.axis_index("gz")
    side = lax.rem(me, RADIX)
    team = me // RADIX
    teams = groups // RADIX
    length_x = source.shape[2]
    length_y = source.shape[3]
    length_z = groups * planes
    depth = RADIX * planes
    count = length_x // RADIX
    modes = count // chunks
    first_level = team * depth
    last_level = length_z - first_level - depth

    loads = [
        pltpu.make_async_copy(src, dst, load_sem.at[index])
        for index, (src, dst) in enumerate(
            [
                (source_hbm, source),
                (fwd_hi_hbm, fwd_hi),
                (fwd_lo_hbm, fwd_lo),
                (ids_hbm, ids),
                (mode_hbm.at[side], mode_eig),
                (eig_hbm, eig_y),
                (sine_hi_hbm, sine_hi),
                (sine_lo_hbm, sine_lo),
                (table_hbm, table),
                (shift_hbm, shift),
            ]
        )
    ]
    for load in [loads[3], *loads[8:], *loads[:3], *loads[4:8]]:
        load.start()

    def remote(src, dst, send, recv, target):
        return pltpu.make_async_remote_copy(
            src_ref=src,
            dst_ref=dst,
            send_sem=send,
            recv_sem=recv,
            device_id={"gz": target},
            device_id_type=pl.DeviceIdType.MESH,
        )

    def peer(offset):
        return lax.rem(me + offset, groups)

    def mate(offset):
        return lax.rem(side + offset, RADIX)

    def rows(index):
        return pl.ds(index * planes, planes)

    def cond_copy(offset):
        return remote(
            cond_own, cond_all.at[me], cond_send.at[offset], cond_recv.at[offset], peer(offset)
        )

    def sum_copy(offset):
        return remote(
            sum_own, sums.at[me], sum_send.at[offset], sum_recv.at[offset], peer(offset)
        )

    def in_copy(chunk, offset):
        target = mate(offset)
        return remote(
            spectra.at[target, chunk],
            forcing.at[chunk, rows(side)],
            in_send.at[chunk, offset],
            in_recv.at[chunk, offset],
            team * RADIX + target,
        )

    def out_copy(chunk, offset):
        target = mate(offset)
        return remote(
            result.at[chunk, rows(target)],
            slabs.at[side, chunk],
            out_send.at[chunk, offset],
            out_recv.at[chunk, offset],
            team * RADIX + target,
        )

    def own_copy(chunk):
        return pltpu.make_async_copy(
            result.at[chunk, rows(side)], slabs.at[side, chunk], own_sem.at[chunk]
        )

    even = lax.rem(team, 2) == 0
    inner = (team == 1) | (team == 2)
    lower = team < 2
    partner = team + 1 - 2 * lax.rem(team, 2)

    def pair_copy(turn_id, chunk):
        return remote(
            pair_out.at[turn_id, chunk],
            pair_in.at[turn_id, chunk],
            pair_send.at[turn_id, chunk],
            pair_recv.at[turn_id, chunk],
            partner * RADIX + side,
        )

    def comb_copy(turn_id, chunk, which):
        target = [teams - 1 - team, (teams - 1) * (2 - team)][which]
        return remote(
            comb_out.at[turn_id, chunk],
            comb_in.at[turn_id, chunk],
            comb_send.at[turn_id, chunk, which],
            comb_recv.at[turn_id, chunk],
            target * RADIX + side,
        )

    def each_peer(act):
        def run(offset, carry):
            act(offset)
            return carry

        lax.fori_loop(1, groups, run, 0)

    barrier = pltpu.get_barrier_semaphore()

    @each_peer
    def _(offset):
        pl.semaphore_signal(
            barrier, inc=1, device_id={"gz": peer(offset)}, device_id_type=pl.DeviceIdType.MESH
        )

    loads[3].wait()
    loads[8].wait()
    loads[9].wait()
    found = jnp.zeros((planes, length_y), jnp.float32)
    for layer in range(layers):
        found = found + jnp.where(ids[...] == layer, table[layer], 0.0)
    cond_own[...] = found
    cond_all[me] = found
    for load in loads[:3]:
        load.wait()

    def forward(plane, carry):
        parts = [
            (
                source[0, plane, q * count : (q + 1) * count, :],
                source[1, plane, q * count : (q + 1) * count, :],
            )
            for q in range(RADIX)
        ]
        for residue in range(RADIX):
            mixed = combine(parts, [-residue * q for q in range(RADIX)])
            right = split(jnp.concatenate(mixed, axis=0))
            values = dot3((fwd_hi[residue], fwd_lo[residue]), right)
            for chunk in range(chunks):
                for part in range(2):
                    start = part * count + chunk * modes
                    spectra[residue, chunk, plane, part] = values[start : start + modes]
        return carry

    lax.fori_loop(0, planes, forward, 0)
    pl.semaphore_wait(barrier, groups - 1)

    @each_peer
    def _(offset):
        cond_copy(offset).start()

    def send_in(chunk, carry):
        for offset in (2, 3, 1):
            in_copy(chunk, offset).start()
        return carry

    lax.fori_loop(0, chunks, send_in, 0)

    def keep(chunk, carry):
        forcing[chunk, rows(side)] = spectra[side, chunk]
        return carry

    lax.fori_loop(0, chunks, keep, 0)
    for load in loads[4:8]:
        load.wait()

    @each_peer
    def _(offset):
        cond_copy(offset).wait()

    def spread(index, total):
        for plane in range(planes):
            row = jnp.broadcast_to(cond_all[index, plane : plane + 1, :], (8, length_y))
            cond[index * planes + plane + 1] = row
            total = total + row
        return total

    total = lax.fori_loop(0, groups, spread, jnp.zeros((8, length_y), jnp.float32))
    cond[0] = cond[1]
    cond[length_z + 1] = cond[length_z]
    mean_cond = jnp.sum(total) / (8 * length_y * length_z)
    shift_re = shift[0]
    shift_im = shift[1]
    scale = relax / mean_cond
    offset_re = shift_re / mean_cond
    diag_im = shift_im / mean_cond
    none = jnp.zeros((modes, length_y), jnp.float32)
    one = jnp.ones((modes, length_y), jnp.float32)
    row_lane = lax.broadcasted_iota(jnp.int32, (8, length_y), 1)
    last = length_y - 1

    def make_faces(index, carry):
        level = first_level + index
        here = cond[level + 1]
        right = jnp.where(row_lane == last, here, pltpu.roll(here, last, 1))
        left = jnp.where(row_lane == 0, here, pltpu.roll(here, 1, 1))
        face_yp = 0.5 * (here + right)
        face_ym = 0.5 * (here + left)
        face_zp = 0.5 * (here + cond[level + 2])
        face_zm = 0.5 * (here + cond[level])
        faces[index, 0] = here
        faces[index, 1] = face_yp + face_ym + face_zp + face_zm + shift_re
        faces[index, 2] = jnp.where(row_lane == last, 0.0, face_yp)
        faces[index, 3] = jnp.where(row_lane == 0, 0.0, face_ym)
        faces[index, 4] = face_zp
        faces[index, 5] = face_zm
        return carry

    lax.fori_loop(0, depth, make_faces, 0)

    def eigen(chunk):
        return jnp.concatenate([mode_eig[chunk]] * (length_y // 128), axis=1)

    def factors(chunk):
        diag_re = eigen(chunk) + (eig_y[0:1, :] + offset_re)

        def factor(level, carry):
            gap_re = diag_re - carry[0]
            gap_im = diag_im - carry[1]
            inverse = 1.0 / (gap_re * gap_re + gap_im * gap_im)
            now = (gap_re * inverse, -gap_im * inverse)
            put(alpha, now, chunk, level)
            return now

        def segment(index, carry):
            def inner_level(level, state):
                now = factor(index * depth + level + 1, state[:2])
                return (*now, *times(now, state[2:]))

            state = lax.fori_loop(0, depth, inner_level, (*carry, one, none), unroll=True)
            put(lines, state[2:], chunk, index)
            return state[:2]

        put(alpha, (none, none), chunk, 0)
        lax.fori_loop(0, teams, segment, (none, none))

    sine = jnp.concatenate([sine_hi[...], sine_hi[...], sine_lo[...]], axis=0)

    def sine_rows(values):
        flat = values.reshape(values.shape[0] * 2 * modes, length_y)
        return dot_wide(split(flat), sine).reshape(values.shape)

    def launch(turn_id, chunk):
        def rise(index, carry):
            up = times(
                pair(alpha, chunk, first_level + index + 1),
                plus(pair(work, chunk, index), carry[:2]),
            )
            down = times(
                pair(alpha, chunk, last_level + index + 1),
                plus(pair(work, chunk, depth - 1 - index), carry[2:]),
            )
            return (*up, *down)

        ends = lax.fori_loop(0, depth, rise, (none, none, none, none), unroll=True)
        put(pair_out, choose(even, ends[:2], ends[2:]), turn_id, chunk)
        pair_copy(turn_id, chunk).start()
        put(rest_out, choose(even, ends[2:], ends[:2]), turn_id, chunk)

    def relay(turn_id, chunk):
        pair_copy(turn_id, chunk).wait_recv()

        @pl.when(inner)
        def _():
            more = times(pair(lines, chunk, 1), pair(pair_in, turn_id, chunk))
            put(comb_out, plus(pair(rest_out, turn_id, chunk), more), turn_id, chunk)
            comb_copy(turn_id, chunk, 1).start()
            comb_copy(turn_id, chunk, 0).start()

    def solve(turn_id, chunk):
        comb_copy(turn_id, chunk, 0).wait_recv()
        near = pair(pair_in, turn_id, chunk)
        wide = pair(comb_in, turn_id, chunk)
        joined = plus(near, times(pair(lines, chunk, teams - 2), wide))
        far = choose(inner, wide, joined)
        near = choose(inner, near, (none, none))
        below = choose(lower, near, far)
        above = choose(lower, far, near)

        def ahead(index, carry):
            factor = pair(alpha, chunk, first_level + index + 1)
            now = times(factor, plus(pair(work, chunk, index), carry))
            put(work, now, chunk, index)
            return now

        reached = lax.fori_loop(0, depth, ahead, below, unroll=True)
        factor = pair(alpha, chunk, first_level + depth)
        edge = pair(alpha, chunk, last_level)
        echo = times(factor, edge)
        gap_re = 1.0 - echo[0]
        inverse = 1.0 / (gap_re * gap_re + echo[1] * echo[1])
        top = plus(reached, times(factor, above))
        top = times(top, (gap_re * inverse, echo[1] * inverse))
        outer = plus(above, times(edge, top))
        put(work, outer, chunk, depth + 1)

        def behind(step, carry):
            index = depth - 1 - step
            factor = pair(alpha, chunk, first_level + index + 1)
            now = plus(pair(work, chunk, index), times(factor, carry))
            put(work, now, chunk, index)
            return now

        bottom = lax.fori_loop(0, depth, behind, outer, unroll=True)
        put(work, plus(below, times(pair(alpha, chunk, first_level), bottom)), chunk, depth)

    def blocks(values):
        return values.reshape(modes // 8, 8, length_y)

    def residual(chunk):
        eig = blocks(eigen(chunk))

        def run(index, carry):
            given_sum, rest_sum = carry
            center = faces[index, 0] * eig + faces[index, 1]
            values = pair(field, chunk, index + 1)
            turned = (-shift_im * values[1], shift_im * values[0])
            above = pair(field, chunk, index + 2)
            below = pair(field, chunk, index)
            for part in range(2):
                value = values[part]
                applied = center * blocks(value) + blocks(turned[part])
                applied = applied - faces[index, 2] * blocks(pltpu.roll(value, last, 1))
                applied = applied - faces[index, 3] * blocks(pltpu.roll(value, 1, 1))
                applied = applied - faces[index, 4] * blocks(above[part])
                applied = applied - faces[index, 5] * blocks(below[part])
                given = forcing[chunk, index, part]
                rest = given - applied.reshape(modes, length_y)
                work[chunk, index, part] = rest
                given_sum = given_sum + given * given
                rest_sum = rest_sum + rest * rest
            return (given_sum, rest_sum)

        given_sum, rest_sum = lax.fori_loop(0, depth, run, (none, none), unroll=4)
        squares[0] = squares[0] + given_sum
        squares[1] = squares[1] + rest_sum

    squares[0] = none
    squares[1] = none
    factors(0)

    def begin(chunk):
        for offset in range(1, RADIX):
            in_copy(chunk, offset).wait()
        work[chunk, pl.ds(0, depth)] = sine_rows(forcing[chunk])
        launch(0, chunk)

    def middle(chunk):
        solve(0, chunk)
        values = sine_rows(work[chunk]) * scale
        field[chunk, pl.ds(1, depth)] = values[:depth]
        field[chunk, 0] = values[depth]
        field[chunk, depth + 1] = values[depth + 1]
        residual(chunk)
        work[chunk, pl.ds(0, depth)] = sine_rows(work[chunk, pl.ds(0, depth)])
        launch(1, chunk)

        @pl.when(chunk == chunks - 1)
        def _():
            row = lax.broadcasted_iota(jnp.int32, (ITERS, 128), 0)
            both = jnp.where(row == 0, jnp.sum(squares[0]), jnp.sum(squares[1]))
            sum_own[...] = both / length_x

            @each_peer
            def _(offset):
                sum_copy(offset).start()

            pltpu.make_async_copy(sum_own, sums.at[me], own_sem.at[chunks]).start()

    def finish(chunk):
        solve(1, chunk)
        values = sine_rows(work[chunk, pl.ds(0, depth)]) * scale
        result[chunk] = field[chunk, pl.ds(1, depth)] + values
        for offset in (2, 3, 1):
            out_copy(chunk, offset).start()
        own_copy(chunk).start()

    def ready(chunk):
        @pl.when(chunk + 1 < chunks)
        def _():
            factors(chunk + 1)

    stages = {
        "begin": (0, begin),
        "ready": (0, ready),
        "relay": (LAGS[0], functools.partial(relay, 0)),
        "middle": (LAGS[1], middle),
        "again": (LAGS[2], functools.partial(relay, 1)),
        "finish": (LAGS[3], finish),
    }

    def step(index, carry):
        for name in ORDER:
            lag, act = stages[name]

            @pl.when((index >= lag) & (index < chunks + lag))
            def _():
                act(index - lag)

        return carry

    lax.fori_loop(0, chunks + LAGS[3], step, 0)

    def settle(chunk, carry):
        for turn_id in range(2):
            pair_copy(turn_id, chunk).wait_send()

            @pl.when(inner)
            def _():
                comb_copy(turn_id, chunk, 0).wait_send()
                comb_copy(turn_id, chunk, 1).wait_send()

        own_copy(chunk).wait()
        for offset in range(1, RADIX):
            out_copy(chunk, offset).wait()
        return carry

    pltpu.make_async_copy(sum_own, sums.at[me], own_sem.at[chunks]).wait()

    @each_peer
    def _(offset):
        sum_copy(offset).wait()

    lax.fori_loop(0, chunks, settle, 0)


def ending(cells, slabs, sums, bwd_hi, bwd_lo, out, norms, stage, out_sem):
    chunks, planes, _, modes, length_y = slabs.shape[1:]
    count = chunks * modes

    def store(plane, q):
        return pltpu.make_async_copy(
            stage.at[:, plane, pl.ds(q * count, count), :],
            out.at[:, plane, pl.ds(q * count, count), :],
            out_sem.at[plane, q],
        )

    for plane in range(planes):
        parts = []
        for residue in range(RADIX):
            blocks = [
                slabs[residue, chunk, plane, part] for part in range(2) for chunk in range(chunks)
            ]
            right = split(jnp.concatenate(blocks, axis=0))
            values = dot3((bwd_hi[residue], bwd_lo[residue]), right)
            parts.append((values[:count], values[count:]))
        for q in range(RADIX):
            re, im = combine(parts, [residue * q for residue in range(RADIX)])
            stage[0, plane, q * count : (q + 1) * count, :] = re
            stage[1, plane, q * count : (q + 1) * count, :] = im
            store(plane, q).start()
    root = jnp.sqrt(jnp.sum(sums[...], axis=0) / cells)
    for index in range(ITERS):
        norms[index] = root[index, 0]
    for plane in range(planes):
        for q in range(RADIX):
            store(plane, q).wait()


CHUNKS = 8
LAGS = (1, 2, 3, 5)
ORDER = ("begin", "relay", "finish", "middle", "ready", "again")


def body(source, layer_ids, conduct_table, shift):
    planes = source.shape[1]
    length_x = source.shape[2]
    length_y = source.shape[3]
    groups = lax.axis_size("gz")
    length_z = planes * groups
    count = length_x // RADIX
    modes = count // CHUNKS
    if groups != 4 * RADIX or modes % 8 or planes > 8 or length_z > 64 or length_y % 128:
        return body_plain(source, layer_ids, conduct_table, shift)
    depth = planes * RADIX
    layers = conduct_table.shape[0]
    mode_ids = RADIX * np.arange(count)[None, :] + np.arange(RADIX)[:, None]
    mode_eig = (2.0 - 2.0 * np.cos(2.0 * np.pi / length_x * mode_ids)).astype(np.float32)
    mode_eig = np.broadcast_to(mode_eig[:, :, None], (RADIX, count, 128))
    mode_eig = np.ascontiguousarray(mode_eig).reshape(RADIX, CHUNKS, modes, 128)
    eig_y = 4.0 - 2.0 * np.cos(np.pi / (length_y + 1) * (np.arange(length_y) + 1.0))
    eig_y = np.ascontiguousarray(np.broadcast_to(eig_y.astype(np.float32), (8, length_y)))
    forward, backward = radix_tables(length_x)
    tables = [*halves(forward), *halves(sine_host(length_y))]
    tile = (2, modes, length_y)
    smem = pl.BlockSpec(memory_space=pltpu.SMEM)
    hbm = pl.BlockSpec(memory_space=pl.ANY)
    f32 = jnp.float32
    dma = pltpu.SemaphoreType.DMA
    in_hbm = functools.partial(pltpu.with_memory_space_constraint, memory_space=pltpu.HBM)
    slabs, sums = pl.pallas_call(
        functools.partial(kernel, groups, planes, CHUNKS, layers),
        out_shape=(
            pltpu.VMEM((RADIX, CHUNKS, planes, *tile), f32),
            pltpu.VMEM((groups, ITERS, 128), f32),
        ),
        in_specs=[hbm] * 10,
        out_specs=(hbm, hbm),
        scratch_shapes=[
            pltpu.VMEM(source.shape, f32),
            pltpu.VMEM(layer_ids.shape, jnp.int32),
            pltpu.SMEM(conduct_table.shape, f32),
            pltpu.SMEM(shift.shape, f32),
            pltpu.VMEM((CHUNKS, modes, 128), f32),
            pltpu.VMEM((8, length_y), f32),
        ]
        + [pltpu.VMEM(table.shape, jnp.bfloat16) for table in tables]
        + [
            pltpu.VMEM((RADIX, CHUNKS, planes, *tile), f32),
            pltpu.VMEM((CHUNKS, depth, *tile), f32),
            pltpu.VMEM((planes, length_y), f32),
            pltpu.VMEM((groups, planes, length_y), f32),
            pltpu.VMEM((length_z + 2, 8, length_y), f32),
            pltpu.VMEM((depth, 6, 8, length_y), f32),
            pltpu.VMEM((CHUNKS, depth + 2, *tile), f32),
            pltpu.VMEM((CHUNKS, length_z + 1, *tile), f32),
            pltpu.VMEM((CHUNKS, groups // RADIX, *tile), f32),
            pltpu.VMEM((CHUNKS, depth + 2, *tile), f32),
            pltpu.VMEM((CHUNKS, depth, *tile), f32),
            pltpu.VMEM((ITERS, 128), f32),
            pltpu.VMEM(tile, f32),
        ]
        + [pltpu.VMEM((ITERS, CHUNKS, *tile), f32)] * 5
        + [dma((10,))]
        + [dma((CHUNKS, RADIX))] * 2
        + [dma((groups,))] * 2
        + [dma((CHUNKS, RADIX))] * 2
        + [dma((groups,))] * 2
        + [dma((CHUNKS + 1,))]
        + [dma((ITERS, CHUNKS))] * 2
        + [dma((ITERS, CHUNKS, 2)), dma((ITERS, CHUNKS))],
        compiler_params=pltpu.CompilerParams(
            collective_id=0, has_side_effects=True, vmem_limit_bytes=50 << 20
        ),
    )(
        in_hbm(source),
        in_hbm(layer_ids),
        in_hbm(conduct_table),
        in_hbm(shift),
        *[in_hbm(jnp.asarray(table)) for table in (mode_eig, eig_y, *tables)],
    )
    cells = length_x * length_y * length_z
    back = halves(backward)
    vmem = pl.BlockSpec(memory_space=pltpu.VMEM)
    return pl.pallas_call(
        functools.partial(ending, cells),
        out_shape=(
            jax.ShapeDtypeStruct(source.shape, f32),
            jax.ShapeDtypeStruct((ITERS,), f32),
        ),
        in_specs=[vmem] * 4,
        out_specs=(hbm, smem),
        scratch_shapes=[pltpu.VMEM(source.shape, f32), dma((planes, RADIX))],
        compiler_params=pltpu.CompilerParams(vmem_limit_bytes=20 << 20),
    )(slabs, sums, *back)


def solution(mesh):
    placed = (P(None, ("node", "gz"), None, None), P(("node", "gz"), None), P(), P("node"))
    return jax.shard_map(
        body,
        mesh=mesh,
        in_specs=placed,
        out_specs=(P(None, ("node", "gz"), None, None), P("node")),
        check_vma=False,
    )
```

```python
import functools

import jax
import jax.numpy as jnp
import numpy as np
from jax import lax
from jax.experimental import pallas as pl
from jax.experimental.pallas import tpu as pltpu
from jax.sharding import PartitionSpec as P

ITERS = 2


relax = 0.6
highest = lax.Precision.HIGH


def with_halo(cells, sides, width):
    for axis, dim in sides:
        count = lax.axis_size(axis)
        ends = count - 1
        head = lax.slice_in_dim(cells, 0, width, axis=dim)
        tail = lax.slice_in_dim(cells, cells.shape[dim] - width, cells.shape[dim], axis=dim)
        cells = jnp.concatenate(
            [
                lax.ppermute(tail, axis, [(i, (i + 1) % count) for i in range(ends)]),
                cells,
                lax.ppermute(head, axis, [((i + 1) % count, i) for i in range(ends)]),
            ],
            axis=dim,
        )
    return cells


def sine_table(length):
    indices = lax.iota(jnp.int32, length) + 1
    product = indices[:, None] * indices[None, :] % (2 * (length + 1))
    return jnp.sqrt(2.0 / (length + 1)) * jnp.sin(
        jnp.pi / (length + 1) * product.astype(jnp.float32)
    )


def sine_eigen(length):
    indices = lax.iota(jnp.float32, length) + 1.0
    return 2.0 - 2.0 * jnp.cos(jnp.pi / (length + 1) * indices)


def dft_tables(length):
    indices = lax.iota(jnp.int32, length)
    product = indices[:, None] * indices[None, :] % length
    angles = 2.0 * jnp.pi / length * product.astype(jnp.float32)
    return (jnp.cos(angles), jnp.sin(angles))


def transform(field, cos_t, sin_t, inverse):

    def project(component, matrix):
        return jnp.einsum("zxy,xk->zky", component, matrix, precision=highest)

    re_cos = project(field[0], cos_t)
    re_sin = project(field[0], sin_t)
    im_cos = project(field[1], cos_t)
    im_sin = project(field[1], sin_t)
    if inverse:
        return jnp.stack([re_cos - im_sin, im_cos + re_sin]) / cos_t.shape[0]
    return jnp.stack([re_cos + im_sin, im_cos - re_sin])


def expand(weights):
    return weights[None, :, None, :]


def yz_part(field, upper, lower, conduct, cond_hi, cond_lo):
    cond_pad = jnp.pad(conduct, ((0, 0), (1, 1)), mode="edge")
    face_yp = 0.5 * (conduct + cond_pad[:, 2:])
    face_ym = 0.5 * (conduct + cond_pad[:, :-2])
    face_zp = 0.5 * (conduct + cond_hi)
    face_zm = 0.5 * (conduct + cond_lo)
    field_pad = jnp.pad(field, ((0, 0), (0, 0), (0, 0), (1, 1)))
    total = expand(face_yp) * (field - field_pad[..., 2:]) + expand(face_ym) * (
        field - field_pad[..., :-2]
    )
    return total + expand(face_zp) * (field - upper) + expand(face_zm) * (field - lower)


def shift_mult(shift_re, shift_im, field):
    return jnp.stack(
        [shift_re * field[0] - shift_im * field[1], shift_re * field[1] + shift_im * field[0]]
    )


def sine_both(field, sine_y, sine_z):
    field = jnp.einsum("pzxy,yj->pzxj", field, sine_y, precision=highest)
    return jnp.einsum("pzxy,zk->pkxy", field, sine_z, precision=highest)


def precondition(coeffs, mode_eig, mean_cond, shift_re, shift_im, sine_y, sine_z, eig_y, eig_z):
    coeffs = sine_both(coeffs, sine_y, sine_z)
    eigen = eig_z[:, None, None] + mode_eig[None, :, None] + eig_y[None, None, :]
    real_den = shift_re + mean_cond * eigen
    inv = 1.0 / (real_den * real_den + shift_im * shift_im)
    scaled = jnp.stack(
        [
            (coeffs[0] * real_den + coeffs[1] * shift_im) * inv,
            (coeffs[1] * real_den - coeffs[0] * shift_im) * inv,
        ]
    )
    return sine_both(scaled, sine_y, sine_z)


def body_plain(source, layer_ids, conduct_table, shift):
    shift_re = shift[0]
    shift_im = shift[1]
    planes = source.shape[1]
    length_x = source.shape[2]
    length_y = source.shape[3]
    groups = lax.axis_size("gz")
    length_z = planes * groups
    modes = length_x // groups
    first_mode = lax.axis_index("gz") * modes
    layers = conduct_table.shape[0]
    onehot = layer_ids[:, :, None] == lax.iota(jnp.int32, layers)[None, None, :]
    local = jnp.sum(jnp.where(onehot, conduct_table[None, None, :], 0.0), axis=-1)
    conduct = lax.all_gather(local, "gz", axis=0, tiled=True)
    mean_cond = jnp.sum(conduct) / (length_y * length_z)
    cond_z = jnp.pad(conduct, ((1, 1), (0, 0)), mode="edge")
    cos_t, sin_t = dft_tables(length_x)
    sine_y = sine_table(length_y)
    sine_z = sine_table(length_z)
    eig_y = sine_eigen(length_y)
    eig_z = sine_eigen(length_z)
    mode_ids = (first_mode + lax.iota(jnp.int32, modes)).astype(jnp.float32)
    mode_eig = 2.0 - 2.0 * jnp.cos(2.0 * jnp.pi / length_x * mode_ids)
    cells = length_x * length_y * length_z
    spectra = transform(source, cos_t, sin_t, False)
    forcing = lax.all_to_all(spectra, "gz", split_axis=2, concat_axis=1, tiled=True)
    partials = []
    solution = jnp.zeros_like(forcing)
    for iteration in range(ITERS):
        if iteration == 0:
            resid = forcing
        else:
            padded = jnp.pad(solution, ((0, 0), (1, 1), (0, 0), (0, 0)))
            lap = expand(conduct) * mode_eig[None, None, :, None] * solution
            lap = lap + yz_part(
                solution, padded[:, 2:], padded[:, :-2], conduct, cond_z[2:], cond_z[:-2]
            )
            resid = forcing - (shift_mult(shift_re, shift_im, solution) + lap)
        partials.append(jnp.sum(resid * resid) / length_x)
        update = precondition(
            resid, mode_eig, mean_cond, shift_re, shift_im, sine_y, sine_z, eig_y, eig_z
        )
        solution = solution + relax * update
    slabs = lax.all_to_all(solution, "gz", split_axis=1, concat_axis=2, tiled=True)
    result = transform(slabs, cos_t, sin_t, True)
    sums = jnp.sum(lax.all_gather(jnp.stack(partials)[None, :], "gz", axis=0, tiled=True), axis=0)
    return (result, jnp.sqrt(sums / cells))


RADIX = 4


def halves(table):
    high = table.astype(jnp.bfloat16)
    low = (table - high.astype(np.float32)).astype(jnp.bfloat16)
    return (jnp.asarray(high), jnp.asarray(low))


def radix_tables(length_x):
    count = length_x // RADIX
    pos = np.arange(count)
    forward = []
    for residue in range(RADIX):
        modes = RADIX * pos + residue
        angle = 2.0 * np.pi / length_x * (modes[:, None] * pos[None, :] % length_x)
        cos_t, sin_t = np.cos(angle), np.sin(angle)
        forward.append(np.block([[cos_t, sin_t], [-sin_t, cos_t]]))
    forward = np.stack(forward)
    backward = np.swapaxes(forward, 1, 2) / length_x
    return (forward.astype(np.float32), backward.astype(np.float32))


def sine_host(length):
    indices = np.arange(length) + 1
    product = indices[:, None] * indices[None, :] % (2 * (length + 1))
    return (np.sqrt(2.0 / (length + 1)) * np.sin(np.pi / (length + 1) * product)).astype(np.float32)


def split(values):
    high = values.astype(jnp.bfloat16)
    return (high, (values - high.astype(jnp.float32)).astype(jnp.bfloat16))


def dot3(left, right):
    mul = functools.partial(jnp.dot, preferred_element_type=jnp.float32)
    return mul(left[0], right[0]) + (mul(left[0], right[1]) + mul(left[1], right[0]))


def dot_wide(left, right):
    wide = jnp.concatenate([left[0], left[1], left[0]], axis=1)
    return jnp.dot(wide, right, preferred_element_type=jnp.float32)


def turn(re, im, quarter):
    quarter = quarter % 4
    return [(re, im), (-im, re), (-re, -im), (im, -re)][quarter]


def combine(parts, quarters):
    re, im = turn(*parts[0], quarters[0])
    for part, quarter in zip(parts[1:], quarters[1:]):
        more_re, more_im = turn(*part, quarter)
        re, im = re + more_re, im + more_im
    return (re, im)


def times(left, right):
    return (left[0] * right[0] - left[1] * right[1], left[0] * right[1] + left[1] * right[0])


def plus(left, right):
    return (left[0] + right[0], left[1] + right[1])


def pair(ref, *index):
    return (ref[(*index, 0)], ref[(*index, 1)])


def put(ref, values, *index):
    ref[(*index, 0)] = values[0]
    ref[(*index, 1)] = values[1]


def choose(test, left, right):
    return (jnp.where(test, left[0], right[0]), jnp.where(test, left[1], right[1]))


def kernel(
    groups,
    planes,
    chunks,
    layers,
    source_hbm,
    ids_hbm,
    table_hbm,
    shift_hbm,
    mode_hbm,
    eig_hbm,
    fwd_hi_hbm,
    fwd_lo_hbm,
    sine_hi_hbm,
    sine_lo_hbm,
    slabs,
    sums,
    source,
    ids,
    table,
    shift,
    mode_eig,
    eig_y,
    fwd_hi,
    fwd_lo,
    sine_hi,
    sine_lo,
    spectra,
    forcing,
    cond_own,
    cond_team,
    cond,
    edge_out,
    edge_in,
    half_out,
    half_in,
    faces,
    work,
    alpha,
    lines,
    field,
    result,
    sum_own,
    squares,
    pair_out,
    pair_in,
    rest_out,
    comb_out,
    comb_in,
    load_sem,
    in_send,
    in_recv,
    cond_send,
    cond_recv,
    edge_send,
    edge_recv,
    half_send,
    half_recv,
    out_send,
    out_recv,
    sum_send,
    sum_recv,
    own_sem,
    pair_send,
    pair_recv,
    comb_send,
    comb_recv,
):
    me = lax.axis_index("gz")
    side = lax.rem(me, RADIX)
    team = me // RADIX
    teams = groups // RADIX
    length_x = source.shape[2]
    length_y = source.shape[3]
    length_z = groups * planes
    depth = RADIX * planes
    count = length_x // RADIX
    modes = count // chunks
    first_level = team * depth
    last_level = length_z - first_level - depth

    pieces = [(ids_hbm, ids), (table_hbm, table), (shift_hbm, shift)]
    pieces += [(source_hbm.at[:, 0], source.at[:, 0])]
    for residue in range(RADIX):
        pieces += [(fwd_hi_hbm.at[residue], fwd_hi.at[residue])]
        pieces += [(fwd_lo_hbm.at[residue], fwd_lo.at[residue])]
    pieces += [(source_hbm.at[:, plane], source.at[:, plane]) for plane in range(1, planes)]
    pieces += [(sine_hi_hbm, sine_hi), (sine_lo_hbm, sine_lo)]
    pieces += [(mode_hbm.at[side], mode_eig), (eig_hbm, eig_y)]
    loads = [
        pltpu.make_async_copy(src, dst, load_sem.at[index])
        for index, (src, dst) in enumerate(pieces)
    ]
    for load in loads:
        load.start()

    def remote(src, dst, send, recv, target):
        return pltpu.make_async_remote_copy(
            src_ref=src,
            dst_ref=dst,
            send_sem=send,
            recv_sem=recv,
            device_id={"gz": target},
            device_id_type=pl.DeviceIdType.MESH,
        )

    def peer(offset):
        return lax.rem(me + offset, groups)

    def mate(offset):
        return lax.rem(side + offset, RADIX)

    def rows(index):
        return pl.ds(index * planes, planes)

    def cond_copy(offset):
        return remote(
            cond_own,
            cond_team.at[side],
            cond_send.at[offset],
            cond_recv.at[offset],
            team * RADIX + mate(offset),
        )

    def edge_copy(which):
        return remote(
            edge_out,
            edge_in.at[which],
            edge_send.at[which],
            edge_recv.at[which],
            me + [RADIX, -RADIX][which],
        )

    def half_copy(which):
        target = [teams - 1 - team, (teams - 1) * (2 - team)][which]
        return remote(
            half_out, half_in, half_send.at[which], half_recv.at[0], target * RADIX + side
        )

    def sum_copy(offset):
        return remote(
            sum_own, sums.at[me], sum_send.at[offset], sum_recv.at[offset], peer(offset)
        )

    def in_piece(chunk, offset, plane):
        target = mate(offset)
        return remote(
            spectra.at[target, chunk, pl.ds(plane, 1)],
            forcing.at[chunk, pl.ds(side * planes + plane, 1)],
            in_send.at[chunk, offset],
            in_recv.at[chunk, offset],
            team * RADIX + target,
        )

    def in_copy(chunk, offset):
        target = mate(offset)
        return remote(
            spectra.at[target, chunk],
            forcing.at[chunk, rows(side)],
            in_send.at[chunk, offset],
            in_recv.at[chunk, offset],
            team * RADIX + target,
        )

    def out_copy(chunk, offset):
        target = mate(offset)
        return remote(
            result.at[chunk, rows(target)],
            slabs.at[side, chunk],
            out_send.at[chunk, offset],
            out_recv.at[chunk, offset],
            team * RADIX + target,
        )

    def own_copy(chunk):
        return pltpu.make_async_copy(
            result.at[chunk, rows(side)], slabs.at[side, chunk], own_sem.at[chunk]
        )

    even = lax.rem(team, 2) == 0
    inner = (team == 1) | (team == 2)
    lower = team < 2
    partner = team + 1 - 2 * lax.rem(team, 2)

    def pair_copy(turn_id, chunk):
        return remote(
            pair_out.at[turn_id, chunk],
            pair_in.at[turn_id, chunk],
            pair_send.at[turn_id, chunk],
            pair_recv.at[turn_id, chunk],
            partner * RADIX + side,
        )

    def comb_copy(turn_id, chunk, which):
        target = [teams - 1 - team, (teams - 1) * (2 - team)][which]
        return remote(
            comb_out.at[turn_id, chunk],
            comb_in.at[turn_id, chunk],
            comb_send.at[turn_id, chunk, which],
            comb_recv.at[turn_id, chunk],
            target * RADIX + side,
        )

    def each_peer(act):
        def run(offset, carry):
            act(offset)
            return carry

        lax.fori_loop(1, groups, run, 0)

    barrier = pltpu.get_barrier_semaphore()

    def greet(target):
        pl.semaphore_signal(
            barrier, inc=1, device_id={"gz": target}, device_id_type=pl.DeviceIdType.MESH
        )

    for offset in range(1, RADIX):
        greet(team * RADIX + mate(offset))

    @pl.when(team > 0)
    def _():
        greet(me - RADIX)

    @pl.when(team < teams - 1)
    def _():
        greet(me + RADIX)

    for load in loads[:3]:
        load.wait()
    found = jnp.zeros((planes, length_y), jnp.float32)
    for layer in range(layers):
        found = found + jnp.where(ids[...] == layer, table[layer], 0.0)
    cond_own[...] = found
    cond_team[side] = found

    def forward(plane):
        loads[3 if plane == 0 else 3 + 2 * RADIX + plane].wait()
        parts = [
            (
                source[0, plane, q * count : (q + 1) * count, :],
                source[1, plane, q * count : (q + 1) * count, :],
            )
            for q in range(RADIX)
        ]
        for residue in range(RADIX):
            if plane == 0:
                loads[4 + 2 * residue].wait()
                loads[5 + 2 * residue].wait()
            mixed = combine(parts, [-residue * q for q in range(RADIX)])
            right = split(jnp.concatenate(mixed, axis=0))
            values = dot3((fwd_hi[residue], fwd_lo[residue]), right)
            for chunk in range(chunks):
                for part in range(2):
                    start = part * count + chunk * modes
                    spectra[residue, chunk, plane, part] = values[start : start + modes]

    forward(0)
    pl.semaphore_wait(barrier, RADIX - 1 + jnp.where(team > 0, 1, 0) + jnp.where(team < teams - 1, 1, 0))
    for offset in range(1, RADIX):
        cond_copy(offset).start()
    for offset in (2, 3, 1):
        in_piece(0, offset, 0).start()
    for plane in range(1, planes):
        forward(plane)
        for offset in (2, 3, 1):
            in_piece(0, offset, plane).start()

    for load in loads[3 + 2 * RADIX + planes :]:
        load.wait()
    sine = jnp.concatenate([sine_hi[...], sine_hi[...], sine_lo[...]], axis=0)

    def sine_rows(values):
        flat = values.reshape(-1, length_y)
        return dot_wide(split(flat), sine).reshape(values.shape)

    def send_in(chunk, carry):
        spectra[:, chunk] = sine_rows(spectra[:, chunk])
        for offset in (2, 3, 1):
            in_copy(chunk, offset).start()
        return carry

    lax.fori_loop(1, 2, send_in, 0)
    for offset in range(1, RADIX):
        cond_copy(offset).wait()
    total = jnp.zeros((1, length_y), jnp.float32)
    for index in range(RADIX):
        for plane in range(planes):
            row = cond_team[index, plane : plane + 1, :]
            cond[index * planes + plane + 1] = jnp.broadcast_to(row, (8, length_y))
            total = total + row
    edge_out[0:1] = total
    edge_out[1:2] = cond_team[0, 0:1, :]
    edge_out[2:3] = cond_team[RADIX - 1, planes - 1 : planes, :]

    @pl.when(team < teams - 1)
    def _():
        edge_copy(0).start()

    @pl.when(team > 0)
    def _():
        edge_copy(1).start()

    lax.fori_loop(2, chunks - 3, send_in, 0)


    @pl.when(team > 0)
    def _():
        edge_copy(0).wait_recv()
        cond[0] = jnp.broadcast_to(edge_in[0, 2:3, :], (8, length_y))

    @pl.when(team == 0)
    def _():
        cond[0] = cond[1]

    @pl.when(team < teams - 1)
    def _():
        edge_copy(1).wait_recv()
        cond[depth + 1] = jnp.broadcast_to(edge_in[1, 1:2, :], (8, length_y))

    @pl.when(team == teams - 1)
    def _():
        cond[depth + 1] = cond[depth]

    @pl.when(even)
    def _():
        half_out[0:1] = total + edge_in[1, 0:1, :]

    @pl.when(jnp.logical_not(even))
    def _():
        half_out[0:1] = total + edge_in[0, 0:1, :]

    @pl.when(inner)
    def _():
        half_copy(1).start()
        half_copy(0).start()

    shift_re = shift[0]
    shift_im = shift[1]
    row_lane = lax.broadcasted_iota(jnp.int32, (8, length_y), 1)
    last = length_y - 1

    lax.fori_loop(chunks - 3, chunks, send_in, 0)

    def keep(chunk, carry):
        forcing[chunk, rows(side)] = spectra[side, chunk]
        return carry

    lax.fori_loop(0, chunks, keep, 0)

    def make_faces(index, carry):
        here = cond[index + 1]
        right = jnp.where(row_lane == last, here, pltpu.roll(here, last, 1))
        left = jnp.where(row_lane == 0, here, pltpu.roll(here, 1, 1))
        face_yp = 0.5 * (here + right)
        face_ym = 0.5 * (here + left)
        face_zp = 0.5 * (here + cond[index + 2])
        face_zm = 0.5 * (here + cond[index])
        faces[index, 0] = here
        faces[index, 1] = face_yp + face_ym + face_zp + face_zm + shift_re
        faces[index, 2] = jnp.where(row_lane == last, 0.0, face_yp)
        faces[index, 3] = jnp.where(row_lane == 0, 0.0, face_ym)
        faces[index, 4] = face_zp
        faces[index, 5] = face_zm
        return carry

    lax.fori_loop(0, depth, make_faces, 0)
    def take(chunk):
        for offset in range(1, RADIX):
            in_copy(chunk, offset).wait()

    take(0)
    forcing[0] = sine_rows(forcing[0])
    half_copy(0).wait_recv()
    total = half_out[0:1, :] + half_in[0:1, :]
    mean_cond = jnp.sum(total) / (length_y * length_z)
    scale = relax / mean_cond
    offset_re = shift_re / mean_cond
    diag_im = shift_im / mean_cond
    none = jnp.zeros((modes, length_y), jnp.float32)
    one = jnp.ones((modes, length_y), jnp.float32)

    def eigen(chunk):
        return jnp.concatenate([mode_eig[chunk]] * (length_y // 128), axis=1)

    def factors(chunk):
        diag_re = eigen(chunk) + (eig_y[0:1, :] + offset_re)

        def factor(level, carry):
            gap_re = diag_re - carry[0]
            gap_im = diag_im - carry[1]
            inverse = 1.0 / (gap_re * gap_re + gap_im * gap_im)
            now = (gap_re * inverse, -gap_im * inverse)
            put(alpha, now, chunk, level)
            return now

        def segment(index, carry):
            def inner_level(level, state):
                now = factor(index * depth + level + 1, state[:2])
                return (*now, *times(now, state[2:]))

            state = lax.fori_loop(0, depth, inner_level, (*carry, one, none), unroll=True)
            put(lines, state[2:], chunk, index)
            return state[:2]

        put(alpha, (none, none), chunk, 0)
        lax.fori_loop(0, teams, segment, (none, none))

    given = (forcing, work)

    def launch(turn_id, chunk):
        def rise(index, carry):
            up = times(
                pair(alpha, chunk, first_level + index + 1),
                plus(pair(given[turn_id], chunk, index), carry[:2]),
            )
            down = times(
                pair(alpha, chunk, last_level + index + 1),
                plus(pair(given[turn_id], chunk, depth - 1 - index), carry[2:]),
            )
            return (*up, *down)

        ends = lax.fori_loop(0, depth, rise, (none, none, none, none), unroll=True)
        put(pair_out, choose(even, ends[:2], ends[2:]), turn_id, chunk)
        pair_copy(turn_id, chunk).start()
        put(rest_out, choose(even, ends[2:], ends[:2]), turn_id, chunk)

    def relay(turn_id, chunk):
        pair_copy(turn_id, chunk).wait_recv()

        @pl.when(inner)
        def _():
            more = times(pair(lines, chunk, 1), pair(pair_in, turn_id, chunk))
            put(comb_out, plus(pair(rest_out, turn_id, chunk), more), turn_id, chunk)
            comb_copy(turn_id, chunk, 1).start()
            comb_copy(turn_id, chunk, 0).start()

    def solve(turn_id, chunk):
        comb_copy(turn_id, chunk, 0).wait_recv()
        near = pair(pair_in, turn_id, chunk)
        wide = pair(comb_in, turn_id, chunk)
        joined = plus(near, times(pair(lines, chunk, teams - 2), wide))
        far = choose(inner, wide, joined)
        near = choose(inner, near, (none, none))
        below = choose(lower, near, far)
        above = choose(lower, far, near)

        def ahead(index, carry):
            factor = pair(alpha, chunk, first_level + index + 1)
            now = times(factor, plus(pair(given[turn_id], chunk, index), carry))
            put(work, now, chunk, index)
            return now

        reached = lax.fori_loop(0, depth, ahead, below, unroll=True)
        factor = pair(alpha, chunk, first_level + depth)
        edge = pair(alpha, chunk, last_level)
        echo = times(factor, edge)
        gap_re = 1.0 - echo[0]
        inverse = 1.0 / (gap_re * gap_re + echo[1] * echo[1])
        top = plus(reached, times(factor, above))
        top = times(top, (gap_re * inverse, echo[1] * inverse))
        outer = plus(above, times(edge, top))
        put(work, outer, chunk, depth + 1)

        def behind(step, carry):
            index = depth - 1 - step
            factor = pair(alpha, chunk, first_level + index + 1)
            now = plus(pair(work, chunk, index), times(factor, carry))
            put(work, now, chunk, index)
            return now

        bottom = lax.fori_loop(0, depth, behind, outer, unroll=True)
        put(work, plus(below, times(pair(alpha, chunk, first_level), bottom)), chunk, depth)

    def blocks(values):
        return values.reshape(modes // 8, 8, length_y)

    def operator(chunk):
        eig = blocks(eigen(chunk))

        def run(index, carry):
            center = faces[index, 0] * eig + faces[index, 1]
            values = pair(field, chunk, index + 1)
            turned = (-shift_im * values[1], shift_im * values[0])
            above = pair(field, chunk, index + 2)
            below = pair(field, chunk, index)
            for part in range(2):
                value = values[part]
                applied = center * blocks(value) + blocks(turned[part])
                applied = applied - faces[index, 2] * blocks(pltpu.roll(value, last, 1))
                applied = applied - faces[index, 3] * blocks(pltpu.roll(value, 1, 1))
                applied = applied - faces[index, 4] * blocks(above[part])
                applied = applied - faces[index, 5] * blocks(below[part])
                work[chunk, index, part] = applied.reshape(modes, length_y)
            return carry

        lax.fori_loop(0, depth, run, 0, unroll=8)

    squares[0] = none
    squares[1] = none
    factors(0)

    def begin(chunk):
        @pl.when(chunk > 0)
        def _():
            take(chunk)

        launch(0, chunk)

    def middle(chunk):
        solve(0, chunk)
        values = sine_rows(work[chunk]) * scale
        field[chunk, pl.ds(1, depth)] = values[:depth]
        field[chunk, 0] = values[depth]
        field[chunk, depth + 1] = values[depth + 1]
        operator(chunk)
        here = forcing[chunk]
        rest = here - sine_rows(work[chunk, pl.ds(0, depth)])
        work[chunk, pl.ds(0, depth)] = rest
        launch(1, chunk)
        squares[0] = squares[0] + jnp.sum(here * here, axis=(0, 1))
        squares[1] = squares[1] + jnp.sum(rest * rest, axis=(0, 1))

        @pl.when(chunk == chunks - 1)
        def _():
            row = lax.broadcasted_iota(jnp.int32, (ITERS, 128), 0)
            both = jnp.where(row == 0, jnp.sum(squares[0]), jnp.sum(squares[1]))
            sum_own[...] = both / length_x

            @each_peer
            def _(offset):
                sum_copy(offset).start()

            pltpu.make_async_copy(sum_own, sums.at[me], own_sem.at[chunks]).start()

    def finish(chunk):
        solve(1, chunk)
        values = sine_rows(work[chunk, pl.ds(0, depth)]) * scale
        result[chunk] = field[chunk, pl.ds(1, depth)] + values
        for offset in (2, 3, 1):
            out_copy(chunk, offset).start()
        own_copy(chunk).start()

    def ready(chunk):
        @pl.when(chunk + 1 < chunks)
        def _():
            factors(chunk + 1)

    stages = {
        "begin": (0, begin),
        "ready": (0, ready),
        "relay": (LAGS[0], functools.partial(relay, 0)),
        "middle": (LAGS[1], middle),
        "again": (LAGS[2], functools.partial(relay, 1)),
        "finish": (LAGS[3], finish),
    }

    def step(index, carry):
        for name in ORDER:
            lag, act = stages[name]

            @pl.when((index >= lag) & (index < chunks + lag))
            def _():
                act(index - lag)

        return carry

    lax.fori_loop(0, chunks + LAGS[3], step, 0)

    def settle(chunk, carry):
        for turn_id in range(2):
            pair_copy(turn_id, chunk).wait_send()

            @pl.when(inner)
            def _():
                comb_copy(turn_id, chunk, 0).wait_send()
                comb_copy(turn_id, chunk, 1).wait_send()

        own_copy(chunk).wait()
        for offset in range(1, RADIX):
            out_copy(chunk, offset).wait()
        return carry

    pltpu.make_async_copy(sum_own, sums.at[me], own_sem.at[chunks]).wait()

    @pl.when(team < teams - 1)
    def _():
        edge_copy(0).wait_send()

    @pl.when(team > 0)
    def _():
        edge_copy(1).wait_send()

    @pl.when(inner)
    def _():
        half_copy(0).wait_send()
        half_copy(1).wait_send()

    @each_peer
    def _(offset):
        sum_copy(offset).wait()

    lax.fori_loop(0, chunks, settle, 0)


def ending(cells, slabs, sums, bwd_hi, bwd_lo, out, norms, stage, out_sem):
    chunks, planes, _, modes, length_y = slabs.shape[1:]
    count = chunks * modes

    def store(plane, q):
        return pltpu.make_async_copy(
            stage.at[:, plane, pl.ds(q * count, count), :],
            out.at[:, plane, pl.ds(q * count, count), :],
            out_sem.at[plane, q],
        )

    for plane in range(planes):
        parts = []
        for residue in range(RADIX):
            blocks = [
                slabs[residue, chunk, plane, part] for part in range(2) for chunk in range(chunks)
            ]
            right = split(jnp.concatenate(blocks, axis=0))
            values = dot3((bwd_hi[residue], bwd_lo[residue]), right)
            parts.append((values[:count], values[count:]))
        for q in range(RADIX):
            re, im = combine(parts, [residue * q for residue in range(RADIX)])
            stage[0, plane, q * count : (q + 1) * count, :] = re
            stage[1, plane, q * count : (q + 1) * count, :] = im
            store(plane, q).start()
    root = jnp.sqrt(jnp.sum(sums[...], axis=0) / cells)
    for index in range(ITERS):
        norms[index] = root[index, 0]
    for plane in range(planes):
        for q in range(RADIX):
            store(plane, q).wait()


CHUNKS = 8
LAGS = (1, 2, 3, 5)
ORDER = ("begin", "relay", "finish", "middle", "ready", "again")


def body(source, layer_ids, conduct_table, shift):
    planes = source.shape[1]
    length_x = source.shape[2]
    length_y = source.shape[3]
    groups = lax.axis_size("gz")
    length_z = planes * groups
    count = length_x // RADIX
    modes = count // CHUNKS
    if groups != 4 * RADIX or modes % 8 or planes > 8 or length_z > 64 or length_y % 128:
        return body_plain(source, layer_ids, conduct_table, shift)
    depth = planes * RADIX
    layers = conduct_table.shape[0]
    mode_ids = RADIX * np.arange(count)[None, :] + np.arange(RADIX)[:, None]
    mode_eig = (2.0 - 2.0 * np.cos(2.0 * np.pi / length_x * mode_ids)).astype(np.float32)
    mode_eig = np.broadcast_to(mode_eig[:, :, None], (RADIX, count, 128))
    mode_eig = np.ascontiguousarray(mode_eig).reshape(RADIX, CHUNKS, modes, 128)
    eig_y = 4.0 - 2.0 * np.cos(np.pi / (length_y + 1) * (np.arange(length_y) + 1.0))
    eig_y = np.ascontiguousarray(np.broadcast_to(eig_y.astype(np.float32), (8, length_y)))
    forward, backward = radix_tables(length_x)
    tables = [*halves(forward), *halves(sine_host(length_y))]
    tile = (2, modes, length_y)
    smem = pl.BlockSpec(memory_space=pltpu.SMEM)
    hbm = pl.BlockSpec(memory_space=pl.ANY)
    f32 = jnp.float32
    dma = pltpu.SemaphoreType.DMA
    in_hbm = functools.partial(pltpu.with_memory_space_constraint, memory_space=pltpu.HBM)
    slabs, sums = pl.pallas_call(
        functools.partial(kernel, groups, planes, CHUNKS, layers),
        out_shape=(
            pltpu.VMEM((RADIX, CHUNKS, planes, *tile), f32),
            pltpu.VMEM((groups, ITERS, 128), f32),
        ),
        in_specs=[hbm] * 10,
        out_specs=(hbm, hbm),
        scratch_shapes=[
            pltpu.VMEM(source.shape, f32),
            pltpu.VMEM(layer_ids.shape, jnp.int32),
            pltpu.SMEM(conduct_table.shape, f32),
            pltpu.SMEM(shift.shape, f32),
            pltpu.VMEM((CHUNKS, modes, 128), f32),
            pltpu.VMEM((8, length_y), f32),
        ]
        + [pltpu.VMEM(table.shape, jnp.bfloat16) for table in tables]
        + [
            pltpu.VMEM((RADIX, CHUNKS, planes, *tile), f32),
            pltpu.VMEM((CHUNKS, depth, *tile), f32),
            pltpu.VMEM((planes, length_y), f32),
            pltpu.VMEM((RADIX, planes, length_y), f32),
            pltpu.VMEM((depth + 2, 8, length_y), f32),
            pltpu.VMEM((4, length_y), f32),
            pltpu.VMEM((2, 4, length_y), f32),
            pltpu.VMEM((4, length_y), f32),
            pltpu.VMEM((4, length_y), f32),
            pltpu.VMEM((depth, 6, 8, length_y), f32),
            pltpu.VMEM((CHUNKS, depth + 2, *tile), f32),
            pltpu.VMEM((CHUNKS, length_z + 1, *tile), f32),
            pltpu.VMEM((CHUNKS, groups // RADIX, *tile), f32),
            pltpu.VMEM((CHUNKS, depth + 2, *tile), f32),
            pltpu.VMEM((CHUNKS, depth, *tile), f32),
            pltpu.VMEM((ITERS, 128), f32),
            pltpu.VMEM(tile, f32),
        ]
        + [pltpu.VMEM((ITERS, CHUNKS, *tile), f32)] * 5
        + [dma((7 + 2 * RADIX + planes,))]
        + [dma((CHUNKS, RADIX))] * 2
        + [dma((RADIX,))] * 2
        + [dma((2,))] * 2
        + [dma((2,)), dma((1,))]
        + [dma((CHUNKS, RADIX))] * 2
        + [dma((groups,))] * 2
        + [dma((CHUNKS + 1,))]
        + [dma((ITERS, CHUNKS))] * 2
        + [dma((ITERS, CHUNKS, 2)), dma((ITERS, CHUNKS))],
        compiler_params=pltpu.CompilerParams(
            collective_id=0, has_side_effects=True, vmem_limit_bytes=50 << 20
        ),
    )(
        in_hbm(source),
        in_hbm(layer_ids),
        in_hbm(conduct_table),
        in_hbm(shift),
        *[in_hbm(jnp.asarray(table)) for table in (mode_eig, eig_y, *tables)],
    )
    cells = length_x * length_y * length_z
    back = halves(backward)
    vmem = pl.BlockSpec(memory_space=pltpu.VMEM)
    return pl.pallas_call(
        functools.partial(ending, cells),
        out_shape=(
            jax.ShapeDtypeStruct(source.shape, f32),
            jax.ShapeDtypeStruct((ITERS,), f32),
        ),
        in_specs=[vmem] * 4,
        out_specs=(hbm, smem),
        scratch_shapes=[pltpu.VMEM(source.shape, f32), dma((planes, RADIX))],
        compiler_params=pltpu.CompilerParams(vmem_limit_bytes=20 << 20),
    )(slabs, sums, *back)


def solution(mesh):
    placed = (P(None, ("node", "gz"), None, None), P(("node", "gz"), None), P(), P("node"))
    return jax.shard_map(
        body,
        mesh=mesh,
        in_specs=placed,
        out_specs=(P(None, ("node", "gz"), None, None), P("node")),
        check_vma=False,
    )
```

```python
import functools

import jax
import jax.numpy as jnp
import numpy as np
from jax import lax
from jax.experimental import pallas as pl
from jax.experimental.pallas import tpu as pltpu
from jax.sharding import PartitionSpec as P

ITERS = 2


relax = 0.6
highest = lax.Precision.HIGH


def with_halo(cells, sides, width):
    for axis, dim in sides:
        count = lax.axis_size(axis)
        ends = count - 1
        head = lax.slice_in_dim(cells, 0, width, axis=dim)
        tail = lax.slice_in_dim(cells, cells.shape[dim] - width, cells.shape[dim], axis=dim)
        cells = jnp.concatenate(
            [
                lax.ppermute(tail, axis, [(i, (i + 1) % count) for i in range(ends)]),
                cells,
                lax.ppermute(head, axis, [((i + 1) % count, i) for i in range(ends)]),
            ],
            axis=dim,
        )
    return cells


def sine_table(length):
    indices = lax.iota(jnp.int32, length) + 1
    product = indices[:, None] * indices[None, :] % (2 * (length + 1))
    return jnp.sqrt(2.0 / (length + 1)) * jnp.sin(
        jnp.pi / (length + 1) * product.astype(jnp.float32)
    )


def sine_eigen(length):
    indices = lax.iota(jnp.float32, length) + 1.0
    return 2.0 - 2.0 * jnp.cos(jnp.pi / (length + 1) * indices)


def dft_tables(length):
    indices = lax.iota(jnp.int32, length)
    product = indices[:, None] * indices[None, :] % length
    angles = 2.0 * jnp.pi / length * product.astype(jnp.float32)
    return (jnp.cos(angles), jnp.sin(angles))


def transform(field, cos_t, sin_t, inverse):

    def project(component, matrix):
        return jnp.einsum("zxy,xk->zky", component, matrix, precision=highest)

    re_cos = project(field[0], cos_t)
    re_sin = project(field[0], sin_t)
    im_cos = project(field[1], cos_t)
    im_sin = project(field[1], sin_t)
    if inverse:
        return jnp.stack([re_cos - im_sin, im_cos + re_sin]) / cos_t.shape[0]
    return jnp.stack([re_cos + im_sin, im_cos - re_sin])


def expand(weights):
    return weights[None, :, None, :]


def yz_part(field, upper, lower, conduct, cond_hi, cond_lo):
    cond_pad = jnp.pad(conduct, ((0, 0), (1, 1)), mode="edge")
    face_yp = 0.5 * (conduct + cond_pad[:, 2:])
    face_ym = 0.5 * (conduct + cond_pad[:, :-2])
    face_zp = 0.5 * (conduct + cond_hi)
    face_zm = 0.5 * (conduct + cond_lo)
    field_pad = jnp.pad(field, ((0, 0), (0, 0), (0, 0), (1, 1)))
    total = expand(face_yp) * (field - field_pad[..., 2:]) + expand(face_ym) * (
        field - field_pad[..., :-2]
    )
    return total + expand(face_zp) * (field - upper) + expand(face_zm) * (field - lower)


def shift_mult(shift_re, shift_im, field):
    return jnp.stack(
        [shift_re * field[0] - shift_im * field[1], shift_re * field[1] + shift_im * field[0]]
    )


def sine_both(field, sine_y, sine_z):
    field = jnp.einsum("pzxy,yj->pzxj", field, sine_y, precision=highest)
    return jnp.einsum("pzxy,zk->pkxy", field, sine_z, precision=highest)


def precondition(coeffs, mode_eig, mean_cond, shift_re, shift_im, sine_y, sine_z, eig_y, eig_z):
    coeffs = sine_both(coeffs, sine_y, sine_z)
    eigen = eig_z[:, None, None] + mode_eig[None, :, None] + eig_y[None, None, :]
    real_den = shift_re + mean_cond * eigen
    inv = 1.0 / (real_den * real_den + shift_im * shift_im)
    scaled = jnp.stack(
        [
            (coeffs[0] * real_den + coeffs[1] * shift_im) * inv,
            (coeffs[1] * real_den - coeffs[0] * shift_im) * inv,
        ]
    )
    return sine_both(scaled, sine_y, sine_z)


def body_plain(source, layer_ids, conduct_table, shift):
    shift_re = shift[0]
    shift_im = shift[1]
    planes = source.shape[1]
    length_x = source.shape[2]
    length_y = source.shape[3]
    groups = lax.axis_size("gz")
    length_z = planes * groups
    modes = length_x // groups
    first_mode = lax.axis_index("gz") * modes
    layers = conduct_table.shape[0]
    onehot = layer_ids[:, :, None] == lax.iota(jnp.int32, layers)[None, None, :]
    local = jnp.sum(jnp.where(onehot, conduct_table[None, None, :], 0.0), axis=-1)
    conduct = lax.all_gather(local, "gz", axis=0, tiled=True)
    mean_cond = jnp.sum(conduct) / (length_y * length_z)
    cond_z = jnp.pad(conduct, ((1, 1), (0, 0)), mode="edge")
    cos_t, sin_t = dft_tables(length_x)
    sine_y = sine_table(length_y)
    sine_z = sine_table(length_z)
    eig_y = sine_eigen(length_y)
    eig_z = sine_eigen(length_z)
    mode_ids = (first_mode + lax.iota(jnp.int32, modes)).astype(jnp.float32)
    mode_eig = 2.0 - 2.0 * jnp.cos(2.0 * jnp.pi / length_x * mode_ids)
    cells = length_x * length_y * length_z
    spectra = transform(source, cos_t, sin_t, False)
    forcing = lax.all_to_all(spectra, "gz", split_axis=2, concat_axis=1, tiled=True)
    partials = []
    solution = jnp.zeros_like(forcing)
    for iteration in range(ITERS):
        if iteration == 0:
            resid = forcing
        else:
            padded = jnp.pad(solution, ((0, 0), (1, 1), (0, 0), (0, 0)))
            lap = expand(conduct) * mode_eig[None, None, :, None] * solution
            lap = lap + yz_part(
                solution, padded[:, 2:], padded[:, :-2], conduct, cond_z[2:], cond_z[:-2]
            )
            resid = forcing - (shift_mult(shift_re, shift_im, solution) + lap)
        partials.append(jnp.sum(resid * resid) / length_x)
        update = precondition(
            resid, mode_eig, mean_cond, shift_re, shift_im, sine_y, sine_z, eig_y, eig_z
        )
        solution = solution + relax * update
    slabs = lax.all_to_all(solution, "gz", split_axis=1, concat_axis=2, tiled=True)
    result = transform(slabs, cos_t, sin_t, True)
    sums = jnp.sum(lax.all_gather(jnp.stack(partials)[None, :], "gz", axis=0, tiled=True), axis=0)
    return (result, jnp.sqrt(sums / cells))


RADIX = 4


def halves(table):
    high = table.astype(jnp.bfloat16)
    low = (table - high.astype(np.float32)).astype(jnp.bfloat16)
    return (jnp.asarray(high), jnp.asarray(low))


def radix_tables(length_x):
    count = length_x // RADIX
    pos = np.arange(count)
    forward = []
    for residue in range(RADIX):
        modes = RADIX * pos + residue
        angle = 2.0 * np.pi / length_x * (modes[:, None] * pos[None, :] % length_x)
        cos_t, sin_t = np.cos(angle), np.sin(angle)
        forward.append(np.block([[cos_t, sin_t], [-sin_t, cos_t]]))
    forward = np.stack(forward)
    backward = np.swapaxes(forward, 1, 2) / length_x
    return (forward.astype(np.float32), backward.astype(np.float32))


def sine_host(length):
    indices = np.arange(length) + 1
    product = indices[:, None] * indices[None, :] % (2 * (length + 1))
    return (np.sqrt(2.0 / (length + 1)) * np.sin(np.pi / (length + 1) * product)).astype(np.float32)


def split(values):
    high = values.astype(jnp.bfloat16)
    return (high, (values - high.astype(jnp.float32)).astype(jnp.bfloat16))


def dot3(left, right):
    mul = functools.partial(jnp.dot, preferred_element_type=jnp.float32)
    return mul(left[0], right[0]) + (mul(left[0], right[1]) + mul(left[1], right[0]))


def dot_wide(left, right):
    wide = jnp.concatenate([left[0], left[1], left[0]], axis=1)
    return jnp.dot(wide, right, preferred_element_type=jnp.float32)


def turn(re, im, quarter):
    quarter = quarter % 4
    return [(re, im), (-im, re), (-re, -im), (im, -re)][quarter]


def combine(parts, quarters):
    re, im = turn(*parts[0], quarters[0])
    for part, quarter in zip(parts[1:], quarters[1:]):
        more_re, more_im = turn(*part, quarter)
        re, im = re + more_re, im + more_im
    return (re, im)


def times(left, right):
    return (left[0] * right[0] - left[1] * right[1], left[0] * right[1] + left[1] * right[0])


def plus(left, right):
    return (left[0] + right[0], left[1] + right[1])


def pair(ref, *index):
    return (ref[(*index, 0)], ref[(*index, 1)])


def put(ref, values, *index):
    ref[(*index, 0)] = values[0]
    ref[(*index, 1)] = values[1]


def choose(test, left, right):
    return (jnp.where(test, left[0], right[0]), jnp.where(test, left[1], right[1]))


def kernel(
    groups,
    planes,
    chunks,
    layers,
    source_hbm,
    ids_hbm,
    table_hbm,
    shift_hbm,
    mode_hbm,
    eig_hbm,
    fwd_hi_hbm,
    fwd_lo_hbm,
    sine_hi_hbm,
    sine_lo_hbm,
    bwd_hi_hbm,
    bwd_lo_hbm,
    partial,
    tail,
    sums,
    source,
    ids,
    table,
    shift,
    mode_eig,
    eig_y,
    fwd_hi,
    fwd_lo,
    sine_hi,
    sine_lo,
    bwd_hi,
    bwd_lo,
    slabs,
    spectra,
    forcing,
    cond_own,
    cond_team,
    cond,
    edge_out,
    edge_in,
    half_out,
    half_in,
    faces,
    work,
    alpha,
    lines,
    field,
    result,
    sum_own,
    squares,
    pair_out,
    pair_in,
    rest_out,
    comb_out,
    comb_in,
    load_sem,
    in_send,
    in_recv,
    cond_send,
    cond_recv,
    edge_send,
    edge_recv,
    half_send,
    half_recv,
    out_send,
    out_recv,
    sum_send,
    sum_recv,
    own_sem,
    pair_send,
    pair_recv,
    comb_send,
    comb_recv,
):
    me = lax.axis_index("gz")
    side = lax.rem(me, RADIX)
    team = me // RADIX
    teams = groups // RADIX
    length_x = source.shape[2]
    length_y = source.shape[3]
    length_z = groups * planes
    depth = RADIX * planes
    count = length_x // RADIX
    modes = count // chunks
    first_level = team * depth
    last_level = length_z - first_level - depth

    pieces = [(ids_hbm, ids), (table_hbm, table), (shift_hbm, shift)]
    pieces += [(source_hbm.at[:, 0], source.at[:, 0])]
    for residue in range(RADIX):
        pieces += [(fwd_hi_hbm.at[residue], fwd_hi.at[residue])]
        pieces += [(fwd_lo_hbm.at[residue], fwd_lo.at[residue])]
    pieces += [(source_hbm.at[:, plane], source.at[:, plane]) for plane in range(1, planes)]
    pieces += [(sine_hi_hbm, sine_hi), (sine_lo_hbm, sine_lo)]
    pieces += [(mode_hbm.at[side], mode_eig), (eig_hbm, eig_y)]
    later = len(pieces)
    pieces += [(bwd_hi_hbm, bwd_hi), (bwd_lo_hbm, bwd_lo)]
    loads = [
        pltpu.make_async_copy(src, dst, load_sem.at[index])
        for index, (src, dst) in enumerate(pieces)
    ]
    for load in loads[:later]:
        load.start()

    def remote(src, dst, send, recv, target):
        return pltpu.make_async_remote_copy(
            src_ref=src,
            dst_ref=dst,
            send_sem=send,
            recv_sem=recv,
            device_id={"gz": target},
            device_id_type=pl.DeviceIdType.MESH,
        )

    def peer(offset):
        return lax.rem(me + offset, groups)

    def mate(offset):
        return lax.rem(side + offset, RADIX)

    def rows(index):
        return pl.ds(index * planes, planes)

    def cond_copy(offset):
        return remote(
            cond_own,
            cond_team.at[side],
            cond_send.at[offset],
            cond_recv.at[offset],
            team * RADIX + mate(offset),
        )

    def edge_copy(which):
        return remote(
            edge_out,
            edge_in.at[which],
            edge_send.at[which],
            edge_recv.at[which],
            me + [RADIX, -RADIX][which],
        )

    def half_copy(which):
        target = [teams - 1 - team, (teams - 1) * (2 - team)][which]
        return remote(
            half_out, half_in, half_send.at[which], half_recv.at[0], target * RADIX + side
        )

    def sum_copy(offset):
        return remote(
            sum_own, sums.at[me], sum_send.at[offset], sum_recv.at[offset], peer(offset)
        )

    def in_piece(chunk, offset, plane):
        target = mate(offset)
        return remote(
            spectra.at[target, chunk, pl.ds(plane, 1)],
            forcing.at[chunk, pl.ds(side * planes + plane, 1)],
            in_send.at[chunk, offset],
            in_recv.at[chunk, offset],
            team * RADIX + target,
        )

    def in_copy(chunk, offset):
        target = mate(offset)
        return remote(
            spectra.at[target, chunk],
            forcing.at[chunk, rows(side)],
            in_send.at[chunk, offset],
            in_recv.at[chunk, offset],
            team * RADIX + target,
        )

    def landing(chunk):
        return tail.at[side] if chunk is None else slabs.at[side, chunk]

    def out_copy(chunk, offset):
        target = mate(offset)
        index = chunks - 1 if chunk is None else chunk
        return remote(
            result.at[index, rows(target)],
            landing(chunk),
            out_send.at[index, offset],
            out_recv.at[index, offset],
            team * RADIX + target,
        )

    def own_copy(chunk):
        index = chunks - 1 if chunk is None else chunk
        return pltpu.make_async_copy(
            result.at[index, rows(side)], landing(chunk), own_sem.at[index]
        )

    even = lax.rem(team, 2) == 0
    inner = (team == 1) | (team == 2)
    lower = team < 2
    partner = team + 1 - 2 * lax.rem(team, 2)

    def pair_copy(turn_id, chunk):
        return remote(
            pair_out.at[turn_id, chunk],
            pair_in.at[turn_id, chunk],
            pair_send.at[turn_id, chunk],
            pair_recv.at[turn_id, chunk],
            partner * RADIX + side,
        )

    def comb_copy(turn_id, chunk, which):
        target = [teams - 1 - team, (teams - 1) * (2 - team)][which]
        return remote(
            comb_out.at[turn_id, chunk],
            comb_in.at[turn_id, chunk],
            comb_send.at[turn_id, chunk, which],
            comb_recv.at[turn_id, chunk],
            target * RADIX + side,
        )

    def each_peer(act):
        def run(offset, carry):
            act(offset)
            return carry

        lax.fori_loop(1, groups, run, 0)

    barrier = pltpu.get_barrier_semaphore()

    def greet(target):
        pl.semaphore_signal(
            barrier, inc=1, device_id={"gz": target}, device_id_type=pl.DeviceIdType.MESH
        )

    for offset in range(1, RADIX):
        greet(team * RADIX + mate(offset))

    @pl.when(team > 0)
    def _():
        greet(me - RADIX)

    @pl.when(team < teams - 1)
    def _():
        greet(me + RADIX)

    for load in loads[:3]:
        load.wait()
    found = jnp.zeros((planes, length_y), jnp.float32)
    for layer in range(layers):
        found = found + jnp.where(ids[...] == layer, table[layer], 0.0)
    cond_own[...] = found
    cond_team[side] = found

    def forward(plane):
        loads[3 if plane == 0 else 3 + 2 * RADIX + plane].wait()
        parts = [
            (
                source[0, plane, q * count : (q + 1) * count, :],
                source[1, plane, q * count : (q + 1) * count, :],
            )
            for q in range(RADIX)
        ]
        for residue in range(RADIX):
            if plane == 0:
                loads[4 + 2 * residue].wait()
                loads[5 + 2 * residue].wait()
            mixed = combine(parts, [-residue * q for q in range(RADIX)])
            right = split(jnp.concatenate(mixed, axis=0))
            values = dot3((fwd_hi[residue], fwd_lo[residue]), right)
            for chunk in range(chunks):
                for part in range(2):
                    start = part * count + chunk * modes
                    spectra[residue, chunk, plane, part] = values[start : start + modes]

    ends = jnp.where((team > 0) & (team < teams - 1), 0, 1)
    pl.semaphore_wait(barrier, RADIX + 1 - ends)
    for offset in range(1, RADIX):
        cond_copy(offset).start()
    forward(0)
    for offset in (2, 3, 1):
        in_piece(0, offset, 0).start()
    for plane in range(1, planes):
        forward(plane)
        for offset in (2, 3, 1):
            in_piece(0, offset, plane).start()

    for load in loads[3 + 2 * RADIX + planes : later]:
        load.wait()
    for load in loads[later:]:
        load.start()
    sine = jnp.concatenate([sine_hi[...], sine_hi[...], sine_lo[...]], axis=0)

    def sine_rows(values):
        flat = values.reshape(-1, length_y)
        return dot_wide(split(flat), sine).reshape(values.shape)

    def send_in(chunk, carry):
        spectra[:, chunk] = sine_rows(spectra[:, chunk])
        for offset in (2, 3, 1):
            in_copy(chunk, offset).start()
        return carry

    lax.fori_loop(1, 2, send_in, 0)
    for offset in range(1, RADIX):
        cond_copy(offset).wait()
    total = jnp.zeros((1, length_y), jnp.float32)
    for index in range(RADIX):
        for plane in range(planes):
            row = cond_team[index, plane : plane + 1, :]
            cond[index * planes + plane + 1] = jnp.broadcast_to(row, (8, length_y))
            total = total + row
    edge_out[0:1] = total
    edge_out[1:2] = cond_team[0, 0:1, :]
    edge_out[2:3] = cond_team[RADIX - 1, planes - 1 : planes, :]

    @pl.when(team < teams - 1)
    def _():
        edge_copy(0).start()

    @pl.when(team > 0)
    def _():
        edge_copy(1).start()

    lax.fori_loop(2, chunks - 3, send_in, 0)


    @pl.when(team > 0)
    def _():
        edge_copy(0).wait_recv()
        cond[0] = jnp.broadcast_to(edge_in[0, 2:3, :], (8, length_y))

    @pl.when(team == 0)
    def _():
        cond[0] = cond[1]

    @pl.when(team < teams - 1)
    def _():
        edge_copy(1).wait_recv()
        cond[depth + 1] = jnp.broadcast_to(edge_in[1, 1:2, :], (8, length_y))

    @pl.when(team == teams - 1)
    def _():
        cond[depth + 1] = cond[depth]

    @pl.when(even)
    def _():
        half_out[0:1] = total + edge_in[1, 0:1, :]

    @pl.when(jnp.logical_not(even))
    def _():
        half_out[0:1] = total + edge_in[0, 0:1, :]

    @pl.when(inner)
    def _():
        half_copy(1).start()
        half_copy(0).start()

    shift_re = shift[0]
    shift_im = shift[1]
    row_lane = lax.broadcasted_iota(jnp.int32, (8, length_y), 1)
    last = length_y - 1

    lax.fori_loop(chunks - 3, chunks, send_in, 0)

    def keep(chunk, carry):
        forcing[chunk, rows(side)] = spectra[side, chunk]
        return carry

    lax.fori_loop(0, chunks, keep, 0)

    def make_faces(index, carry):
        here = cond[index + 1]
        right = jnp.where(row_lane == last, here, pltpu.roll(here, last, 1))
        left = jnp.where(row_lane == 0, here, pltpu.roll(here, 1, 1))
        face_yp = 0.5 * (here + right)
        face_ym = 0.5 * (here + left)
        face_zp = 0.5 * (here + cond[index + 2])
        face_zm = 0.5 * (here + cond[index])
        faces[index, 0] = here
        faces[index, 1] = face_yp + face_ym + face_zp + face_zm + shift_re
        faces[index, 2] = jnp.where(row_lane == last, 0.0, face_yp)
        faces[index, 3] = jnp.where(row_lane == 0, 0.0, face_ym)
        faces[index, 4] = face_zp
        faces[index, 5] = face_zm
        return carry

    lax.fori_loop(0, depth, make_faces, 0)
    def take(chunk):
        for offset in range(1, RADIX):
            in_copy(chunk, offset).wait()

    take(0)
    forcing[0] = sine_rows(forcing[0])
    half_copy(0).wait_recv()
    total = half_out[0:1, :] + half_in[0:1, :]
    mean_cond = jnp.sum(total) / (length_y * length_z)
    scale = relax / mean_cond
    offset_re = shift_re / mean_cond
    diag_im = shift_im / mean_cond
    none = jnp.zeros((modes, length_y), jnp.float32)
    one = jnp.ones((modes, length_y), jnp.float32)

    def eigen(chunk):
        return jnp.concatenate([mode_eig[chunk]] * (length_y // 128), axis=1)

    def factors(chunk):
        diag_re = eigen(chunk) + (eig_y[0:1, :] + offset_re)

        def factor(level, carry):
            gap_re = diag_re - carry[0]
            gap_im = diag_im - carry[1]
            inverse = 1.0 / (gap_re * gap_re + gap_im * gap_im)
            now = (gap_re * inverse, -gap_im * inverse)
            put(alpha, now, chunk, level)
            return now

        def segment(index, carry):
            def inner_level(level, state):
                now = factor(index * depth + level + 1, state[:2])
                return (*now, *times(now, state[2:]))

            state = lax.fori_loop(0, depth, inner_level, (*carry, one, none), unroll=True)
            put(lines, state[2:], chunk, index)
            return state[:2]

        put(alpha, (none, none), chunk, 0)
        lax.fori_loop(0, teams, segment, (none, none))

    given = (forcing, work)

    def launch(turn_id, chunk):
        def rise(index, carry):
            up = times(
                pair(alpha, chunk, first_level + index + 1),
                plus(pair(given[turn_id], chunk, index), carry[:2]),
            )
            down = times(
                pair(alpha, chunk, last_level + index + 1),
                plus(pair(given[turn_id], chunk, depth - 1 - index), carry[2:]),
            )
            return (*up, *down)

        ends = lax.fori_loop(0, depth, rise, (none, none, none, none), unroll=True)
        put(pair_out, choose(even, ends[:2], ends[2:]), turn_id, chunk)
        pair_copy(turn_id, chunk).start()
        put(rest_out, choose(even, ends[2:], ends[:2]), turn_id, chunk)

    def relay(turn_id, chunk):
        pair_copy(turn_id, chunk).wait_recv()

        @pl.when(inner)
        def _():
            more = times(pair(lines, chunk, 1), pair(pair_in, turn_id, chunk))
            put(comb_out, plus(pair(rest_out, turn_id, chunk), more), turn_id, chunk)
            comb_copy(turn_id, chunk, 1).start()
            comb_copy(turn_id, chunk, 0).start()

    def solve(turn_id, chunk):
        comb_copy(turn_id, chunk, 0).wait_recv()
        near = pair(pair_in, turn_id, chunk)
        wide = pair(comb_in, turn_id, chunk)
        joined = plus(near, times(pair(lines, chunk, teams - 2), wide))
        far = choose(inner, wide, joined)
        near = choose(inner, near, (none, none))
        below = choose(lower, near, far)
        above = choose(lower, far, near)

        def ahead(index, carry):
            factor = pair(alpha, chunk, first_level + index + 1)
            now = times(factor, plus(pair(given[turn_id], chunk, index), carry))
            put(work, now, chunk, index)
            return now

        reached = lax.fori_loop(0, depth, ahead, below, unroll=True)
        factor = pair(alpha, chunk, first_level + depth)
        edge = pair(alpha, chunk, last_level)
        echo = times(factor, edge)
        gap_re = 1.0 - echo[0]
        inverse = 1.0 / (gap_re * gap_re + echo[1] * echo[1])
        top = plus(reached, times(factor, above))
        top = times(top, (gap_re * inverse, echo[1] * inverse))
        outer = plus(above, times(edge, top))
        put(work, outer, chunk, depth + 1)

        def behind(step, carry):
            index = depth - 1 - step
            factor = pair(alpha, chunk, first_level + index + 1)
            now = plus(pair(work, chunk, index), times(factor, carry))
            put(work, now, chunk, index)
            return now

        bottom = lax.fori_loop(0, depth, behind, outer, unroll=True)
        put(work, plus(below, times(pair(alpha, chunk, first_level), bottom)), chunk, depth)

    def blocks(values):
        return values.reshape(modes // 8, 8, length_y)

    def operator(chunk):
        eig = blocks(eigen(chunk))

        def run(index, carry):
            center = faces[index, 0] * eig + faces[index, 1]
            values = pair(field, chunk, index + 1)
            turned = (-shift_im * values[1], shift_im * values[0])
            above = pair(field, chunk, index + 2)
            below = pair(field, chunk, index)
            for part in range(2):
                value = values[part]
                applied = center * blocks(value) + blocks(turned[part])
                applied = applied - faces[index, 2] * blocks(pltpu.roll(value, last, 1))
                applied = applied - faces[index, 3] * blocks(pltpu.roll(value, 1, 1))
                applied = applied - faces[index, 4] * blocks(above[part])
                applied = applied - faces[index, 5] * blocks(below[part])
                work[chunk, index, part] = applied.reshape(modes, length_y)
            return carry

        lax.fori_loop(0, depth, run, 0, unroll=8)

    squares[0] = none
    squares[1] = none
    factors(0)

    def begin(chunk):
        @pl.when(chunk > 0)
        def _():
            take(chunk)

        launch(0, chunk)

    def middle(chunk):
        solve(0, chunk)
        values = sine_rows(work[chunk]) * scale
        field[chunk, pl.ds(1, depth)] = values[:depth]
        field[chunk, 0] = values[depth]
        field[chunk, depth + 1] = values[depth + 1]
        operator(chunk)
        here = forcing[chunk]
        rest = here - sine_rows(work[chunk, pl.ds(0, depth)])
        work[chunk, pl.ds(0, depth)] = rest
        launch(1, chunk)
        squares[0] = squares[0] + jnp.sum(here * here, axis=(0, 1))
        squares[1] = squares[1] + jnp.sum(rest * rest, axis=(0, 1))

        @pl.when(chunk == chunks - 1)
        def _():
            row = lax.broadcasted_iota(jnp.int32, (ITERS, 128), 0)
            both = jnp.where(row == 0, jnp.sum(squares[0]), jnp.sum(squares[1]))
            sum_own[...] = both / length_x

            @each_peer
            def _(offset):
                sum_copy(offset).start()

            pltpu.make_async_copy(sum_own, sums.at[me], own_sem.at[chunks]).start()

    def finish(chunk):
        solve(1, chunk)
        values = sine_rows(work[chunk, pl.ds(0, depth)]) * scale
        result[chunk] = field[chunk, pl.ds(1, depth)] + values

        def put_out(which):
            for offset in (2, 3, 1):
                out_copy(which, offset).start()
            own_copy(which).start()

        @pl.when(chunk < chunks - 1)
        def _():
            put_out(chunk)

        @pl.when(chunk == chunks - 1)
        def _():
            put_out(None)

    def ready(chunk):
        @pl.when(chunk + 1 < chunks)
        def _():
            factors(chunk + 1)

    stages = {
        "begin": (0, begin),
        "ready": (0, ready),
        "relay": (LAGS[0], functools.partial(relay, 0)),
        "middle": (LAGS[1], middle),
        "again": (LAGS[2], functools.partial(relay, 1)),
        "finish": (LAGS[3], finish),
    }

    def step(index, carry):
        for name in ORDER:
            lag, act = stages[name]

            @pl.when((index >= lag) & (index < chunks + lag))
            def _():
                act(index - lag)

        return carry

    lax.fori_loop(0, chunks + LAGS[3], step, 0)

    def settle(chunk, carry):
        for turn_id in range(2):
            pair_copy(turn_id, chunk).wait_send()

            @pl.when(inner)
            def _():
                comb_copy(turn_id, chunk, 0).wait_send()
                comb_copy(turn_id, chunk, 1).wait_send()

        return carry

    def arrive(chunk, carry):
        own_copy(chunk).wait()
        for offset in range(1, RADIX):
            out_copy(chunk, offset).wait()
        return carry

    for load in loads[later:]:
        load.wait()
    lax.fori_loop(0, chunks - 1, arrive, 0)

    def gather(plane, carry):
        for residue in range(RADIX):
            blocks = []
            for part in range(2):
                blocks += [slabs[residue, chunk, plane, part] for chunk in range(chunks - 1)]
                blocks += [none]
            right = split(jnp.concatenate(blocks, axis=0))
            partial[plane, residue] = dot3((bwd_hi[residue], bwd_lo[residue]), right)
        return carry

    lax.fori_loop(0, planes, gather, 0)

    pltpu.make_async_copy(sum_own, sums.at[me], own_sem.at[chunks]).wait()

    @pl.when(team < teams - 1)
    def _():
        edge_copy(0).wait_send()

    @pl.when(team > 0)
    def _():
        edge_copy(1).wait_send()

    @pl.when(inner)
    def _():
        half_copy(0).wait_send()
        half_copy(1).wait_send()

    @each_peer
    def _(offset):
        sum_copy(offset).wait()

    lax.fori_loop(0, chunks, settle, 0)
    arrive(None, 0)


def ending(cells, partial, tail, sums, table, out, norms, stage, out_sem):
    planes, _, twice, length_y = partial.shape
    count = twice // 2
    modes = tail.shape[3]

    def store(plane, q):
        return pltpu.make_async_copy(
            stage.at[:, plane, pl.ds(q * count, count), :],
            out.at[:, plane, pl.ds(q * count, count), :],
            out_sem.at[plane, q],
        )

    for plane in range(planes):
        parts = []
        for residue in range(RADIX):
            high, low = split(tail[residue, plane].reshape(2 * modes, length_y))
            right = jnp.concatenate([high, low, high], axis=0)
            more = jnp.dot(table[residue], right, preferred_element_type=jnp.float32)
            values = partial[plane, residue] + more
            parts.append((values[:count], values[count:]))
        for q in range(RADIX):
            re, im = combine(parts, [residue * q for residue in range(RADIX)])
            stage[0, plane, q * count : (q + 1) * count, :] = re
            stage[1, plane, q * count : (q + 1) * count, :] = im
            store(plane, q).start()
    root = jnp.sqrt(jnp.sum(sums[...], axis=0) / cells)
    for index in range(ITERS):
        norms[index] = root[index, 0]
    for plane in range(planes):
        for q in range(RADIX):
            store(plane, q).wait()


CHUNKS = 8
LAGS = (1, 2, 3, 5)
ORDER = ("begin", "relay", "finish", "middle", "ready", "again")


def body(source, layer_ids, conduct_table, shift):
    planes = source.shape[1]
    length_x = source.shape[2]
    length_y = source.shape[3]
    groups = lax.axis_size("gz")
    length_z = planes * groups
    count = length_x // RADIX
    modes = count // CHUNKS
    if groups != 4 * RADIX or modes % 8 or planes > 8 or length_z > 64 or length_y % 128:
        return body_plain(source, layer_ids, conduct_table, shift)
    depth = planes * RADIX
    layers = conduct_table.shape[0]
    mode_ids = RADIX * np.arange(count)[None, :] + np.arange(RADIX)[:, None]
    mode_eig = (2.0 - 2.0 * np.cos(2.0 * np.pi / length_x * mode_ids)).astype(np.float32)
    mode_eig = np.broadcast_to(mode_eig[:, :, None], (RADIX, count, 128))
    mode_eig = np.ascontiguousarray(mode_eig).reshape(RADIX, CHUNKS, modes, 128)
    eig_y = 4.0 - 2.0 * np.cos(np.pi / (length_y + 1) * (np.arange(length_y) + 1.0))
    eig_y = np.ascontiguousarray(np.broadcast_to(eig_y.astype(np.float32), (8, length_y)))
    forward, backward = radix_tables(length_x)
    tables = [*halves(forward), *halves(sine_host(length_y)), *halves(backward)]
    final = np.concatenate([part * count + np.arange(count - modes, count) for part in range(2)])
    final = backward[:, :, final]
    high = final.astype(jnp.bfloat16)
    low = (final - high.astype(np.float32)).astype(jnp.bfloat16)
    final = jnp.asarray(np.concatenate([high, high, low], axis=2))
    tile = (2, modes, length_y)
    smem = pl.BlockSpec(memory_space=pltpu.SMEM)
    hbm = pl.BlockSpec(memory_space=pl.ANY)
    vmem = pl.BlockSpec(memory_space=pltpu.VMEM)
    f32 = jnp.float32
    dma = pltpu.SemaphoreType.DMA
    in_hbm = functools.partial(pltpu.with_memory_space_constraint, memory_space=pltpu.HBM)
    partial, tail, sums = pl.pallas_call(
        functools.partial(kernel, groups, planes, CHUNKS, layers),
        out_shape=(
            pltpu.VMEM((planes, RADIX, 2 * count, length_y), f32),
            pltpu.VMEM((RADIX, planes, *tile), f32),
            pltpu.VMEM((groups, ITERS, 128), f32),
        ),
        in_specs=[hbm] * 12,
        out_specs=(vmem, hbm, hbm),
        scratch_shapes=[
            pltpu.VMEM(source.shape, f32),
            pltpu.VMEM(layer_ids.shape, jnp.int32),
            pltpu.SMEM(conduct_table.shape, f32),
            pltpu.SMEM(shift.shape, f32),
            pltpu.VMEM((CHUNKS, modes, 128), f32),
            pltpu.VMEM((8, length_y), f32),
        ]
        + [pltpu.VMEM(table.shape, jnp.bfloat16) for table in tables]
        + [
            pltpu.VMEM((RADIX, CHUNKS - 1, planes, *tile), f32),
            pltpu.VMEM((RADIX, CHUNKS, planes, *tile), f32),
            pltpu.VMEM((CHUNKS, depth, *tile), f32),
            pltpu.VMEM((planes, length_y), f32),
            pltpu.VMEM((RADIX, planes, length_y), f32),
            pltpu.VMEM((depth + 2, 8, length_y), f32),
            pltpu.VMEM((4, length_y), f32),
            pltpu.VMEM((2, 4, length_y), f32),
            pltpu.VMEM((4, length_y), f32),
            pltpu.VMEM((4, length_y), f32),
            pltpu.VMEM((depth, 6, 8, length_y), f32),
            pltpu.VMEM((CHUNKS, depth + 2, *tile), f32),
            pltpu.VMEM((CHUNKS, length_z + 1, *tile), f32),
            pltpu.VMEM((CHUNKS, groups // RADIX, *tile), f32),
            pltpu.VMEM((CHUNKS, depth + 2, *tile), f32),
            pltpu.VMEM((CHUNKS, depth, *tile), f32),
            pltpu.VMEM((ITERS, 128), f32),
            pltpu.VMEM(tile, f32),
        ]
        + [pltpu.VMEM((ITERS, CHUNKS, *tile), f32)] * 5
        + [dma((9 + 2 * RADIX + planes,))]
        + [dma((CHUNKS, RADIX))] * 2
        + [dma((RADIX,))] * 2
        + [dma((2,))] * 2
        + [dma((2,)), dma((1,))]
        + [dma((CHUNKS, RADIX))] * 2
        + [dma((groups,))] * 2
        + [dma((CHUNKS + 1,))]
        + [dma((ITERS, CHUNKS))] * 2
        + [dma((ITERS, CHUNKS, 2)), dma((ITERS, CHUNKS))],
        compiler_params=pltpu.CompilerParams(
            collective_id=0, has_side_effects=True, vmem_limit_bytes=50 << 20
        ),
    )(
        in_hbm(source),
        in_hbm(layer_ids),
        in_hbm(conduct_table),
        in_hbm(shift),
        *[in_hbm(jnp.asarray(table)) for table in (mode_eig, eig_y, *tables)],
    )
    cells = length_x * length_y * length_z
    return pl.pallas_call(
        functools.partial(ending, cells),
        out_shape=(
            jax.ShapeDtypeStruct(source.shape, f32),
            jax.ShapeDtypeStruct((ITERS,), f32),
        ),
        in_specs=[vmem] * 4,
        out_specs=(hbm, smem),
        scratch_shapes=[pltpu.VMEM(source.shape, f32), dma((planes, RADIX))],
        compiler_params=pltpu.CompilerParams(vmem_limit_bytes=20 << 20),
    )(partial, tail, sums, final)


def solution(mesh):
    placed = (P(None, ("node", "gz"), None, None), P(("node", "gz"), None), P(), P("node"))
    return jax.shard_map(
        body,
        mesh=mesh,
        in_specs=placed,
        out_specs=(P(None, ("node", "gz"), None, None), P("node")),
        check_vma=False,
    )
```

```python
import functools

import jax
import jax.numpy as jnp
import numpy as np
from jax import lax
from jax.experimental import pallas as pl
from jax.experimental.pallas import tpu as pltpu
from jax.sharding import PartitionSpec as P

ITERS = 2


relax = 0.6
highest = lax.Precision.HIGH


def with_halo(cells, sides, width):
    for axis, dim in sides:
        count = lax.axis_size(axis)
        ends = count - 1
        head = lax.slice_in_dim(cells, 0, width, axis=dim)
        tail = lax.slice_in_dim(cells, cells.shape[dim] - width, cells.shape[dim], axis=dim)
        cells = jnp.concatenate(
            [
                lax.ppermute(tail, axis, [(i, (i + 1) % count) for i in range(ends)]),
                cells,
                lax.ppermute(head, axis, [((i + 1) % count, i) for i in range(ends)]),
            ],
            axis=dim,
        )
    return cells


def sine_table(length):
    indices = lax.iota(jnp.int32, length) + 1
    product = indices[:, None] * indices[None, :] % (2 * (length + 1))
    return jnp.sqrt(2.0 / (length + 1)) * jnp.sin(
        jnp.pi / (length + 1) * product.astype(jnp.float32)
    )


def sine_eigen(length):
    indices = lax.iota(jnp.float32, length) + 1.0
    return 2.0 - 2.0 * jnp.cos(jnp.pi / (length + 1) * indices)


def dft_tables(length):
    indices = lax.iota(jnp.int32, length)
    product = indices[:, None] * indices[None, :] % length
    angles = 2.0 * jnp.pi / length * product.astype(jnp.float32)
    return (jnp.cos(angles), jnp.sin(angles))


def transform(field, cos_t, sin_t, inverse):

    def project(component, matrix):
        return jnp.einsum("zxy,xk->zky", component, matrix, precision=highest)

    re_cos = project(field[0], cos_t)
    re_sin = project(field[0], sin_t)
    im_cos = project(field[1], cos_t)
    im_sin = project(field[1], sin_t)
    if inverse:
        return jnp.stack([re_cos - im_sin, im_cos + re_sin]) / cos_t.shape[0]
    return jnp.stack([re_cos + im_sin, im_cos - re_sin])


def expand(weights):
    return weights[None, :, None, :]


def yz_part(field, upper, lower, conduct, cond_hi, cond_lo):
    cond_pad = jnp.pad(conduct, ((0, 0), (1, 1)), mode="edge")
    face_yp = 0.5 * (conduct + cond_pad[:, 2:])
    face_ym = 0.5 * (conduct + cond_pad[:, :-2])
    face_zp = 0.5 * (conduct + cond_hi)
    face_zm = 0.5 * (conduct + cond_lo)
    field_pad = jnp.pad(field, ((0, 0), (0, 0), (0, 0), (1, 1)))
    total = expand(face_yp) * (field - field_pad[..., 2:]) + expand(face_ym) * (
        field - field_pad[..., :-2]
    )
    return total + expand(face_zp) * (field - upper) + expand(face_zm) * (field - lower)


def shift_mult(shift_re, shift_im, field):
    return jnp.stack(
        [shift_re * field[0] - shift_im * field[1], shift_re * field[1] + shift_im * field[0]]
    )


def sine_both(field, sine_y, sine_z):
    field = jnp.einsum("pzxy,yj->pzxj", field, sine_y, precision=highest)
    return jnp.einsum("pzxy,zk->pkxy", field, sine_z, precision=highest)


def precondition(coeffs, mode_eig, mean_cond, shift_re, shift_im, sine_y, sine_z, eig_y, eig_z):
    coeffs = sine_both(coeffs, sine_y, sine_z)
    eigen = eig_z[:, None, None] + mode_eig[None, :, None] + eig_y[None, None, :]
    real_den = shift_re + mean_cond * eigen
    inv = 1.0 / (real_den * real_den + shift_im * shift_im)
    scaled = jnp.stack(
        [
            (coeffs[0] * real_den + coeffs[1] * shift_im) * inv,
            (coeffs[1] * real_den - coeffs[0] * shift_im) * inv,
        ]
    )
    return sine_both(scaled, sine_y, sine_z)


def body_plain(source, layer_ids, conduct_table, shift):
    shift_re = shift[0]
    shift_im = shift[1]
    planes = source.shape[1]
    length_x = source.shape[2]
    length_y = source.shape[3]
    groups = lax.axis_size("gz")
    length_z = planes * groups
    modes = length_x // groups
    first_mode = lax.axis_index("gz") * modes
    layers = conduct_table.shape[0]
    onehot = layer_ids[:, :, None] == lax.iota(jnp.int32, layers)[None, None, :]
    local = jnp.sum(jnp.where(onehot, conduct_table[None, None, :], 0.0), axis=-1)
    conduct = lax.all_gather(local, "gz", axis=0, tiled=True)
    mean_cond = jnp.sum(conduct) / (length_y * length_z)
    cond_z = jnp.pad(conduct, ((1, 1), (0, 0)), mode="edge")
    cos_t, sin_t = dft_tables(length_x)
    sine_y = sine_table(length_y)
    sine_z = sine_table(length_z)
    eig_y = sine_eigen(length_y)
    eig_z = sine_eigen(length_z)
    mode_ids = (first_mode + lax.iota(jnp.int32, modes)).astype(jnp.float32)
    mode_eig = 2.0 - 2.0 * jnp.cos(2.0 * jnp.pi / length_x * mode_ids)
    cells = length_x * length_y * length_z
    spectra = transform(source, cos_t, sin_t, False)
    forcing = lax.all_to_all(spectra, "gz", split_axis=2, concat_axis=1, tiled=True)
    partials = []
    solution = jnp.zeros_like(forcing)
    for iteration in range(ITERS):
        if iteration == 0:
            resid = forcing
        else:
            padded = jnp.pad(solution, ((0, 0), (1, 1), (0, 0), (0, 0)))
            lap = expand(conduct) * mode_eig[None, None, :, None] * solution
            lap = lap + yz_part(
                solution, padded[:, 2:], padded[:, :-2], conduct, cond_z[2:], cond_z[:-2]
            )
            resid = forcing - (shift_mult(shift_re, shift_im, solution) + lap)
        partials.append(jnp.sum(resid * resid) / length_x)
        update = precondition(
            resid, mode_eig, mean_cond, shift_re, shift_im, sine_y, sine_z, eig_y, eig_z
        )
        solution = solution + relax * update
    slabs = lax.all_to_all(solution, "gz", split_axis=1, concat_axis=2, tiled=True)
    result = transform(slabs, cos_t, sin_t, True)
    sums = jnp.sum(lax.all_gather(jnp.stack(partials)[None, :], "gz", axis=0, tiled=True), axis=0)
    return (result, jnp.sqrt(sums / cells))


RADIX = 4


def halves(table):
    high = table.astype(jnp.bfloat16)
    low = (table - high.astype(np.float32)).astype(jnp.bfloat16)
    return (jnp.asarray(high), jnp.asarray(low))


def radix_tables(length_x):
    count = length_x // RADIX
    pos = np.arange(count)
    forward = []
    for residue in range(RADIX):
        modes = RADIX * pos + residue
        angle = 2.0 * np.pi / length_x * (modes[:, None] * pos[None, :] % length_x)
        cos_t, sin_t = np.cos(angle), np.sin(angle)
        forward.append(np.block([[cos_t, sin_t], [-sin_t, cos_t]]))
    forward = np.stack(forward)
    backward = np.swapaxes(forward, 1, 2) / length_x
    return (forward.astype(np.float32), backward.astype(np.float32))


def sine_host(length):
    indices = np.arange(length) + 1
    product = indices[:, None] * indices[None, :] % (2 * (length + 1))
    return (np.sqrt(2.0 / (length + 1)) * np.sin(np.pi / (length + 1) * product)).astype(np.float32)


def split(values):
    high = values.astype(jnp.bfloat16)
    return (high, (values - high.astype(jnp.float32)).astype(jnp.bfloat16))


def dot3(left, right):
    mul = functools.partial(jnp.dot, preferred_element_type=jnp.float32)
    return mul(left[0], right[0]) + (mul(left[0], right[1]) + mul(left[1], right[0]))


def dot_wide(left, right):
    wide = jnp.concatenate([left[0], left[1], left[0]], axis=1)
    return jnp.dot(wide, right, preferred_element_type=jnp.float32)


def turn(re, im, quarter):
    quarter = quarter % 4
    return [(re, im), (-im, re), (-re, -im), (im, -re)][quarter]


def combine(parts, quarters):
    re, im = turn(*parts[0], quarters[0])
    for part, quarter in zip(parts[1:], quarters[1:]):
        more_re, more_im = turn(*part, quarter)
        re, im = re + more_re, im + more_im
    return (re, im)


def times(left, right):
    return (left[0] * right[0] - left[1] * right[1], left[0] * right[1] + left[1] * right[0])


def plus(left, right):
    return (left[0] + right[0], left[1] + right[1])


def pair(ref, *index):
    return (ref[(*index, 0)], ref[(*index, 1)])


def put(ref, values, *index):
    ref[(*index, 0)] = values[0]
    ref[(*index, 1)] = values[1]


def choose(test, left, right):
    return (jnp.where(test, left[0], right[0]), jnp.where(test, left[1], right[1]))


def kernel(
    groups,
    planes,
    chunks,
    layers,
    source_hbm,
    ids_hbm,
    table_hbm,
    shift_hbm,
    mode_hbm,
    eig_hbm,
    fwd_hi_hbm,
    fwd_lo_hbm,
    sine_hi_hbm,
    sine_lo_hbm,
    bwd_hi_hbm,
    bwd_lo_hbm,
    partial,
    tail,
    sums,
    source,
    ids,
    table,
    shift,
    mode_eig,
    eig_y,
    fwd_hi,
    fwd_lo,
    sine_hi,
    sine_lo,
    bwd_hi,
    bwd_lo,
    slabs,
    spectra,
    forcing,
    cond_own,
    cond_team,
    cond,
    edge_out,
    edge_in,
    half_out,
    half_in,
    faces,
    work,
    alpha,
    lines,
    field,
    result,
    sum_own,
    squares,
    pair_out,
    pair_in,
    rest_out,
    comb_out,
    comb_in,
    load_sem,
    in_send,
    in_recv,
    cond_send,
    cond_recv,
    edge_send,
    edge_recv,
    half_send,
    half_recv,
    out_send,
    out_recv,
    sum_send,
    sum_recv,
    own_sem,
    pair_send,
    pair_recv,
    comb_send,
    comb_recv,
):
    me = lax.axis_index("gz")
    side = lax.rem(me, RADIX)
    team = me // RADIX
    teams = groups // RADIX
    length_x = source.shape[2]
    length_y = source.shape[3]
    length_z = groups * planes
    depth = RADIX * planes
    count = length_x // RADIX
    modes = count // chunks
    first_level = team * depth
    last_level = length_z - first_level - depth

    pieces = [(ids_hbm, ids), (table_hbm, table), (shift_hbm, shift)]
    pieces += [(source_hbm.at[:, 0], source.at[:, 0])]
    across = jnp.where(side < RADIX // 2, RADIX // 2, 0)
    for step in range(RADIX):
        residue = lax.rem(across + step, RADIX)
        pieces += [(fwd_hi_hbm.at[residue], fwd_hi.at[residue])]
        pieces += [(fwd_lo_hbm.at[residue], fwd_lo.at[residue])]
    pieces += [(source_hbm.at[:, plane], source.at[:, plane]) for plane in range(1, planes)]
    pieces += [(sine_hi_hbm, sine_hi), (sine_lo_hbm, sine_lo)]
    pieces += [(mode_hbm.at[side], mode_eig), (eig_hbm, eig_y)]
    later = len(pieces)
    pieces += [(bwd_hi_hbm, bwd_hi), (bwd_lo_hbm, bwd_lo)]
    loads = [
        pltpu.make_async_copy(src, dst, load_sem.at[index])
        for index, (src, dst) in enumerate(pieces)
    ]
    first = 4 + RADIX
    for load in loads[:first]:
        load.start()

    def remote(src, dst, send, recv, target):
        return pltpu.make_async_remote_copy(
            src_ref=src,
            dst_ref=dst,
            send_sem=send,
            recv_sem=recv,
            device_id={"gz": target},
            device_id_type=pl.DeviceIdType.MESH,
        )

    def peer(offset):
        return lax.rem(me + offset, groups)

    def mate(offset):
        return lax.rem(side + offset, RADIX)

    def rows(index):
        return pl.ds(index * planes, planes)

    def cond_copy(offset):
        return remote(
            cond_own,
            cond_team.at[side],
            cond_send.at[offset],
            cond_recv.at[offset],
            team * RADIX + mate(offset),
        )

    def edge_copy(which):
        return remote(
            edge_out,
            edge_in.at[which],
            edge_send.at[which],
            edge_recv.at[which],
            me + [RADIX, -RADIX][which],
        )

    def half_copy(which):
        target = [teams - 1 - team, (teams - 1) * (2 - team)][which]
        return remote(
            half_out, half_in, half_send.at[which], half_recv.at[0], target * RADIX + side
        )

    def sum_copy(offset):
        return remote(
            sum_own, sums.at[me], sum_send.at[offset], sum_recv.at[offset], peer(offset)
        )

    def in_piece(chunk, offset, plane):
        target = mate(offset)
        return remote(
            spectra.at[target, chunk, pl.ds(plane, 1)],
            forcing.at[chunk, pl.ds(side * planes + plane, 1)],
            in_send.at[chunk, offset],
            in_recv.at[chunk, offset],
            team * RADIX + target,
        )

    def in_copy(chunk, offset):
        target = mate(offset)
        return remote(
            spectra.at[target, chunk],
            forcing.at[chunk, rows(side)],
            in_send.at[chunk, offset],
            in_recv.at[chunk, offset],
            team * RADIX + target,
        )

    def landing(chunk):
        return tail.at[side] if chunk is None else slabs.at[side, chunk]

    def out_copy(chunk, offset):
        target = mate(offset)
        index = chunks - 1 if chunk is None else chunk
        return remote(
            result.at[index, rows(target)],
            landing(chunk),
            out_send.at[index, offset],
            out_recv.at[index, offset],
            team * RADIX + target,
        )

    def own_copy(chunk):
        index = chunks - 1 if chunk is None else chunk
        return pltpu.make_async_copy(
            result.at[index, rows(side)], landing(chunk), own_sem.at[index]
        )

    even = lax.rem(team, 2) == 0
    inner = (team == 1) | (team == 2)
    lower = team < 2
    partner = team + 1 - 2 * lax.rem(team, 2)

    def pair_copy(turn_id, chunk):
        return remote(
            pair_out.at[turn_id, chunk],
            pair_in.at[turn_id, chunk],
            pair_send.at[turn_id, chunk],
            pair_recv.at[turn_id, chunk],
            partner * RADIX + side,
        )

    def comb_copy(turn_id, chunk, which):
        target = [teams - 1 - team, (teams - 1) * (2 - team)][which]
        return remote(
            comb_out.at[turn_id, chunk],
            comb_in.at[turn_id, chunk],
            comb_send.at[turn_id, chunk, which],
            comb_recv.at[turn_id, chunk],
            target * RADIX + side,
        )

    def each_peer(act):
        def run(offset, carry):
            act(offset)
            return carry

        lax.fori_loop(1, groups, run, 0)

    barrier = pltpu.get_barrier_semaphore()

    def greet(target):
        pl.semaphore_signal(
            barrier, inc=1, device_id={"gz": target}, device_id_type=pl.DeviceIdType.MESH
        )

    for offset in range(1, RADIX):
        greet(team * RADIX + mate(offset))

    @pl.when(team > 0)
    def _():
        greet(me - RADIX)

    @pl.when(team < teams - 1)
    def _():
        greet(me + RADIX)

    for load in loads[:3]:
        load.wait()
    for load in loads[first:later]:
        load.start()
    found = jnp.zeros((planes, length_y), jnp.float32)
    for layer in range(layers):
        found = found + jnp.where(ids[...] == layer, table[layer], 0.0)
    cond_own[...] = found
    cond_team[side] = found

    def forward(plane, order, act):
        parts = [
            (
                source[0, plane, q * count : (q + 1) * count, :],
                source[1, plane, q * count : (q + 1) * count, :],
            )
            for q in range(RADIX)
        ]
        for step, residue in enumerate(order):
            if plane == 0:
                loads[4 + 2 * step].wait()
                loads[5 + 2 * step].wait()
            mixed = combine(parts, [-residue * q for q in range(RADIX)])
            right = split(jnp.concatenate(mixed, axis=0))
            values = dot3((fwd_hi[residue], fwd_lo[residue]), right)
            for chunk in range(chunks):
                for part in range(2):
                    start = part * count + chunk * modes
                    spectra[residue, chunk, plane, part] = values[start : start + modes]
            act(step, residue)

    ends = jnp.where((team > 0) & (team < teams - 1), 0, 1)
    pl.semaphore_wait(barrier, RADIX + 1 - ends)
    for offset in range(1, RADIX):
        cond_copy(offset).start()
    loads[3].wait()

    def send_piece(step, residue):
        if step < RADIX // 2:
            in_piece(0, lax.rem(residue + RADIX - side, RADIX), 0).start()

    halves_of = [list(range(RADIX // 2)), list(range(RADIX // 2, RADIX))]

    @pl.when(side < RADIX // 2)
    def _():
        forward(0, halves_of[1] + halves_of[0], send_piece)

    @pl.when(side >= RADIX // 2)
    def _():
        forward(0, halves_of[0] + halves_of[1], send_piece)

    near = lax.rem(side + 1 - 2 * lax.rem(side, 2) + RADIX - side, RADIX)
    in_piece(0, near, 0).start()
    for plane in range(1, planes):
        loads[3 + 2 * RADIX + plane].wait()
        forward(plane, range(RADIX), lambda step, residue: None)
        for offset in (2, 3, 1):
            in_piece(0, offset, plane).start()

    for load in loads[3 + 2 * RADIX + planes : later]:
        load.wait()
    for load in loads[later:]:
        load.start()
    sine = jnp.concatenate([sine_hi[...], sine_hi[...], sine_lo[...]], axis=0)

    def sine_rows(values):
        flat = values.reshape(-1, length_y)
        return dot_wide(split(flat), sine).reshape(values.shape)

    def send_in(chunk, carry):
        spectra[:, chunk] = sine_rows(spectra[:, chunk])
        for offset in (2, 3, 1):
            in_copy(chunk, offset).start()
        return carry

    for offset in range(1, RADIX):
        cond_copy(offset).wait()
    total = jnp.zeros((1, length_y), jnp.float32)
    for index in range(RADIX):
        for plane in range(planes):
            row = cond_team[index, plane : plane + 1, :]
            cond[index * planes + plane + 1] = jnp.broadcast_to(row, (8, length_y))
            total = total + row
    edge_out[0:1] = total
    edge_out[1:2] = cond_team[0, 0:1, :]
    edge_out[2:3] = cond_team[RADIX - 1, planes - 1 : planes, :]

    @pl.when(team < teams - 1)
    def _():
        edge_copy(0).start()

    @pl.when(team > 0)
    def _():
        edge_copy(1).start()

    lax.fori_loop(1, chunks - 4, send_in, 0)


    @pl.when(team > 0)
    def _():
        edge_copy(0).wait_recv()
        cond[0] = jnp.broadcast_to(edge_in[0, 2:3, :], (8, length_y))

    @pl.when(team == 0)
    def _():
        cond[0] = cond[1]

    @pl.when(team < teams - 1)
    def _():
        edge_copy(1).wait_recv()
        cond[depth + 1] = jnp.broadcast_to(edge_in[1, 1:2, :], (8, length_y))

    @pl.when(team == teams - 1)
    def _():
        cond[depth + 1] = cond[depth]

    @pl.when(even)
    def _():
        half_out[0:1] = total + edge_in[1, 0:1, :]

    @pl.when(jnp.logical_not(even))
    def _():
        half_out[0:1] = total + edge_in[0, 0:1, :]

    @pl.when(inner)
    def _():
        half_copy(1).start()
        half_copy(0).start()

    shift_re = shift[0]
    shift_im = shift[1]
    row_lane = lax.broadcasted_iota(jnp.int32, (8, length_y), 1)
    last = length_y - 1

    lax.fori_loop(chunks - 4, chunks, send_in, 0)

    def keep(chunk, carry):
        forcing[chunk, rows(side)] = spectra[side, chunk]
        return carry

    lax.fori_loop(0, chunks, keep, 0)

    def make_faces(index, carry):
        here = cond[index + 1]
        right = jnp.where(row_lane == last, here, pltpu.roll(here, last, 1))
        left = jnp.where(row_lane == 0, here, pltpu.roll(here, 1, 1))
        face_yp = 0.5 * (here + right)
        face_ym = 0.5 * (here + left)
        face_zp = 0.5 * (here + cond[index + 2])
        face_zm = 0.5 * (here + cond[index])
        faces[index, 0] = here
        faces[index, 1] = face_yp + face_ym + face_zp + face_zm + shift_re
        faces[index, 2] = jnp.where(row_lane == last, 0.0, face_yp)
        faces[index, 3] = jnp.where(row_lane == 0, 0.0, face_ym)
        faces[index, 4] = face_zp
        faces[index, 5] = face_zm
        return carry

    lax.fori_loop(0, depth, make_faces, 0)
    def take(chunk):
        for offset in range(1, RADIX):
            in_copy(chunk, offset).wait()

    take(0)
    forcing[0] = sine_rows(forcing[0])
    half_copy(0).wait_recv()
    total = half_out[0:1, :] + half_in[0:1, :]
    mean_cond = jnp.sum(total) / (length_y * length_z)
    scale = relax / mean_cond
    offset_re = shift_re / mean_cond
    diag_im = shift_im / mean_cond
    none = jnp.zeros((modes, length_y), jnp.float32)
    one = jnp.ones((modes, length_y), jnp.float32)

    def eigen(chunk):
        return jnp.concatenate([mode_eig[chunk]] * (length_y // 128), axis=1)

    def factors(chunk):
        diag_re = eigen(chunk) + (eig_y[0:1, :] + offset_re)

        def factor(level, carry):
            gap_re = diag_re - carry[0]
            gap_im = diag_im - carry[1]
            inverse = 1.0 / (gap_re * gap_re + gap_im * gap_im)
            now = (gap_re * inverse, -gap_im * inverse)
            put(alpha, now, chunk, level)
            return now

        def segment(index, carry):
            def inner_level(level, state):
                now = factor(index * depth + level + 1, state[:2])
                return (*now, *times(now, state[2:]))

            state = lax.fori_loop(0, depth, inner_level, (*carry, one, none), unroll=True)
            put(lines, state[2:], chunk, index)
            return state[:2]

        put(alpha, (none, none), chunk, 0)
        lax.fori_loop(0, teams, segment, (none, none))

    given = (forcing, work)

    def launch(turn_id, chunk):
        def rise(index, carry):
            up = times(
                pair(alpha, chunk, first_level + index + 1),
                plus(pair(given[turn_id], chunk, index), carry[:2]),
            )
            down = times(
                pair(alpha, chunk, last_level + index + 1),
                plus(pair(given[turn_id], chunk, depth - 1 - index), carry[2:]),
            )
            return (*up, *down)

        ends = lax.fori_loop(0, depth, rise, (none, none, none, none), unroll=True)
        put(pair_out, choose(even, ends[:2], ends[2:]), turn_id, chunk)
        pair_copy(turn_id, chunk).start()
        put(rest_out, choose(even, ends[2:], ends[:2]), turn_id, chunk)

    def relay(turn_id, chunk):
        pair_copy(turn_id, chunk).wait_recv()

        @pl.when(inner)
        def _():
            more = times(pair(lines, chunk, 1), pair(pair_in, turn_id, chunk))
            put(comb_out, plus(pair(rest_out, turn_id, chunk), more), turn_id, chunk)
            comb_copy(turn_id, chunk, 1).start()
            comb_copy(turn_id, chunk, 0).start()

    def solve(turn_id, chunk):
        comb_copy(turn_id, chunk, 0).wait_recv()
        near = pair(pair_in, turn_id, chunk)
        wide = pair(comb_in, turn_id, chunk)
        joined = plus(near, times(pair(lines, chunk, teams - 2), wide))
        far = choose(inner, wide, joined)
        near = choose(inner, near, (none, none))
        below = choose(lower, near, far)
        above = choose(lower, far, near)

        def ahead(index, carry):
            factor = pair(alpha, chunk, first_level + index + 1)
            now = times(factor, plus(pair(given[turn_id], chunk, index), carry))
            put(work, now, chunk, index)
            return now

        reached = lax.fori_loop(0, depth, ahead, below, unroll=True)
        factor = pair(alpha, chunk, first_level + depth)
        edge = pair(alpha, chunk, last_level)
        echo = times(factor, edge)
        gap_re = 1.0 - echo[0]
        inverse = 1.0 / (gap_re * gap_re + echo[1] * echo[1])
        top = plus(reached, times(factor, above))
        top = times(top, (gap_re * inverse, echo[1] * inverse))
        outer = plus(above, times(edge, top))
        put(work, outer, chunk, depth + 1)

        def behind(step, carry):
            index = depth - 1 - step
            factor = pair(alpha, chunk, first_level + index + 1)
            now = plus(pair(work, chunk, index), times(factor, carry))
            put(work, now, chunk, index)
            return now

        bottom = lax.fori_loop(0, depth, behind, outer, unroll=True)
        put(work, plus(below, times(pair(alpha, chunk, first_level), bottom)), chunk, depth)

    def blocks(values):
        return values.reshape(modes // 8, 8, length_y)

    def operator(chunk):
        eig = blocks(eigen(chunk))

        def run(index, carry):
            center = faces[index, 0] * eig + faces[index, 1]
            values = pair(field, chunk, index + 1)
            turned = (-shift_im * values[1], shift_im * values[0])
            above = pair(field, chunk, index + 2)
            below = pair(field, chunk, index)
            for part in range(2):
                value = values[part]
                applied = center * blocks(value) + blocks(turned[part])
                applied = applied - faces[index, 2] * blocks(pltpu.roll(value, last, 1))
                applied = applied - faces[index, 3] * blocks(pltpu.roll(value, 1, 1))
                applied = applied - faces[index, 4] * blocks(above[part])
                applied = applied - faces[index, 5] * blocks(below[part])
                work[chunk, index, part] = applied.reshape(modes, length_y)
            return carry

        lax.fori_loop(0, depth, run, 0, unroll=8)

    squares[0] = none
    squares[1] = none
    factors(0)

    def begin(chunk):
        @pl.when(chunk > 0)
        def _():
            take(chunk)

        launch(0, chunk)

    def middle(chunk):
        solve(0, chunk)
        values = sine_rows(work[chunk]) * scale
        field[chunk, pl.ds(1, depth)] = values[:depth]
        field[chunk, 0] = values[depth]
        field[chunk, depth + 1] = values[depth + 1]
        operator(chunk)
        here = forcing[chunk]
        rest = here - sine_rows(work[chunk, pl.ds(0, depth)])
        work[chunk, pl.ds(0, depth)] = rest
        launch(1, chunk)
        squares[0] = squares[0] + jnp.sum(here * here, axis=(0, 1))
        squares[1] = squares[1] + jnp.sum(rest * rest, axis=(0, 1))

        @pl.when(chunk == chunks - 1)
        def _():
            row = lax.broadcasted_iota(jnp.int32, (ITERS, 128), 0)
            both = jnp.where(row == 0, jnp.sum(squares[0]), jnp.sum(squares[1]))
            sum_own[...] = both / length_x

            @each_peer
            def _(offset):
                sum_copy(offset).start()

            pltpu.make_async_copy(sum_own, sums.at[me], own_sem.at[chunks]).start()

    def finish(chunk):
        solve(1, chunk)
        values = sine_rows(work[chunk, pl.ds(0, depth)]) * scale
        result[chunk] = field[chunk, pl.ds(1, depth)] + values

        def put_out(which):
            for offset in (2, 3, 1):
                out_copy(which, offset).start()
            own_copy(which).start()

        @pl.when(chunk < chunks - 1)
        def _():
            put_out(chunk)

        @pl.when(chunk == chunks - 1)
        def _():
            put_out(None)

    def ready(chunk):
        @pl.when(chunk + 1 < chunks)
        def _():
            factors(chunk + 1)

    stages = {
        "begin": (0, begin),
        "ready": (0, ready),
        "relay": (LAGS[0], functools.partial(relay, 0)),
        "middle": (LAGS[1], middle),
        "again": (LAGS[2], functools.partial(relay, 1)),
        "finish": (LAGS[3], finish),
    }

    def step(index, carry):
        for name in ORDER:
            lag, act = stages[name]

            @pl.when((index >= lag) & (index < chunks + lag))
            def _():
                act(index - lag)

        return carry

    lax.fori_loop(0, chunks + LAGS[3], step, 0)

    def settle(chunk, carry):
        for turn_id in range(2):
            pair_copy(turn_id, chunk).wait_send()

            @pl.when(inner)
            def _():
                comb_copy(turn_id, chunk, 0).wait_send()
                comb_copy(turn_id, chunk, 1).wait_send()

        return carry

    def arrive(chunk, carry):
        own_copy(chunk).wait()
        for offset in range(1, RADIX):
            out_copy(chunk, offset).wait()
        return carry

    for load in loads[later:]:
        load.wait()
    lax.fori_loop(0, chunks - 1, arrive, 0)

    def gather(plane, carry):
        for residue in range(RADIX):
            blocks = []
            for part in range(2):
                blocks += [slabs[residue, chunk, plane, part] for chunk in range(chunks - 1)]
                blocks += [none]
            right = split(jnp.concatenate(blocks, axis=0))
            partial[plane, residue] = dot3((bwd_hi[residue], bwd_lo[residue]), right)
        return carry

    lax.fori_loop(0, planes, gather, 0)

    pltpu.make_async_copy(sum_own, sums.at[me], own_sem.at[chunks]).wait()

    @pl.when(team < teams - 1)
    def _():
        edge_copy(0).wait_send()

    @pl.when(team > 0)
    def _():
        edge_copy(1).wait_send()

    @pl.when(inner)
    def _():
        half_copy(0).wait_send()
        half_copy(1).wait_send()

    @each_peer
    def _(offset):
        sum_copy(offset).wait()

    lax.fori_loop(0, chunks, settle, 0)
    arrive(None, 0)


def ending(cells, partial, tail, sums, table, out, norms, stage, out_sem):
    planes, _, twice, length_y = partial.shape
    count = twice // 2
    modes = tail.shape[3]

    def store(plane, q):
        return pltpu.make_async_copy(
            stage.at[:, plane, pl.ds(q * count, count), :],
            out.at[:, plane, pl.ds(q * count, count), :],
            out_sem.at[plane, q],
        )

    for plane in range(planes):
        parts = []
        for residue in range(RADIX):
            high, low = split(tail[residue, plane].reshape(2 * modes, length_y))
            right = jnp.concatenate([high, low, high], axis=0)
            more = jnp.dot(table[residue], right, preferred_element_type=jnp.float32)
            values = partial[plane, residue] + more
            parts.append((values[:count], values[count:]))
        for q in range(RADIX):
            re, im = combine(parts, [residue * q for residue in range(RADIX)])
            stage[0, plane, q * count : (q + 1) * count, :] = re
            stage[1, plane, q * count : (q + 1) * count, :] = im
            store(plane, q).start()
    root = jnp.sqrt(jnp.sum(sums[...], axis=0) / cells)
    for index in range(ITERS):
        norms[index] = root[index, 0]
    for plane in range(planes):
        for q in range(RADIX):
            store(plane, q).wait()


CHUNKS = 8
LAGS = (1, 2, 3, 5)
ORDER = ("begin", "relay", "finish", "middle", "ready", "again")


def body(source, layer_ids, conduct_table, shift):
    planes = source.shape[1]
    length_x = source.shape[2]
    length_y = source.shape[3]
    groups = lax.axis_size("gz")
    length_z = planes * groups
    count = length_x // RADIX
    modes = count // CHUNKS
    if groups != 4 * RADIX or modes % 8 or planes > 8 or length_z > 64 or length_y % 128:
        return body_plain(source, layer_ids, conduct_table, shift)
    depth = planes * RADIX
    layers = conduct_table.shape[0]
    mode_ids = RADIX * np.arange(count)[None, :] + np.arange(RADIX)[:, None]
    mode_eig = (2.0 - 2.0 * np.cos(2.0 * np.pi / length_x * mode_ids)).astype(np.float32)
    mode_eig = np.broadcast_to(mode_eig[:, :, None], (RADIX, count, 128))
    mode_eig = np.ascontiguousarray(mode_eig).reshape(RADIX, CHUNKS, modes, 128)
    eig_y = 4.0 - 2.0 * np.cos(np.pi / (length_y + 1) * (np.arange(length_y) + 1.0))
    eig_y = np.ascontiguousarray(np.broadcast_to(eig_y.astype(np.float32), (8, length_y)))
    forward, backward = radix_tables(length_x)
    tables = [*halves(forward), *halves(sine_host(length_y)), *halves(backward)]
    final = np.concatenate([part * count + np.arange(count - modes, count) for part in range(2)])
    final = backward[:, :, final]
    high = final.astype(jnp.bfloat16)
    low = (final - high.astype(np.float32)).astype(jnp.bfloat16)
    final = jnp.asarray(np.concatenate([high, high, low], axis=2))
    tile = (2, modes, length_y)
    smem = pl.BlockSpec(memory_space=pltpu.SMEM)
    hbm = pl.BlockSpec(memory_space=pl.ANY)
    vmem = pl.BlockSpec(memory_space=pltpu.VMEM)
    f32 = jnp.float32
    dma = pltpu.SemaphoreType.DMA
    in_hbm = functools.partial(pltpu.with_memory_space_constraint, memory_space=pltpu.HBM)
    partial, tail, sums = pl.pallas_call(
        functools.partial(kernel, groups, planes, CHUNKS, layers),
        out_shape=(
            pltpu.VMEM((planes, RADIX, 2 * count, length_y), f32),
            pltpu.VMEM((RADIX, planes, *tile), f32),
            pltpu.VMEM((groups, ITERS, 128), f32),
        ),
        in_specs=[hbm] * 12,
        out_specs=(vmem, hbm, hbm),
        scratch_shapes=[
            pltpu.VMEM(source.shape, f32),
            pltpu.VMEM(layer_ids.shape, jnp.int32),
            pltpu.SMEM(conduct_table.shape, f32),
            pltpu.SMEM(shift.shape, f32),
            pltpu.VMEM((CHUNKS, modes, 128), f32),
            pltpu.VMEM((8, length_y), f32),
        ]
        + [pltpu.VMEM(table.shape, jnp.bfloat16) for table in tables]
        + [
            pltpu.VMEM((RADIX, CHUNKS - 1, planes, *tile), f32),
            pltpu.VMEM((RADIX, CHUNKS, planes, *tile), f32),
            pltpu.VMEM((CHUNKS, depth, *tile), f32),
            pltpu.VMEM((planes, length_y), f32),
            pltpu.VMEM((RADIX, planes, length_y), f32),
            pltpu.VMEM((depth + 2, 8, length_y), f32),
            pltpu.VMEM((4, length_y), f32),
            pltpu.VMEM((2, 4, length_y), f32),
            pltpu.VMEM((4, length_y), f32),
            pltpu.VMEM((4, length_y), f32),
            pltpu.VMEM((depth, 6, 8, length_y), f32),
            pltpu.VMEM((CHUNKS, depth + 2, *tile), f32),
            pltpu.VMEM((CHUNKS, length_z + 1, *tile), f32),
            pltpu.VMEM((CHUNKS, groups // RADIX, *tile), f32),
            pltpu.VMEM((CHUNKS, depth + 2, *tile), f32),
            pltpu.VMEM((CHUNKS, depth, *tile), f32),
            pltpu.VMEM((ITERS, 128), f32),
            pltpu.VMEM(tile, f32),
        ]
        + [pltpu.VMEM((ITERS, CHUNKS, *tile), f32)] * 5
        + [dma((9 + 2 * RADIX + planes,))]
        + [dma((CHUNKS, RADIX))] * 2
        + [dma((RADIX,))] * 2
        + [dma((2,))] * 2
        + [dma((2,)), dma((1,))]
        + [dma((CHUNKS, RADIX))] * 2
        + [dma((groups,))] * 2
        + [dma((CHUNKS + 1,))]
        + [dma((ITERS, CHUNKS))] * 2
        + [dma((ITERS, CHUNKS, 2)), dma((ITERS, CHUNKS))],
        compiler_params=pltpu.CompilerParams(
            collective_id=0, has_side_effects=True, vmem_limit_bytes=50 << 20
        ),
    )(
        in_hbm(source),
        in_hbm(layer_ids),
        in_hbm(conduct_table),
        in_hbm(shift),
        *[in_hbm(jnp.asarray(table)) for table in (mode_eig, eig_y, *tables)],
    )
    cells = length_x * length_y * length_z
    return pl.pallas_call(
        functools.partial(ending, cells),
        out_shape=(
            jax.ShapeDtypeStruct(source.shape, f32),
            jax.ShapeDtypeStruct((ITERS,), f32),
        ),
        in_specs=[vmem] * 4,
        out_specs=(hbm, smem),
        scratch_shapes=[pltpu.VMEM(source.shape, f32), dma((planes, RADIX))],
        compiler_params=pltpu.CompilerParams(vmem_limit_bytes=20 << 20),
    )(partial, tail, sums, final)


def solution(mesh):
    placed = (P(None, ("node", "gz"), None, None), P(("node", "gz"), None), P(), P("node"))
    return jax.shard_map(
        body,
        mesh=mesh,
        in_specs=placed,
        out_specs=(P(None, ("node", "gz"), None, None), P("node")),
        check_vma=False,
    )
```

```python
import functools

import jax
import jax.numpy as jnp
import numpy as np
from jax import lax
from jax.experimental import pallas as pl
from jax.experimental.pallas import tpu as pltpu
from jax.sharding import PartitionSpec as P

ITERS = 2


relax = 0.6
highest = lax.Precision.HIGH


def with_halo(cells, sides, width):
    for axis, dim in sides:
        count = lax.axis_size(axis)
        ends = count - 1
        head = lax.slice_in_dim(cells, 0, width, axis=dim)
        tail = lax.slice_in_dim(cells, cells.shape[dim] - width, cells.shape[dim], axis=dim)
        cells = jnp.concatenate(
            [
                lax.ppermute(tail, axis, [(i, (i + 1) % count) for i in range(ends)]),
                cells,
                lax.ppermute(head, axis, [((i + 1) % count, i) for i in range(ends)]),
            ],
            axis=dim,
        )
    return cells


def sine_table(length):
    indices = lax.iota(jnp.int32, length) + 1
    product = indices[:, None] * indices[None, :] % (2 * (length + 1))
    return jnp.sqrt(2.0 / (length + 1)) * jnp.sin(
        jnp.pi / (length + 1) * product.astype(jnp.float32)
    )


def sine_eigen(length):
    indices = lax.iota(jnp.float32, length) + 1.0
    return 2.0 - 2.0 * jnp.cos(jnp.pi / (length + 1) * indices)


def dft_tables(length):
    indices = lax.iota(jnp.int32, length)
    product = indices[:, None] * indices[None, :] % length
    angles = 2.0 * jnp.pi / length * product.astype(jnp.float32)
    return (jnp.cos(angles), jnp.sin(angles))


def transform(field, cos_t, sin_t, inverse):

    def project(component, matrix):
        return jnp.einsum("zxy,xk->zky", component, matrix, precision=highest)

    re_cos = project(field[0], cos_t)
    re_sin = project(field[0], sin_t)
    im_cos = project(field[1], cos_t)
    im_sin = project(field[1], sin_t)
    if inverse:
        return jnp.stack([re_cos - im_sin, im_cos + re_sin]) / cos_t.shape[0]
    return jnp.stack([re_cos + im_sin, im_cos - re_sin])


def expand(weights):
    return weights[None, :, None, :]


def yz_part(field, upper, lower, conduct, cond_hi, cond_lo):
    cond_pad = jnp.pad(conduct, ((0, 0), (1, 1)), mode="edge")
    face_yp = 0.5 * (conduct + cond_pad[:, 2:])
    face_ym = 0.5 * (conduct + cond_pad[:, :-2])
    face_zp = 0.5 * (conduct + cond_hi)
    face_zm = 0.5 * (conduct + cond_lo)
    field_pad = jnp.pad(field, ((0, 0), (0, 0), (0, 0), (1, 1)))
    total = expand(face_yp) * (field - field_pad[..., 2:]) + expand(face_ym) * (
        field - field_pad[..., :-2]
    )
    return total + expand(face_zp) * (field - upper) + expand(face_zm) * (field - lower)


def shift_mult(shift_re, shift_im, field):
    return jnp.stack(
        [shift_re * field[0] - shift_im * field[1], shift_re * field[1] + shift_im * field[0]]
    )


def sine_both(field, sine_y, sine_z):
    field = jnp.einsum("pzxy,yj->pzxj", field, sine_y, precision=highest)
    return jnp.einsum("pzxy,zk->pkxy", field, sine_z, precision=highest)


def precondition(coeffs, mode_eig, mean_cond, shift_re, shift_im, sine_y, sine_z, eig_y, eig_z):
    coeffs = sine_both(coeffs, sine_y, sine_z)
    eigen = eig_z[:, None, None] + mode_eig[None, :, None] + eig_y[None, None, :]
    real_den = shift_re + mean_cond * eigen
    inv = 1.0 / (real_den * real_den + shift_im * shift_im)
    scaled = jnp.stack(
        [
            (coeffs[0] * real_den + coeffs[1] * shift_im) * inv,
            (coeffs[1] * real_den - coeffs[0] * shift_im) * inv,
        ]
    )
    return sine_both(scaled, sine_y, sine_z)


def body_plain(source, layer_ids, conduct_table, shift):
    shift_re = shift[0]
    shift_im = shift[1]
    planes = source.shape[1]
    length_x = source.shape[2]
    length_y = source.shape[3]
    groups = lax.axis_size("gz")
    length_z = planes * groups
    modes = length_x // groups
    first_mode = lax.axis_index("gz") * modes
    layers = conduct_table.shape[0]
    onehot = layer_ids[:, :, None] == lax.iota(jnp.int32, layers)[None, None, :]
    local = jnp.sum(jnp.where(onehot, conduct_table[None, None, :], 0.0), axis=-1)
    conduct = lax.all_gather(local, "gz", axis=0, tiled=True)
    mean_cond = jnp.sum(conduct) / (length_y * length_z)
    cond_z = jnp.pad(conduct, ((1, 1), (0, 0)), mode="edge")
    cos_t, sin_t = dft_tables(length_x)
    sine_y = sine_table(length_y)
    sine_z = sine_table(length_z)
    eig_y = sine_eigen(length_y)
    eig_z = sine_eigen(length_z)
    mode_ids = (first_mode + lax.iota(jnp.int32, modes)).astype(jnp.float32)
    mode_eig = 2.0 - 2.0 * jnp.cos(2.0 * jnp.pi / length_x * mode_ids)
    cells = length_x * length_y * length_z
    spectra = transform(source, cos_t, sin_t, False)
    forcing = lax.all_to_all(spectra, "gz", split_axis=2, concat_axis=1, tiled=True)
    partials = []
    solution = jnp.zeros_like(forcing)
    for iteration in range(ITERS):
        if iteration == 0:
            resid = forcing
        else:
            padded = jnp.pad(solution, ((0, 0), (1, 1), (0, 0), (0, 0)))
            lap = expand(conduct) * mode_eig[None, None, :, None] * solution
            lap = lap + yz_part(
                solution, padded[:, 2:], padded[:, :-2], conduct, cond_z[2:], cond_z[:-2]
            )
            resid = forcing - (shift_mult(shift_re, shift_im, solution) + lap)
        partials.append(jnp.sum(resid * resid) / length_x)
        update = precondition(
            resid, mode_eig, mean_cond, shift_re, shift_im, sine_y, sine_z, eig_y, eig_z
        )
        solution = solution + relax * update
    slabs = lax.all_to_all(solution, "gz", split_axis=1, concat_axis=2, tiled=True)
    result = transform(slabs, cos_t, sin_t, True)
    sums = jnp.sum(lax.all_gather(jnp.stack(partials)[None, :], "gz", axis=0, tiled=True), axis=0)
    return (result, jnp.sqrt(sums / cells))


RADIX = 4


def halves(table):
    high = table.astype(jnp.bfloat16)
    low = (table - high.astype(np.float32)).astype(jnp.bfloat16)
    return (jnp.asarray(high), jnp.asarray(low))


def radix_tables(length_x):
    count = length_x // RADIX
    pos = np.arange(count)
    forward = []
    for residue in range(RADIX):
        modes = RADIX * pos + residue
        angle = 2.0 * np.pi / length_x * (modes[:, None] * pos[None, :] % length_x)
        cos_t, sin_t = np.cos(angle), np.sin(angle)
        forward.append(np.block([[cos_t, sin_t], [-sin_t, cos_t]]))
    forward = np.stack(forward)
    backward = np.swapaxes(forward, 1, 2) / length_x
    return (forward.astype(np.float32), backward.astype(np.float32))


def sine_host(length):
    indices = np.arange(length) + 1
    product = indices[:, None] * indices[None, :] % (2 * (length + 1))
    return (np.sqrt(2.0 / (length + 1)) * np.sin(np.pi / (length + 1) * product)).astype(np.float32)


def split(values):
    high = values.astype(jnp.bfloat16)
    return (high, (values - high.astype(jnp.float32)).astype(jnp.bfloat16))


def dot3(left, right):
    mul = functools.partial(jnp.dot, preferred_element_type=jnp.float32)
    return mul(left[0], right[0]) + (mul(left[0], right[1]) + mul(left[1], right[0]))


def dot_wide(left, right):
    wide = jnp.concatenate([left[0], left[1], left[0]], axis=1)
    return jnp.dot(wide, right, preferred_element_type=jnp.float32)


def turn(re, im, quarter):
    quarter = quarter % 4
    return [(re, im), (-im, re), (-re, -im), (im, -re)][quarter]


def combine(parts, quarters):
    re, im = turn(*parts[0], quarters[0])
    for part, quarter in zip(parts[1:], quarters[1:]):
        more_re, more_im = turn(*part, quarter)
        re, im = re + more_re, im + more_im
    return (re, im)


def times(left, right):
    return (left[0] * right[0] - left[1] * right[1], left[0] * right[1] + left[1] * right[0])


def plus(left, right):
    return (left[0] + right[0], left[1] + right[1])


def pair(ref, *index):
    return (ref[(*index, 0)], ref[(*index, 1)])


def put(ref, values, *index):
    ref[(*index, 0)] = values[0]
    ref[(*index, 1)] = values[1]


def choose(test, left, right):
    return (jnp.where(test, left[0], right[0]), jnp.where(test, left[1], right[1]))


def kernel(
    groups,
    planes,
    chunks,
    layers,
    source_hbm,
    ids_hbm,
    table_hbm,
    shift_hbm,
    mode_hbm,
    eig_hbm,
    fwd_hi_hbm,
    fwd_lo_hbm,
    sine_hi_hbm,
    sine_lo_hbm,
    bwd_hi_hbm,
    bwd_lo_hbm,
    partial,
    tail,
    sums,
    source,
    ids,
    table,
    shift,
    mode_eig,
    eig_y,
    fwd_hi,
    fwd_lo,
    sine_hi,
    sine_lo,
    bwd_hi,
    bwd_lo,
    slabs,
    spectra,
    forcing,
    cond_own,
    cond_team,
    cond,
    edge_out,
    edge_in,
    half_out,
    half_in,
    faces,
    work,
    alpha,
    lines,
    field,
    result,
    sum_own,
    squares,
    pair_out,
    pair_in,
    rest_out,
    comb_out,
    comb_in,
    load_sem,
    in_send,
    in_recv,
    cond_send,
    cond_recv,
    edge_send,
    edge_recv,
    half_send,
    half_recv,
    out_send,
    out_recv,
    sum_send,
    sum_recv,
    own_sem,
    pair_send,
    pair_recv,
    comb_send,
    comb_recv,
):
    me = lax.axis_index("gz")
    side = lax.rem(me, RADIX)
    team = me // RADIX
    teams = groups // RADIX
    length_x = source.shape[2]
    length_y = source.shape[3]
    length_z = groups * planes
    depth = RADIX * planes
    count = length_x // RADIX
    modes = count // chunks
    first_level = team * depth
    last_level = length_z - first_level - depth

    pieces = [(ids_hbm, ids), (table_hbm, table), (shift_hbm, shift)]
    pieces += [(source_hbm.at[:, 0], source.at[:, 0])]
    across = jnp.where(side < RADIX // 2, RADIX // 2, 0)
    for step in range(RADIX):
        residue = lax.rem(across + step, RADIX)
        pieces += [(fwd_hi_hbm.at[residue], fwd_hi.at[residue])]
        pieces += [(fwd_lo_hbm.at[residue], fwd_lo.at[residue])]
    pieces += [(source_hbm.at[:, plane], source.at[:, plane]) for plane in range(1, planes)]
    pieces += [(sine_hi_hbm, sine_hi), (sine_lo_hbm, sine_lo)]
    pieces += [(mode_hbm.at[side], mode_eig), (eig_hbm, eig_y)]
    later = len(pieces)
    pieces += [(bwd_hi_hbm, bwd_hi), (bwd_lo_hbm, bwd_lo)]
    loads = [
        pltpu.make_async_copy(src, dst, load_sem.at[index])
        for index, (src, dst) in enumerate(pieces)
    ]
    first = 4 + RADIX
    for load in loads[:first]:
        load.start()

    def remote(src, dst, send, recv, target):
        return pltpu.make_async_remote_copy(
            src_ref=src,
            dst_ref=dst,
            send_sem=send,
            recv_sem=recv,
            device_id={"gz": target},
            device_id_type=pl.DeviceIdType.MESH,
        )

    def peer(offset):
        return lax.rem(me + offset, groups)

    def mate(offset):
        return lax.rem(side + offset, RADIX)

    def rows(index):
        return pl.ds(index * planes, planes)

    def cond_copy(offset):
        return remote(
            cond_own,
            cond_team.at[side],
            cond_send.at[offset],
            cond_recv.at[offset],
            team * RADIX + mate(offset),
        )

    def edge_copy(which):
        return remote(
            edge_out,
            edge_in.at[which],
            edge_send.at[which],
            edge_recv.at[which],
            me + [RADIX, -RADIX][which],
        )

    def half_copy(which):
        target = [teams - 1 - team, (teams - 1) * (2 - team)][which]
        return remote(
            half_out, half_in, half_send.at[which], half_recv.at[0], target * RADIX + side
        )

    def sum_copy(offset):
        return remote(
            sum_own, sums.at[me], sum_send.at[offset], sum_recv.at[offset], peer(offset)
        )

    def in_piece(chunk, offset, plane):
        target = mate(offset)
        return remote(
            spectra.at[target, chunk, pl.ds(plane, 1)],
            forcing.at[chunk, pl.ds(side * planes + plane, 1)],
            in_send.at[chunk, offset],
            in_recv.at[chunk, offset],
            team * RADIX + target,
        )

    def in_copy(chunk, offset):
        target = mate(offset)
        return remote(
            spectra.at[target, chunk],
            forcing.at[chunk, rows(side)],
            in_send.at[chunk, offset],
            in_recv.at[chunk, offset],
            team * RADIX + target,
        )

    def landing(chunk):
        return tail.at[side] if chunk is None else slabs.at[side, chunk]

    def out_copy(chunk, offset):
        target = mate(offset)
        index = chunks - 1 if chunk is None else chunk
        return remote(
            result.at[index, rows(target)],
            landing(chunk),
            out_send.at[index, offset],
            out_recv.at[index, offset],
            team * RADIX + target,
        )

    def own_copy(chunk):
        index = chunks - 1 if chunk is None else chunk
        return pltpu.make_async_copy(
            result.at[index, rows(side)], landing(chunk), own_sem.at[index]
        )

    even = lax.rem(team, 2) == 0
    inner = (team == 1) | (team == 2)
    lower = team < 2
    partner = team + 1 - 2 * lax.rem(team, 2)

    def pair_copy(turn_id, chunk):
        return remote(
            pair_out.at[turn_id, chunk],
            pair_in.at[turn_id, chunk],
            pair_send.at[turn_id, chunk],
            pair_recv.at[turn_id, chunk],
            partner * RADIX + side,
        )

    def comb_copy(turn_id, chunk, which):
        target = [teams - 1 - team, (teams - 1) * (2 - team)][which]
        return remote(
            comb_out.at[turn_id, chunk],
            comb_in.at[turn_id, chunk],
            comb_send.at[turn_id, chunk, which],
            comb_recv.at[turn_id, chunk],
            target * RADIX + side,
        )

    def each_peer(act):
        def run(offset, carry):
            act(offset)
            return carry

        lax.fori_loop(1, groups, run, 0)

    barrier = pltpu.get_barrier_semaphore()

    def greet(target):
        pl.semaphore_signal(
            barrier, inc=1, device_id={"gz": target}, device_id_type=pl.DeviceIdType.MESH
        )

    for offset in range(1, RADIX):
        greet(team * RADIX + mate(offset))

    @pl.when(team > 0)
    def _():
        greet(me - RADIX)

    @pl.when(team < teams - 1)
    def _():
        greet(me + RADIX)

    for load in loads[:3]:
        load.wait()
    for load in loads[first:later]:
        load.start()
    found = jnp.zeros((planes, length_y), jnp.float32)
    for layer in range(layers):
        found = found + jnp.where(ids[...] == layer, table[layer], 0.0)
    cond_own[...] = found
    cond_team[side] = found

    def forward(plane, order, act):
        parts = [
            (
                source[0, plane, q * count : (q + 1) * count, :],
                source[1, plane, q * count : (q + 1) * count, :],
            )
            for q in range(RADIX)
        ]
        for step, residue in enumerate(order):
            if plane == 0:
                loads[4 + 2 * step].wait()
                loads[5 + 2 * step].wait()
            mixed = combine(parts, [-residue * q for q in range(RADIX)])
            right = split(jnp.concatenate(mixed, axis=0))
            values = dot3((fwd_hi[residue], fwd_lo[residue]), right)
            for chunk in range(chunks):
                for part in range(2):
                    start = part * count + chunk * modes
                    spectra[residue, chunk, plane, part] = values[start : start + modes]
            act(step, residue)

    ends = jnp.where((team > 0) & (team < teams - 1), 0, 1)
    pl.semaphore_wait(barrier, RADIX + 1 - ends)
    for offset in range(1, RADIX):
        cond_copy(offset).start()
    loads[3].wait()

    def send_piece(step, residue):
        if step < RADIX // 2:
            in_piece(0, lax.rem(residue + RADIX - side, RADIX), 0).start()

    halves_of = [list(range(RADIX // 2)), list(range(RADIX // 2, RADIX))]

    @pl.when(side < RADIX // 2)
    def _():
        forward(0, halves_of[1] + halves_of[0], send_piece)

    @pl.when(side >= RADIX // 2)
    def _():
        forward(0, halves_of[0] + halves_of[1], send_piece)

    near = lax.rem(side + 1 - 2 * lax.rem(side, 2) + RADIX - side, RADIX)
    in_piece(0, near, 0).start()
    for plane in range(1, planes):
        loads[3 + 2 * RADIX + plane].wait()
        forward(plane, range(RADIX), lambda step, residue: None)
        for offset in (2, 3, 1):
            in_piece(0, offset, plane).start()

    for load in loads[3 + 2 * RADIX + planes : later]:
        load.wait()
    for load in loads[later:]:
        load.start()
    sine = jnp.concatenate([sine_hi[...], sine_hi[...], sine_lo[...]], axis=0)

    def sine_rows(values):
        flat = values.reshape(-1, length_y)
        return dot_wide(split(flat), sine).reshape(values.shape)

    def send_in(chunk, carry):
        spectra[:, chunk] = sine_rows(spectra[:, chunk])
        for offset in (2, 3, 1):
            in_copy(chunk, offset).start()
        return carry

    for offset in range(1, RADIX):
        cond_copy(offset).wait()
    total = jnp.zeros((1, length_y), jnp.float32)
    for index in range(RADIX):
        for plane in range(planes):
            row = cond_team[index, plane : plane + 1, :]
            cond[index * planes + plane + 1] = jnp.broadcast_to(row, (8, length_y))
            total = total + row
    edge_out[0:1] = total
    edge_out[1:2] = cond_team[0, 0:1, :]
    edge_out[2:3] = cond_team[RADIX - 1, planes - 1 : planes, :]

    @pl.when(team < teams - 1)
    def _():
        edge_copy(0).start()

    @pl.when(team > 0)
    def _():
        edge_copy(1).start()

    lax.fori_loop(1, chunks - 4, send_in, 0)


    @pl.when(team > 0)
    def _():
        edge_copy(0).wait_recv()
        cond[0] = jnp.broadcast_to(edge_in[0, 2:3, :], (8, length_y))

    @pl.when(team == 0)
    def _():
        cond[0] = cond[1]

    @pl.when(team < teams - 1)
    def _():
        edge_copy(1).wait_recv()
        cond[depth + 1] = jnp.broadcast_to(edge_in[1, 1:2, :], (8, length_y))

    @pl.when(team == teams - 1)
    def _():
        cond[depth + 1] = cond[depth]

    @pl.when(even)
    def _():
        half_out[0:1] = total + edge_in[1, 0:1, :]

    @pl.when(jnp.logical_not(even))
    def _():
        half_out[0:1] = total + edge_in[0, 0:1, :]

    @pl.when(inner)
    def _():
        half_copy(1).start()
        half_copy(0).start()

    shift_re = shift[0]
    shift_im = shift[1]
    row_lane = lax.broadcasted_iota(jnp.int32, (8, length_y), 1)
    last = length_y - 1

    lax.fori_loop(chunks - 4, chunks, send_in, 0)

    def keep(chunk, carry):
        forcing[chunk, rows(side)] = spectra[side, chunk]
        return carry

    lax.fori_loop(0, chunks, keep, 0)

    def make_faces(index, carry):
        here = cond[index + 1]
        right = jnp.where(row_lane == last, here, pltpu.roll(here, last, 1))
        left = jnp.where(row_lane == 0, here, pltpu.roll(here, 1, 1))
        face_yp = 0.5 * (here + right)
        face_ym = 0.5 * (here + left)
        face_zp = 0.5 * (here + cond[index + 2])
        face_zm = 0.5 * (here + cond[index])
        faces[index, 0] = here
        faces[index, 1] = face_yp + face_ym + face_zp + face_zm + shift_re
        faces[index, 2] = jnp.where(row_lane == last, 0.0, face_yp)
        faces[index, 3] = jnp.where(row_lane == 0, 0.0, face_ym)
        faces[index, 4] = face_zp
        faces[index, 5] = face_zm
        return carry

    lax.fori_loop(0, depth, make_faces, 0)
    def take(chunk):
        for offset in range(1, RADIX):
            in_copy(chunk, offset).wait()

    take(0)
    forcing[0] = sine_rows(forcing[0])
    half_copy(0).wait_recv()
    total = half_out[0:1, :] + half_in[0:1, :]
    mean_cond = jnp.sum(total) / (length_y * length_z)
    scale = relax / mean_cond
    offset_re = shift_re / mean_cond
    diag_im = shift_im / mean_cond
    none = jnp.zeros((modes, length_y), jnp.float32)
    one = jnp.ones((modes, length_y), jnp.float32)

    def eigen(chunk):
        return jnp.concatenate([mode_eig[chunk]] * (length_y // 128), axis=1)

    def factors(chunk):
        diag_re = eigen(chunk) + (eig_y[0:1, :] + offset_re)

        def factor(level, carry):
            gap_re = diag_re - carry[0]
            gap_im = diag_im - carry[1]
            inverse = 1.0 / (gap_re * gap_re + gap_im * gap_im)
            now = (gap_re * inverse, -gap_im * inverse)
            put(alpha, now, chunk, level)
            return now

        def segment(index, carry):
            def inner_level(level, state):
                now = factor(index * depth + level + 1, state[:2])
                return (*now, *times(now, state[2:]))

            state = lax.fori_loop(0, depth, inner_level, (*carry, one, none), unroll=True)
            put(lines, state[2:], chunk, index)
            return state[:2]

        put(alpha, (none, none), chunk, 0)
        lax.fori_loop(0, teams, segment, (none, none))

    given = (forcing, work)

    def launch(turn_id, chunk):
        def rise(index, carry):
            up = times(
                pair(alpha, chunk, first_level + index + 1),
                plus(pair(given[turn_id], chunk, index), carry[:2]),
            )
            down = times(
                pair(alpha, chunk, last_level + index + 1),
                plus(pair(given[turn_id], chunk, depth - 1 - index), carry[2:]),
            )
            return (*up, *down)

        ends = lax.fori_loop(0, depth, rise, (none, none, none, none), unroll=True)
        put(pair_out, choose(even, ends[:2], ends[2:]), turn_id, chunk)
        pair_copy(turn_id, chunk).start()
        put(rest_out, choose(even, ends[2:], ends[:2]), turn_id, chunk)

    def relay(turn_id, chunk):
        @pl.when(inner)
        def _():
            pair_copy(turn_id, chunk).wait_recv()
            more = times(pair(lines, chunk, 1), pair(pair_in, turn_id, chunk))
            put(comb_out, plus(pair(rest_out, turn_id, chunk), more), turn_id, chunk)
            comb_copy(turn_id, chunk, 1).start()
            comb_copy(turn_id, chunk, 0).start()

    def solve(turn_id, chunk):
        @pl.when(jnp.logical_not(inner))
        def _():
            pair_copy(turn_id, chunk).wait_recv()

        comb_copy(turn_id, chunk, 0).wait_recv()
        near = pair(pair_in, turn_id, chunk)
        wide = pair(comb_in, turn_id, chunk)
        joined = plus(near, times(pair(lines, chunk, teams - 2), wide))
        far = choose(inner, wide, joined)
        near = choose(inner, near, (none, none))
        below = choose(lower, near, far)
        above = choose(lower, far, near)

        def ahead(index, carry):
            factor = pair(alpha, chunk, first_level + index + 1)
            now = times(factor, plus(pair(given[turn_id], chunk, index), carry))
            put(work, now, chunk, index)
            return now

        reached = lax.fori_loop(0, depth, ahead, below, unroll=True)
        factor = pair(alpha, chunk, first_level + depth)
        edge = pair(alpha, chunk, last_level)
        echo = times(factor, edge)
        gap_re = 1.0 - echo[0]
        inverse = 1.0 / (gap_re * gap_re + echo[1] * echo[1])
        top = plus(reached, times(factor, above))
        top = times(top, (gap_re * inverse, echo[1] * inverse))
        outer = plus(above, times(edge, top))
        put(work, outer, chunk, depth + 1)

        def behind(step, carry):
            index = depth - 1 - step
            factor = pair(alpha, chunk, first_level + index + 1)
            now = plus(pair(work, chunk, index), times(factor, carry))
            put(work, now, chunk, index)
            return now

        bottom = lax.fori_loop(0, depth, behind, outer, unroll=True)
        put(work, plus(below, times(pair(alpha, chunk, first_level), bottom)), chunk, depth)

    def blocks(values):
        return values.reshape(modes // 8, 8, length_y)

    def operator(chunk):
        eig = blocks(eigen(chunk))

        def run(index, carry):
            center = faces[index, 0] * eig + faces[index, 1]
            values = pair(field, chunk, index + 1)
            turned = (-shift_im * values[1], shift_im * values[0])
            above = pair(field, chunk, index + 2)
            below = pair(field, chunk, index)
            for part in range(2):
                value = values[part]
                applied = center * blocks(value) + blocks(turned[part])
                applied = applied - faces[index, 2] * blocks(pltpu.roll(value, last, 1))
                applied = applied - faces[index, 3] * blocks(pltpu.roll(value, 1, 1))
                applied = applied - faces[index, 4] * blocks(above[part])
                applied = applied - faces[index, 5] * blocks(below[part])
                work[chunk, index, part] = applied.reshape(modes, length_y)
            return carry

        lax.fori_loop(0, depth, run, 0, unroll=8)

    squares[0] = none
    squares[1] = none
    factors(0)

    def begin(chunk):
        @pl.when(chunk > 0)
        def _():
            take(chunk)

        launch(0, chunk)

    def middle(chunk):
        solve(0, chunk)
        values = sine_rows(work[chunk]) * scale
        field[chunk, pl.ds(1, depth)] = values[:depth]
        field[chunk, 0] = values[depth]
        field[chunk, depth + 1] = values[depth + 1]
        operator(chunk)
        here = forcing[chunk]
        rest = here - sine_rows(work[chunk, pl.ds(0, depth)])
        work[chunk, pl.ds(0, depth)] = rest
        launch(1, chunk)
        squares[0] = squares[0] + jnp.sum(here * here, axis=(0, 1))
        squares[1] = squares[1] + jnp.sum(rest * rest, axis=(0, 1))

        @pl.when(chunk == chunks - 1)
        def _():
            row = lax.broadcasted_iota(jnp.int32, (ITERS, 128), 0)
            both = jnp.where(row == 0, jnp.sum(squares[0]), jnp.sum(squares[1]))
            sum_own[...] = both / length_x

            @each_peer
            def _(offset):
                sum_copy(offset).start()

            pltpu.make_async_copy(sum_own, sums.at[me], own_sem.at[chunks]).start()

    def finish(chunk):
        solve(1, chunk)
        values = sine_rows(work[chunk, pl.ds(0, depth)]) * scale
        result[chunk] = field[chunk, pl.ds(1, depth)] + values

        def put_out(which):
            for offset in (2, 3, 1):
                out_copy(which, offset).start()
            own_copy(which).start()

        @pl.when(chunk < chunks - 1)
        def _():
            put_out(chunk)

        @pl.when(chunk == chunks - 1)
        def _():
            put_out(None)

    def ready(chunk):
        @pl.when(chunk + 1 < chunks)
        def _():
            factors(chunk + 1)

    stages = {
        "begin": (0, begin),
        "ready": (0, ready),
        "relay": (LAGS[0], functools.partial(relay, 0)),
        "middle": (LAGS[1], middle),
        "again": (LAGS[2], functools.partial(relay, 1)),
        "finish": (LAGS[3], finish),
    }

    def step(index, carry):
        for name in ORDER:
            lag, act = stages[name]

            @pl.when((index >= lag) & (index < chunks + lag))
            def _():
                act(index - lag)

        return carry

    lax.fori_loop(0, chunks + LAGS[3], step, 0)

    def settle(chunk, carry):
        for turn_id in range(2):
            pair_copy(turn_id, chunk).wait_send()

            @pl.when(inner)
            def _():
                comb_copy(turn_id, chunk, 0).wait_send()
                comb_copy(turn_id, chunk, 1).wait_send()

        return carry

    def arrive(chunk, carry):
        own_copy(chunk).wait()
        for offset in range(1, RADIX):
            out_copy(chunk, offset).wait()
        return carry

    for load in loads[later:]:
        load.wait()
    lax.fori_loop(0, chunks - 1, arrive, 0)

    def gather(plane, carry):
        for residue in range(RADIX):
            blocks = []
            for part in range(2):
                blocks += [slabs[residue, chunk, plane, part] for chunk in range(chunks - 1)]
                blocks += [none]
            right = split(jnp.concatenate(blocks, axis=0))
            partial[plane, residue] = dot3((bwd_hi[residue], bwd_lo[residue]), right)
        return carry

    lax.fori_loop(0, planes, gather, 0)

    pltpu.make_async_copy(sum_own, sums.at[me], own_sem.at[chunks]).wait()

    @pl.when(team < teams - 1)
    def _():
        edge_copy(0).wait_send()

    @pl.when(team > 0)
    def _():
        edge_copy(1).wait_send()

    @pl.when(inner)
    def _():
        half_copy(0).wait_send()
        half_copy(1).wait_send()

    @each_peer
    def _(offset):
        sum_copy(offset).wait()

    lax.fori_loop(0, chunks, settle, 0)
    arrive(None, 0)


def ending(cells, partial, tail, sums, table, out, norms, stage, out_sem):
    planes, _, twice, length_y = partial.shape
    count = twice // 2
    modes = tail.shape[3]

    def store(plane, q):
        return pltpu.make_async_copy(
            stage.at[:, plane, pl.ds(q * count, count), :],
            out.at[:, plane, pl.ds(q * count, count), :],
            out_sem.at[plane, q],
        )

    for plane in range(planes):
        parts = []
        for residue in range(RADIX):
            high, low = split(tail[residue, plane].reshape(2 * modes, length_y))
            right = jnp.concatenate([high, low, high], axis=0)
            more = jnp.dot(table[residue], right, preferred_element_type=jnp.float32)
            values = partial[plane, residue] + more
            parts.append((values[:count], values[count:]))
        for q in range(RADIX):
            re, im = combine(parts, [residue * q for residue in range(RADIX)])
            stage[0, plane, q * count : (q + 1) * count, :] = re
            stage[1, plane, q * count : (q + 1) * count, :] = im
            store(plane, q).start()
    root = jnp.sqrt(jnp.sum(sums[...], axis=0) / cells)
    for index in range(ITERS):
        norms[index] = root[index, 0]
    for plane in range(planes):
        for q in range(RADIX):
            store(plane, q).wait()


CHUNKS = 8
LAGS = (1, 2, 3, 5)
ORDER = ("begin", "relay", "finish", "middle", "ready", "again")


def body(source, layer_ids, conduct_table, shift):
    planes = source.shape[1]
    length_x = source.shape[2]
    length_y = source.shape[3]
    groups = lax.axis_size("gz")
    length_z = planes * groups
    count = length_x // RADIX
    modes = count // CHUNKS
    if groups != 4 * RADIX or modes % 8 or planes > 8 or length_z > 64 or length_y % 128:
        return body_plain(source, layer_ids, conduct_table, shift)
    depth = planes * RADIX
    layers = conduct_table.shape[0]
    mode_ids = RADIX * np.arange(count)[None, :] + np.arange(RADIX)[:, None]
    mode_eig = (2.0 - 2.0 * np.cos(2.0 * np.pi / length_x * mode_ids)).astype(np.float32)
    mode_eig = np.broadcast_to(mode_eig[:, :, None], (RADIX, count, 128))
    mode_eig = np.ascontiguousarray(mode_eig).reshape(RADIX, CHUNKS, modes, 128)
    eig_y = 4.0 - 2.0 * np.cos(np.pi / (length_y + 1) * (np.arange(length_y) + 1.0))
    eig_y = np.ascontiguousarray(np.broadcast_to(eig_y.astype(np.float32), (8, length_y)))
    forward, backward = radix_tables(length_x)
    tables = [*halves(forward), *halves(sine_host(length_y)), *halves(backward)]
    final = np.concatenate([part * count + np.arange(count - modes, count) for part in range(2)])
    final = backward[:, :, final]
    high = final.astype(jnp.bfloat16)
    low = (final - high.astype(np.float32)).astype(jnp.bfloat16)
    final = jnp.asarray(np.concatenate([high, high, low], axis=2))
    tile = (2, modes, length_y)
    smem = pl.BlockSpec(memory_space=pltpu.SMEM)
    hbm = pl.BlockSpec(memory_space=pl.ANY)
    vmem = pl.BlockSpec(memory_space=pltpu.VMEM)
    f32 = jnp.float32
    dma = pltpu.SemaphoreType.DMA
    in_hbm = functools.partial(pltpu.with_memory_space_constraint, memory_space=pltpu.HBM)
    partial, tail, sums = pl.pallas_call(
        functools.partial(kernel, groups, planes, CHUNKS, layers),
        out_shape=(
            pltpu.VMEM((planes, RADIX, 2 * count, length_y), f32),
            pltpu.VMEM((RADIX, planes, *tile), f32),
            pltpu.VMEM((groups, ITERS, 128), f32),
        ),
        in_specs=[hbm] * 12,
        out_specs=(vmem, hbm, hbm),
        scratch_shapes=[
            pltpu.VMEM(source.shape, f32),
            pltpu.VMEM(layer_ids.shape, jnp.int32),
            pltpu.SMEM(conduct_table.shape, f32),
            pltpu.SMEM(shift.shape, f32),
            pltpu.VMEM((CHUNKS, modes, 128), f32),
            pltpu.VMEM((8, length_y), f32),
        ]
        + [pltpu.VMEM(table.shape, jnp.bfloat16) for table in tables]
        + [
            pltpu.VMEM((RADIX, CHUNKS - 1, planes, *tile), f32),
            pltpu.VMEM((RADIX, CHUNKS, planes, *tile), f32),
            pltpu.VMEM((CHUNKS, depth, *tile), f32),
            pltpu.VMEM((planes, length_y), f32),
            pltpu.VMEM((RADIX, planes, length_y), f32),
            pltpu.VMEM((depth + 2, 8, length_y), f32),
            pltpu.VMEM((4, length_y), f32),
            pltpu.VMEM((2, 4, length_y), f32),
            pltpu.VMEM((4, length_y), f32),
            pltpu.VMEM((4, length_y), f32),
            pltpu.VMEM((depth, 6, 8, length_y), f32),
            pltpu.VMEM((CHUNKS, depth + 2, *tile), f32),
            pltpu.VMEM((CHUNKS, length_z + 1, *tile), f32),
            pltpu.VMEM((CHUNKS, groups // RADIX, *tile), f32),
            pltpu.VMEM((CHUNKS, depth + 2, *tile), f32),
            pltpu.VMEM((CHUNKS, depth, *tile), f32),
            pltpu.VMEM((ITERS, 128), f32),
            pltpu.VMEM(tile, f32),
        ]
        + [pltpu.VMEM((ITERS, CHUNKS, *tile), f32)] * 5
        + [dma((9 + 2 * RADIX + planes,))]
        + [dma((CHUNKS, RADIX))] * 2
        + [dma((RADIX,))] * 2
        + [dma((2,))] * 2
        + [dma((2,)), dma((1,))]
        + [dma((CHUNKS, RADIX))] * 2
        + [dma((groups,))] * 2
        + [dma((CHUNKS + 1,))]
        + [dma((ITERS, CHUNKS))] * 2
        + [dma((ITERS, CHUNKS, 2)), dma((ITERS, CHUNKS))],
        compiler_params=pltpu.CompilerParams(
            collective_id=0, has_side_effects=True, vmem_limit_bytes=50 << 20
        ),
    )(
        in_hbm(source),
        in_hbm(layer_ids),
        in_hbm(conduct_table),
        in_hbm(shift),
        *[in_hbm(jnp.asarray(table)) for table in (mode_eig, eig_y, *tables)],
    )
    cells = length_x * length_y * length_z
    return pl.pallas_call(
        functools.partial(ending, cells),
        out_shape=(
            jax.ShapeDtypeStruct(source.shape, f32),
            jax.ShapeDtypeStruct((ITERS,), f32),
        ),
        in_specs=[vmem] * 4,
        out_specs=(hbm, smem),
        scratch_shapes=[pltpu.VMEM(source.shape, f32), dma((planes, RADIX))],
        compiler_params=pltpu.CompilerParams(vmem_limit_bytes=20 << 20),
    )(partial, tail, sums, final)


def solution(mesh):
    placed = (P(None, ("node", "gz"), None, None), P(("node", "gz"), None), P(), P("node"))
    return jax.shard_map(
        body,
        mesh=mesh,
        in_specs=placed,
        out_specs=(P(None, ("node", "gz"), None, None), P("node")),
        check_vma=False,
    )
```
